32 devices in a mesh: section: 2 (over y), replica: 4 (over x, core), shard: 4 (over z).
Axes of the slice: x: 2, y: 2, z: 4, core: 2. Of those that a mesh axis runs over, the one named last changes fastest.
Arguments:
- tokens: bfloat16 [2, 4, 1024, 1536], P(None, 'replica', 'shard'), may hold values from -6 to 6
- segments: int32 [2, 4, 1024], P(None, 'replica'), may hold values from 0 to 7, never falling along the last dimension, each value on 1 to 512 neighbouring positions
- norm_attn: bfloat16 [2, 1536], P('section', 'shard'), may hold values from 0.25 to 1.75
- w_query: bfloat16 [2, 1536, 1536], P('section', 'shard'), may hold values from -0.15625 to 0.15625
- w_key: bfloat16 [2, 1536, 768], P('section', 'shard'), may hold values from -0.15625 to 0.15625
- w_value: bfloat16 [2, 1536, 768], P('section', 'shard'), may hold values from -0.15625 to 0.15625
- w_out: bfloat16 [2, 1536, 1536], P('section', 'shard'), may hold values from -0.3125 to 0.3125
- norm_ffn: bfloat16 [2, 1536], P('section', 'shard'), may hold values from 0.25 to 1.75
- w_gate: bfloat16 [2, 1536, 4096], P('section', 'shard'), may hold values from -0.15625 to 0.15625
- w_up: bfloat16 [2, 1536, 4096], P('section', 'shard'), may hold values from -0.15625 to 0.15625
- w_down: bfloat16 [2, 4096, 1536], P('section', 'shard'), may hold values from -0.09375 to 0.09375
- cotangent: bfloat16 [2, 4, 1024, 1536], P(None, 'replica', 'shard'), may hold values from -6 to 6
Outputs:
- section_outputs: bfloat16 [2, 2, 4, 1024, 1536], P('section', None, 'replica', 'shard')
- input_grads: float32 [2, 2, 4, 1024, 1536], P('section', None, 'replica', 'shard')
- grad_norm_attn: float32 [2, 1536], P('section', 'shard')
- grad_query: float32 [2, 1536, 1536], P('section', 'shard')
- grad_key: float32 [2, 1536, 768], P('section', 'shard')
- grad_value: float32 [2, 1536, 768], P('section', 'shard')
- grad_out: float32 [2, 1536, 1536], P('section', 'shard')
- grad_norm_ffn: float32 [2, 1536], P('section', 'shard')
- grad_gate: float32 [2, 1536, 4096], P('section', 'shard')
- grad_up: float32 [2, 1536, 4096], P('section', 'shard')
- grad_down: float32 [2, 4096, 1536], P('section', 'shard')
The draws below stay inside these ranges and needn't reach their ends.
Inputs may be any that keep to these rules, and one draw needn't show every extreme that they name: `segments`: along each sequence the numbers never fall; a document holds at most half of 1024 tokens, and one document of each sequence holds exactly that many.
All inputs are finite; a program needn't handle non-finite values.
Results may differ from the reference program's by a relative error of at most 0.023.
Values may be sent and summed in bfloat16 or wider, within the bound.
A program may use at most 448 MiB of HBM per device.

```python
import math
import jax
import jax.numpy as jnp
import numpy as np
from jax import lax

D = 1536
QH = 16
KVH = 8
HD = 96
FF = 4096
QW = 1536
KW = 768
MB = 2
SEQ = 1024
SEQS = 4
LAYERS = 2
DOCS = 8


def block_scale(own_key, dims, shards, smallest, high):
    gain = 1.0
    for dim, blocks in shards:
        draws = jax.random.uniform(jax.random.fold_in(jax.random.fold_in(own_key, 6), dim), (blocks,), jnp.float32, smallest / len(shards), high / len(shards))
        gain = gain * jnp.repeat(jnp.exp(draws), dims[dim] // blocks).reshape((-1,) + (1,) * (len(dims) - 1 - dim))
    return gain


def split_up(count, total, bound, slope):
    loads = [(1 << 20) // math.isqrt(rank ** slope) + 1 for rank in range(2, count + 1)]
    rest, given = total - bound - (count - 1), [1] * (count - 1)
    while rest > 0:
        candidates = [i for i in range(count - 1) if given[i] < bound]
        whole, budget = sum([loads[i] for i in candidates]), rest
        for i in candidates:
            extra = min(bound - given[i], max(1, budget * loads[i] // whole), rest)
            given[i] = given[i] + extra
            rest = rest - extra
    return np.array([bound] + given)


def ragged_sizes(own_key, number_of, total, bound, slope):
    if number_of == 2:
        one = jax.random.randint(own_key, (), max(1, total - bound), min(bound, total - 1) + 1)
        return jnp.stack([one, total - one])
    sizes = jnp.asarray(split_up(number_of, total, bound, slope), jnp.int32)
    couples = (number_of - 1) // 2
    giver, taker = sizes[1:1 + 2 * couples:2], sizes[2:2 + 2 * couples:2]
    margin = jnp.minimum(giver - 1, bound - taker)
    shifted = jax.random.randint(jax.random.fold_in(own_key, 1), (couples,), 0, 1 << 20) % (margin + 1)
    sizes = sizes.at[1:1 + 2 * couples:2].set(giver - shifted).at[2:2 + 2 * couples:2].set(taker + shifted)
    return sizes[jax.random.permutation(jax.random.fold_in(own_key, 2), number_of)]


def bell_draw(own_key, extent, scale, limit, split=(), kind=jnp.bfloat16):
    array = scale * jax.random.normal(own_key, extent, jnp.float32)
    if split:
        array = array * block_scale(own_key, extent, split, -0.22, 0.18)
    return jnp.clip(array, -limit, limit).astype(kind)


def setup_inputs(seed: int = 0) -> dict:
    splits = jax.random.split(jax.random.key(seed), 13)
    return {
        "tokens": bell_draw(splits[0], (MB, SEQS, SEQ, D), 1.0, 6.0, ((1, 4), (2, 4))),
        "segments": jax.vmap(lambda own: jnp.searchsorted(jnp.cumsum(ragged_sizes(own, DOCS, SEQ, SEQ // 2, 2)), jnp.arange(SEQ), side="right"))(jax.random.split(splits[1], MB * SEQS)).reshape((MB, SEQS, SEQ)).astype(jnp.int32),
        "norm_attn": jnp.clip(1.0 + 0.15 * jax.random.normal(splits[2], (LAYERS, D), jnp.float32), 0.25, 1.75).astype(jnp.bfloat16),
        "w_query": bell_draw(splits[3], (LAYERS, D, QW), D ** -0.5, 0.15625, ((0, 2), (1, 4))),
        "w_key": bell_draw(splits[4], (LAYERS, D, KW), D ** -0.5, 0.15625, ((0, 2), (1, 4))),
        "w_value": bell_draw(splits[5], (LAYERS, D, KW), D ** -0.5, 0.15625, ((0, 2), (1, 4))),
        "w_out": bell_draw(splits[6], (LAYERS, QW, D), (QW // 4) ** -0.5, 0.3125, ((0, 2), (1, 4))),
        "norm_ffn": jnp.clip(1.0 + 0.15 * jax.random.normal(splits[7], (LAYERS, D), jnp.float32), 0.25, 1.75).astype(jnp.bfloat16),
        "w_gate": bell_draw(splits[8], (LAYERS, D, FF), D ** -0.5, 0.15625, ((0, 2), (1, 4))),
        "w_up": bell_draw(splits[9], (LAYERS, D, FF), D ** -0.5, 0.15625, ((0, 2), (1, 4))),
        "w_down": bell_draw(splits[10], (LAYERS, FF, D), FF ** -0.5, 0.09375, ((0, 2), (1, 4))),
        "cotangent": bell_draw(splits[11], (MB, SEQS, SEQ, D), 1.0, 6.0, ((1, 4), (2, 4))),
    }


@jax.custom_vjp
def low(v):
    return lax.optimization_barrier(v.astype(jnp.bfloat16)).astype(jnp.float32)

@jax.custom_vjp
def low_back(v):
    return v

def low_keep(v):
    return (low(v), None)

def low_pass(kept, grad):
    return (grad,)

def back_keep(v):
    return (v, None)

def back_low(kept, grad):
    return (low(grad),)
low.defvjp(low_keep, low_pass)
low_back.defvjp(back_keep, back_low)
EPSILON = 1e-05
ROPE_BASE = 100000.0
HIGHEST_PRECISION = lax.Precision.HIGHEST

def product(left, right):
    return jnp.dot(left, right, precision=HIGHEST_PRECISION, preferred_element_type=jnp.float32)

def rotate(values, cosine_table, sine_table):
    half_dim = values.shape[-1] // 2
    leading = values[..., :half_dim]
    trailing = values[..., half_dim:]
    return jnp.concatenate([leading * cosine_table - trailing * sine_table, trailing * cosine_table + leading * sine_table], axis=-1)

def layer_forward(inputs, weights, segment, positions):
    norm_attn, w_query, w_key, w_value, w_out, norm_ffn, w_gate, w_up, w_down = weights
    seq_length = inputs.shape[0]
    groups = QH // KVH
    half_dim = HD // 2
    frequency = ROPE_BASE ** (-(jnp.arange(half_dim, dtype=jnp.float32) * 2.0) / HD)
    angles = positions.astype(jnp.float32)[:, None, None] * frequency[None, None, :]
    cosine_table = jnp.cos(angles)
    sine_table = jnp.sin(angles)
    scaled = inputs * lax.rsqrt(lax.optimization_barrier(jnp.mean(inputs * inputs, axis=-1, keepdims=True)) + EPSILON)
    normed = low(scaled * norm_attn)
    raw_query = low_back(product(normed, w_query)).reshape(seq_length, KVH, groups, HD)
    queries = low(rotate(raw_query, cosine_table[:, :, None, :], sine_table[:, :, None, :]))
    raw_key = low_back(product(normed, w_key)).reshape(seq_length, KVH, HD)
    key_rows = low(rotate(raw_key, cosine_table, sine_table))
    value_rows = low(low_back(product(normed, w_value))).reshape(seq_length, KVH, HD)
    scores = jnp.einsum('ihgd,jhd->hgij', queries, key_rows, precision=HIGHEST_PRECISION) * HD ** (-0.5)
    scores = low_back(scores)
    index_row = jnp.arange(seq_length, dtype=jnp.int32)
    allowed = (index_row[None, :] <= index_row[:, None]) & (segment[None, :] == segment[:, None])
    scores = jnp.where(allowed, scores, -1e+30)
    row_top = lax.optimization_barrier(jnp.max(scores, axis=-1, keepdims=True))
    exponent = jnp.exp(scores - row_top)
    probabilities = low(exponent / lax.optimization_barrier(jnp.sum(exponent, axis=-1, keepdims=True)))
    attended = jnp.einsum('hgij,jhd->ihgd', probabilities, value_rows, precision=HIGHEST_PRECISION)
    attended = low(low_back(attended.reshape(seq_length, QH * HD)))
    middle = inputs + low_back(product(attended, w_out))
    scaled_mid = middle * lax.rsqrt(lax.optimization_barrier(jnp.mean(middle * middle, axis=-1, keepdims=True)) + EPSILON)
    normed_mid = low(scaled_mid * norm_ffn)
    gate_proj = low_back(product(normed_mid, w_gate))
    up_proj = low_back(product(normed_mid, w_up))
    hidden = low(jax.nn.silu(gate_proj) * up_proj)
    return middle + low_back(product(hidden, w_down))

def reference(tokens, segments, norm_attn, w_query, w_key, w_value, w_out, norm_ffn, w_gate, w_up, w_down, cotangent):
    weights = tuple((weight_array.astype(jnp.float32) for weight_array in (norm_attn, w_query, w_key, w_value, w_out, norm_ffn, w_gate, w_up, w_down)))
    micro_count, seq_count, seq_length, width = tokens.shape
    row_total = micro_count * seq_count
    inputs = tokens.astype(jnp.float32).reshape(row_total, seq_length, width)
    segment_rows = segments.reshape(row_total, seq_length)
    offsets = jnp.zeros((row_total, seq_length, width), jnp.float32)

    def forward(inputs, offsets, weights):

        def per_sequence(carry_value, item_value):
            source, offset, segment = item_value
            starts = jnp.searchsorted(segment, segment, side='left').astype(jnp.int32)
            positions = jnp.arange(seq_length, dtype=jnp.int32) - starts
            first_out = layer_forward(source, tuple((weight_array[0] for weight_array in weights)), segment, positions)
            passed = low(low_back(first_out)) + offset
            second_out = layer_forward(passed, tuple((weight_array[1] for weight_array in weights)), segment, positions)
            return (carry_value, (first_out, second_out))
        unused, stacked = lax.scan(jax.checkpoint(per_sequence), jnp.zeros((), jnp.float32), (inputs, offsets, segment_rows))
        return stacked
    (firsts, seconds), pull_back = jax.vjp(forward, inputs, offsets, weights)
    grad_inputs, grad_offsets, grad_weights = pull_back((jnp.zeros_like(firsts), cotangent.astype(jnp.float32).reshape(row_total, seq_length, width)))
    shape_out = (micro_count, seq_count, seq_length, width)
    section_outputs = jnp.stack([firsts.reshape(shape_out), seconds.reshape(shape_out)]).astype(jnp.bfloat16)
    input_grads = jnp.stack([grad_inputs.reshape(shape_out), grad_offsets.reshape(shape_out)])
    return (section_outputs, input_grads, grad_weights[0], grad_weights[1], grad_weights[2], grad_weights[3], grad_weights[4], grad_weights[5], grad_weights[6], grad_weights[7], grad_weights[8])
```

```python
import jax
import jax.numpy as jnp
from jax import lax
from jax.sharding import PartitionSpec as P

QH = 16
KVH = 8
HD = 96


EPSILON = 1e-05
ROPE_BASE = 100000.0


def from_behind(x, axis, by):
    devices = lax.axis_size(axis)
    pairs = [(i, i + by) for i in range(devices) if 0 <= i + by < devices]
    return lax.ppermute(x, axis, pairs)


def rotate(values, cosine_table, sine_table, turn_sign):
    half_dim = values.shape[-1] // 2
    leading = values[..., :half_dim]
    trailing = values[..., half_dim:]
    return jnp.concatenate(
        [
            leading * cosine_table - turn_sign * trailing * sine_table,
            trailing * cosine_table + turn_sign * leading * sine_table,
        ],
        axis=-1,
    )


def gather_rows(piece):
    if piece.ndim == 1:
        return lax.all_gather(piece, "shard", axis=0, tiled=True)
    rows = piece.shape[0] // lax.axis_size("replica")
    own = lax.dynamic_slice_in_dim(piece, lax.axis_index("replica") * rows, rows)
    return lax.all_gather(own, ("shard", "replica"), axis=0, tiled=True)


def scatter_rows(term):
    if term.ndim == 1:
        return lax.psum(lax.psum_scatter(term, "shard", scatter_dimension=0, tiled=True), "replica")
    low = term.astype(jnp.bfloat16)
    part = lax.psum_scatter(low, ("shard", "replica"), scatter_dimension=0, tiled=True)
    return lax.all_gather(part, "replica", axis=0, tiled=True).astype(jnp.float32)


def gather_layer(pieces):
    return tuple(gather_rows(piece) for piece in pieces)


def forward_layer(inputs, weights, segment, row_start):
    norm_attn, w_query, w_key, w_value, w_out, norm_ffn, w_gate, w_up, w_down = weights
    row_count = inputs.shape[0]
    seq_length = segment.shape[0]
    groups = QH // KVH
    half_dim = HD // 2
    local_segment = lax.dynamic_slice_in_dim(segment, row_start, row_count)
    query_index = row_start + jnp.arange(row_count, dtype=jnp.int32)
    starts = jnp.sum((segment[None, :] < local_segment[:, None]).astype(jnp.int32), axis=1)
    positions = query_index - starts
    frequency = ROPE_BASE ** (-(jnp.arange(half_dim, dtype=jnp.float32) * 2.0) / HD)
    angles = positions.astype(jnp.float32)[:, None, None] * frequency[None, None, :]
    cosine_table = jnp.cos(angles)
    sine_table = jnp.sin(angles)
    recip_one = lax.rsqrt(jnp.mean(inputs * inputs, axis=-1, keepdims=True) + EPSILON)
    scaled = inputs * recip_one
    normed = (scaled * norm_attn.astype(jnp.float32)).astype(jnp.bfloat16)
    raw_query = jnp.dot(normed, w_query, preferred_element_type=jnp.float32).reshape(
        row_count, KVH, groups, HD
    )
    queries = rotate(raw_query, cosine_table[:, :, None, :], sine_table[:, :, None, :], 1.0).astype(
        jnp.bfloat16
    )
    raw_key = jnp.dot(normed, w_key, preferred_element_type=jnp.float32).reshape(row_count, KVH, HD)
    key_rows = (
        rotate(raw_key, cosine_table, sine_table, 1.0)
        .astype(jnp.bfloat16)
        .reshape(row_count, KVH * HD)
    )
    value_rows = jnp.dot(normed, w_value, preferred_element_type=jnp.float32).astype(jnp.bfloat16)
    all_keys, all_values = (
        lax.all_gather(key_rows, "shard", axis=0, tiled=True),
        lax.all_gather(value_rows, "shard", axis=0, tiled=True),
    )
    all_keys = all_keys.reshape(seq_length, KVH, HD)
    all_values = all_values.reshape(seq_length, KVH, HD)
    key_index = jnp.arange(seq_length, dtype=jnp.int32)
    allowed = (key_index[None, :] <= query_index[:, None]) & (
        segment[None, :] == local_segment[:, None]
    )
    scores = jnp.einsum(
        "ihgd,jhd->hgij", queries, all_keys, preferred_element_type=jnp.float32
    ) * HD ** (-0.5)
    scores = jnp.where(allowed, scores, -1e30)
    row_top = jnp.max(scores, axis=-1, keepdims=True)
    exponent = jnp.exp(scores - row_top)
    row_total = jnp.sum(exponent, axis=-1, keepdims=True)
    probabilities = exponent / row_total
    log_total = row_top + jnp.log(row_total)
    attended = jnp.einsum(
        "hgij,jhd->ihgd",
        probabilities.astype(jnp.bfloat16),
        all_values,
        preferred_element_type=jnp.float32,
    )
    attended = attended.reshape(row_count, QH * HD).astype(jnp.bfloat16)
    middle = inputs + jnp.dot(attended, w_out, preferred_element_type=jnp.float32)
    recip_two = lax.rsqrt(jnp.mean(middle * middle, axis=-1, keepdims=True) + EPSILON)
    scaled_mid = middle * recip_two
    normed_mid = (scaled_mid * norm_ffn.astype(jnp.float32)).astype(jnp.bfloat16)
    gate_proj = jnp.dot(normed_mid, w_gate, preferred_element_type=jnp.float32)
    up_proj = jnp.dot(normed_mid, w_up, preferred_element_type=jnp.float32)
    hidden = (jax.nn.silu(gate_proj) * up_proj).astype(jnp.bfloat16)
    result = middle + jnp.dot(hidden, w_down, preferred_element_type=jnp.float32)
    saved = (
        scaled,
        recip_one,
        normed,
        queries,
        all_keys,
        all_values,
        allowed,
        log_total,
        attended,
        scaled_mid,
        recip_two,
        normed_mid,
        gate_proj,
        up_proj,
        hidden,
        cosine_table,
        sine_table,
    )
    return (result, saved)


def backward_layer(grad_result, weights, saved):
    norm_attn, w_query, w_key, w_value, w_out, norm_ffn, w_gate, w_up, w_down = weights
    (
        scaled,
        recip_one,
        normed,
        queries,
        all_keys,
        all_values,
        allowed,
        log_total,
        attended,
        scaled_mid,
        recip_two,
        normed_mid,
        gate_proj,
        up_proj,
        hidden,
        cosine_table,
        sine_table,
    ) = saved
    row_count = grad_result.shape[0]
    seq_length = all_keys.shape[0]
    groups = QH // KVH
    score_scale = HD ** (-0.5)
    branch_grad = grad_result.astype(jnp.bfloat16)
    grad_hidden = jnp.einsum("td,fd->tf", branch_grad, w_down, preferred_element_type=jnp.float32)
    sigmoid_gate = jax.nn.sigmoid(gate_proj)
    gate_low = (
        grad_hidden * up_proj * (sigmoid_gate * (1.0 + gate_proj * (1.0 - sigmoid_gate)))
    ).astype(jnp.bfloat16)
    up_low = (grad_hidden * jax.nn.silu(gate_proj)).astype(jnp.bfloat16)
    grad_normed_mid = jnp.einsum("tf,df->td", gate_low, w_gate, preferred_element_type=jnp.float32)
    grad_normed_mid = grad_normed_mid + jnp.einsum(
        "tf,df->td", up_low, w_up, preferred_element_type=jnp.float32
    )
    grad_norm_ffn = jnp.sum(grad_normed_mid * scaled_mid, axis=0)
    grad_scaled_mid = grad_normed_mid * norm_ffn.astype(jnp.float32)
    grad_middle = grad_result + recip_two * (
        grad_scaled_mid
        - scaled_mid * jnp.mean(grad_scaled_mid * scaled_mid, axis=-1, keepdims=True)
    )
    attn_grad = grad_middle.astype(jnp.bfloat16)
    grad_attended = jnp.einsum("td,qd->tq", attn_grad, w_out, preferred_element_type=jnp.float32)
    grad_attended = grad_attended.astype(jnp.bfloat16).reshape(row_count, KVH, groups, HD)
    scores = (
        jnp.einsum("ihgd,jhd->hgij", queries, all_keys, preferred_element_type=jnp.float32)
        * score_scale
    )
    scores = jnp.where(allowed, scores, -1e30)
    probabilities = jnp.exp(scores - log_total)
    grad_probs = jnp.einsum(
        "ihgd,jhd->hgij", grad_attended, all_values, preferred_element_type=jnp.float32
    )
    row_dot = jnp.sum(probabilities * grad_probs, axis=-1, keepdims=True)
    grad_scores = (probabilities * (grad_probs - row_dot)).astype(jnp.bfloat16)
    grad_queries = (
        jnp.einsum("hgij,jhd->ihgd", grad_scores, all_keys, preferred_element_type=jnp.float32)
        * score_scale
    )
    key_terms = (
        jnp.einsum("hgij,ihgd->jhd", grad_scores, queries, preferred_element_type=jnp.float32)
        * score_scale
    )
    value_terms = jnp.einsum(
        "hgij,ihgd->jhd",
        probabilities.astype(jnp.bfloat16),
        grad_attended,
        preferred_element_type=jnp.float32,
    )
    key_terms = key_terms.reshape(seq_length, KVH * HD)
    value_terms = value_terms.reshape(seq_length, KVH * HD)
    grad_keys, grad_values = (
        lax.psum_scatter(
            key_terms.astype(jnp.bfloat16), "shard", scatter_dimension=0, tiled=True
        ).astype(jnp.float32),
        lax.psum_scatter(
            value_terms.astype(jnp.bfloat16), "shard", scatter_dimension=0, tiled=True
        ).astype(jnp.float32),
    )
    query_low = rotate(grad_queries, cosine_table[:, :, None, :], sine_table[:, :, None, :], -1.0)
    query_low = query_low.reshape(row_count, QH * HD).astype(jnp.bfloat16)
    key_low = rotate(grad_keys.reshape(row_count, KVH, HD), cosine_table, sine_table, -1.0)
    key_low = key_low.reshape(row_count, KVH * HD).astype(jnp.bfloat16)
    value_low = grad_values.astype(jnp.bfloat16)
    grad_normed = jnp.einsum("tq,dq->td", query_low, w_query, preferred_element_type=jnp.float32)
    grad_normed = grad_normed + jnp.einsum(
        "tq,dq->td", key_low, w_key, preferred_element_type=jnp.float32
    )
    grad_normed = grad_normed + jnp.einsum(
        "tq,dq->td", value_low, w_value, preferred_element_type=jnp.float32
    )
    grad_norm_attn = jnp.sum(grad_normed * scaled, axis=0)
    grad_scaled = grad_normed * norm_attn.astype(jnp.float32)
    grad_inputs = grad_middle + recip_one * (
        grad_scaled - scaled * jnp.mean(grad_scaled * scaled, axis=-1, keepdims=True)
    )
    operands = (
        normed,
        query_low,
        key_low,
        value_low,
        attended,
        attn_grad,
        normed_mid,
        gate_low,
        up_low,
        hidden,
        branch_grad,
    )
    return (grad_inputs, (grad_norm_attn, grad_norm_ffn), operands)


def row_product(left, right):
    return jnp.einsum("td,tq->dq", left, right, preferred_element_type=jnp.float32)


def weight_terms(gains, operands):
    (
        normed,
        query_low,
        key_low,
        value_low,
        attended,
        attn_grad,
        normed_mid,
        gate_low,
        up_low,
        hidden,
        branch_grad,
    ) = operands
    return (
        gains[0],
        row_product(normed, query_low),
        row_product(normed, key_low),
        row_product(normed, value_low),
        row_product(attended, attn_grad),
        gains[1],
        row_product(normed_mid, gate_low),
        row_product(normed_mid, up_low),
        row_product(hidden, branch_grad),
    )


def add_terms(earlier, later):
    if earlier is None:
        return later
    return tuple((left_term + right_term for left_term, right_term in zip(earlier, later)))


def body(
    tokens,
    segments,
    norm_attn,
    w_query,
    w_key,
    w_value,
    w_out,
    norm_ffn,
    w_gate,
    w_up,
    w_down,
    cotangent,
):
    micro_count = tokens.shape[0]
    row_count = tokens.shape[2]
    width = tokens.shape[3]
    first_section = lax.axis_index("section") == 0
    row_start = lax.axis_index("shard") * row_count
    pieces = (
        norm_attn[0],
        w_query[0],
        w_key[0],
        w_value[0],
        w_out[0],
        norm_ffn[0],
        w_gate[0],
        w_up[0],
        w_down[0],
    )
    held_weights = gather_layer(pieces)
    saved_ticks = []
    result_ticks = []
    arriving = jnp.zeros((row_count, width), jnp.bfloat16)
    for tick_index in range(micro_count + 1):
        weights = held_weights
        own_input = tokens[min(tick_index, micro_count - 1), 0].astype(jnp.float32)
        layer_input = jnp.where(first_section, own_input, arriving.astype(jnp.float32))
        segment = jnp.where(
            first_section,
            segments[min(tick_index, micro_count - 1), 0],
            segments[max(tick_index - 1, 0), 0],
        )
        result, saved = forward_layer(layer_input, weights, segment, row_start)
        result_low = result.astype(jnp.bfloat16)
        result_ticks.append(result_low)
        saved_ticks.append(saved)
        if tick_index < micro_count:
            arriving = from_behind(result_low, "section", 1)
    flow_ticks = []
    gain_sums = None
    operand_ticks = []
    returning = jnp.zeros((row_count, width), jnp.bfloat16)
    for tick_index in range(micro_count + 1):
        weights = held_weights
        later_grad = cotangent[min(tick_index, micro_count - 1), 0].astype(jnp.float32)
        incoming = jnp.where(first_section, returning.astype(jnp.float32), later_grad)
        active = jnp.where(first_section, tick_index >= 1, tick_index < micro_count)
        incoming = jnp.where(active, incoming, 0.0)
        saved = jax.tree.map(
            lambda early_value, late_value: jnp.where(first_section, early_value, late_value),
            saved_ticks[max(tick_index - 1, 0)],
            saved_ticks[min(tick_index + 1, micro_count)],
        )
        grad_inputs, gains, operands = backward_layer(incoming, weights, saved)
        flow_ticks.append(grad_inputs)
        if tick_index < micro_count:
            returning = from_behind(grad_inputs.astype(jnp.bfloat16), "section", -1)
        gain_sums = add_terms(gain_sums, gains)
        operand_ticks.append(operands)
    joined = tuple(
        (
            jnp.concatenate([tick_ops[index_op] for tick_ops in operand_ticks], axis=0)
            for index_op in range(len(operand_ticks[0]))
        )
    )
    full_terms = weight_terms(gain_sums, joined)
    totals = tuple(scatter_rows(term) for term in full_terms)
    section_outputs = jnp.stack(
        [
            jnp.where(first_section, result_ticks[index_micro], result_ticks[index_micro + 1])
            for index_micro in range(micro_count)
        ]
    )
    input_grads = jnp.stack(
        [
            jnp.where(first_section, flow_ticks[index_micro + 1], flow_ticks[index_micro])
            for index_micro in range(micro_count)
        ]
    )
    return (
        section_outputs[None, :, None],
        input_grads[None, :, None],
        totals[0][None],
        totals[1][None],
        totals[2][None],
        totals[3][None],
        totals[4][None],
        totals[5][None],
        totals[6][None],
        totals[7][None],
        totals[8][None],
    )


def solution(mesh):
    in_specs = (
        P(None, "replica", "shard", None),
        P(None, "replica", None),
        P("section", "shard"),
        P("section", "shard", None),
        P("section", "shard", None),
        P("section", "shard", None),
        P("section", "shard", None),
        P("section", "shard"),
        P("section", "shard", None),
        P("section", "shard", None),
        P("section", "shard", None),
        P(None, "replica", "shard", None),
    )
    out_specs = (
        P("section", None, "replica", "shard", None),
        P("section", None, "replica", "shard", None),
        P("section", "shard"),
        P("section", "shard", None),
        P("section", "shard", None),
        P("section", "shard", None),
        P("section", "shard", None),
        P("section", "shard"),
        P("section", "shard", None),
        P("section", "shard", None),
        P("section", "shard", None),
    )
    return jax.shard_map(body, mesh=mesh, in_specs=in_specs, out_specs=out_specs, check_vma=False)
```

```python
import functools

import jax
import jax.numpy as jnp
from jax import lax
from jax.experimental import pallas as pl
from jax.experimental.pallas import tpu as pltpu
from jax.sharding import PartitionSpec as P

QH = 16
KVH = 8
HD = 96


EPSILON = 1e-05
ROPE_BASE = 100000.0


def from_behind(x, axis, by):
    devices = lax.axis_size(axis)
    pairs = [(i, i + by) for i in range(devices) if 0 <= i + by < devices]
    return lax.ppermute(x, axis, pairs)


def rotate(values, cosine_table, sine_table, turn_sign):
    half_dim = values.shape[-1] // 2
    leading = values[..., :half_dim]
    trailing = values[..., half_dim:]
    return jnp.concatenate(
        [
            leading * cosine_table - turn_sign * trailing * sine_table,
            trailing * cosine_table + turn_sign * leading * sine_table,
        ],
        axis=-1,
    )


PARTS = 4


def start_remote(source, target, send_sem, recv_sem, device):
    pltpu.make_async_remote_copy(
        src_ref=source,
        dst_ref=target,
        send_sem=send_sem,
        recv_sem=recv_sem,
        device_id=device,
        device_id_type=pl.DeviceIdType.MESH,
    ).start()


def wait_bytes(ref, sem):
    pltpu.make_async_copy(ref, ref, sem).wait()


def greet(shards):
    place = lax.axis_index("shard")
    member = lax.axis_index("replica")
    barrier = pltpu.get_barrier_semaphore()
    pl.semaphore_signal(barrier, inc=1, device_id={"replica": member ^ 1}, device_id_type=pl.DeviceIdType.MESH)
    pl.semaphore_signal(barrier, inc=1, device_id={"replica": member ^ 2}, device_id_type=pl.DeviceIdType.MESH)

    @pl.when(place > 0)
    def _():
        pl.semaphore_signal(barrier, inc=1, device_id={"shard": place - 1}, device_id_type=pl.DeviceIdType.MESH)

    @pl.when(place < shards - 1)
    def _():
        pl.semaphore_signal(barrier, inc=1, device_id={"shard": place + 1}, device_id_type=pl.DeviceIdType.MESH)

    pl.semaphore_wait(barrier, 2 + (place > 0).astype(jnp.int32) + (place < shards - 1).astype(jnp.int32))


def gather_kernel(shards, chunks, count, *refs):
    pieces, wholes = refs[:count], refs[count : 2 * count]
    held = refs[2 * count : 3 * count]
    (local_sem, own_send, pass_send, line_recv, x_send, x_recv, core_send, core_recv) = refs[
        3 * count :
    ]
    place = lax.axis_index("shard")
    member = lax.axis_index("replica")
    part = member % PARTS
    greet(shards)

    def loads(index):
        return pltpu.make_async_copy(pieces[index], held[index], local_sem.at[index])

    def stores(index):
        rows = pieces[index].shape[0]
        target = wholes[index].at[pl.ds(pl.multiple_of(place * rows, rows), rows), :]
        return pltpu.make_async_copy(held[index], target, local_sem.at[index])

    for index in range(count):
        loads(index).start()

    def window(chunk, block, whose):
        index, first, length = chunk
        rows = pieces[index].shape[0]
        width = pieces[index].shape[1] // PARTS
        return wholes[index].at[
            pl.ds(pl.multiple_of(block * rows + first, length), length),
            pl.ds(pl.multiple_of(whose * width, width), width),
        ]

    def own(j):
        index, first, length = chunks[j]
        width = pieces[index].shape[1] // PARTS
        source = pieces[index].at[
            pl.ds(first, length), pl.ds(pl.multiple_of(part * width, width), width)
        ]
        for slot, way in enumerate((1, -1)):
            @pl.when((place + way >= 0) & (place + way < shards))
            def _():
                start_remote(
                    source,
                    window(chunks[j], place, part),
                    own_send.at[j, slot],
                    line_recv.at[j, place],
                    {"shard": place + way},
                )

    def hop(j, k):
        for way in (1, -1):
            block = place - way * k

            @pl.when((block >= 0) & (block < shards))
            def _():
                mine = window(chunks[j], block, part)
                wait_bytes(mine, line_recv.at[j, block])

                @pl.when((place + way >= 0) & (place + way < shards))
                def _():
                    start_remote(
                        mine, mine, pass_send.at[j, block], line_recv.at[j, block], {"shard": place + way}
                    )

                start_remote(mine, mine, x_send.at[j, block], x_recv.at[j, block], {"replica": member ^ 2})
                start_remote(
                    mine, mine, core_send.at[j, block, 0], core_recv.at[j, block, 0], {"replica": member ^ 1}
                )

    def across(j, k):
        for way in (1, -1):
            block = place - way * k

            @pl.when((block >= 0) & (block < shards))
            def _():
                theirs = window(chunks[j], block, part ^ 2)
                wait_bytes(theirs, x_recv.at[j, block])
                start_remote(
                    theirs, theirs, core_send.at[j, block, 1], core_recv.at[j, block, 1], {"replica": member ^ 1}
                )

    total = len(chunks)
    for step in range(total + shards + 1):
        if step < total:
            own(step)
        if 1 <= step <= count:
            loads(step - 1).wait()
            stores(step - 1).start()
        for k in range(1, shards):
            if 0 <= step - k < total:
                hop(step - k, k)
        for k in range(1, shards):
            if 0 <= step - k - 1 < total:
                across(step - k - 1, k)

    for j in range(total):
        for slot, way in enumerate((1, -1)):
            @pl.when((place + way >= 0) & (place + way < shards))
            def _():
                wait_bytes(window(chunks[j], place, part), own_send.at[j, slot])

        for k in range(1, shards):
            for way in (1, -1):
                block = place - way * k

                @pl.when((block >= 0) & (block < shards))
                def _():
                    mine = window(chunks[j], block, part)

                    @pl.when((place + way >= 0) & (place + way < shards))
                    def _():
                        wait_bytes(mine, pass_send.at[j, block])

                    wait_bytes(mine, x_send.at[j, block])
                    for which in range(2):
                        wait_bytes(mine, core_send.at[j, block, which])
                        wait_bytes(mine, core_recv.at[j, block, which])
    for index in range(count):
        stores(index).wait()


def gather_weights(pieces, shards, pace=192 * 1024):
    chunks = []
    for index, piece in enumerate(pieces):
        rows, width = piece.shape
        cuts = 1
        while rows % (2 * cuts * 16) == 0 and rows // cuts * (width // PARTS) > pace:
            cuts *= 2
        for cut in range(cuts):
            chunks.append((index, cut * (rows // cuts), rows // cuts))
    count, total = len(pieces), len(chunks)
    dma = pltpu.SemaphoreType.DMA
    return pl.pallas_call(
        functools.partial(gather_kernel, shards, tuple(chunks), count),
        out_shape=[jax.ShapeDtypeStruct((shards * p.shape[0], p.shape[1]), p.dtype) for p in pieces],
        in_specs=[pl.BlockSpec(memory_space=pl.ANY)] * count,
        out_specs=[pl.BlockSpec(memory_space=pl.ANY)] * count,
        scratch_shapes=[pltpu.VMEM(p.shape, p.dtype) for p in pieces]
        + [
            dma((count,)),
            dma((total, 2)),
            dma((total, shards)),
            dma((total, shards)),
            dma((total, shards)),
            dma((total, shards)),
            dma((total, shards, 2)),
            dma((total, shards, 2)),
        ],
        compiler_params=pltpu.CompilerParams(collective_id=0, has_side_effects=True, vmem_limit_bytes=24 * 1024 * 1024),
        name="gather_weights",
    )(*pieces)


LANES = 128


def add_rows(target, left, right, rows):
    step = next(size for size in (128, 64, 16) if rows % size == 0)

    def body(i, carry):
        window = pl.ds(pl.multiple_of(i * step, step), step)
        target[window, :] = (
            left[window, :].astype(jnp.float32) + right[window, :].astype(jnp.float32)
        ).astype(target.dtype)
        return carry

    lax.fori_loop(0, rows // step, body, 0)


def reduce_kernel(shards, plan, count, *refs):
    leads, trails, heights, kinds = plan
    chunks = leads + trails
    total = len(chunks)
    terms, refs = refs[:count], refs[count:]
    sums, refs = refs[:count], refs[count:]
    near, refs = refs[:count], refs[count:]
    landed, refs = refs[:total], refs[total:]
    passing, refs = refs[:total], refs[total:]
    swapped, refs = refs[: len(trails)], refs[len(trails) :]
    stages = []
    for kind in range(len(kinds)):
        stages.append(refs[:6])
        refs = refs[6:]
    trail_stage, refs = refs[:4], refs[4:]
    (load_sem, core_send, core_recv, x_send, x_recv, line_send, line_recv) = refs[:7]
    (end_local, end_x_send, end_x_recv, end_core_send, end_core_recv) = refs[7:]
    place = lax.axis_index("shard")
    member = lax.axis_index("replica")
    core = member % 2
    side = (member // 2) % 2
    x_mate = {"replica": member ^ 2}
    core_mate = {"replica": member ^ 1}
    greet(shards)

    def leading(j):
        return j < len(leads)

    def height(j):
        return heights[chunks[j][0]]

    def columns(j, whose):
        index, first, width = chunks[j]
        part = terms[index].shape[1] // PARTS
        return pl.ds(pl.multiple_of(whose * part + first, LANES), width)

    def send_near(j):
        index = chunks[j][0]
        for which in range(2):
            start_remote(
                terms[index].at[:, columns(j, (1 - core) * 2 + which)],
                near[index].at[:, columns(j, which)],
                core_send.at[j, which],
                core_recv.at[j, which],
                core_mate,
            )

    def staged(j):
        if leading(j):
            a0, a1, b0, b1, c, d = stages[kinds.index((height(j), chunks[j][2]))]
            return (b0, b1, c, d) if j % 2 else (a0, a1, c, d)
        return trail_stage

    def load_copies(j):
        index = chunks[j][0]
        whose = (1 - side, side) if leading(j) else (0, 1)
        at = staged(j)
        sem = 0 if leading(j) else 4
        sources = [terms[index].at[:, columns(j, core * 2 + w)] for w in whose]
        sources += [near[index].at[:, columns(j, w)] for w in whose]
        return [pltpu.make_async_copy(s, at[i], load_sem.at[sem + i]) for i, s in enumerate(sources)]

    def load(j):
        for which in range(2):
            wait_bytes(near[chunks[j][0]].at[:, columns(j, which)], core_recv.at[j, which])
        for copy in load_copies(j):
            copy.start()

    def near_sum(j):
        size = shards * height(j)
        at = staged(j)
        for copy in load_copies(j):
            copy.wait()
        if leading(j):
            add_rows(at[0], at[0], at[2], size)
            start_remote(at[0], landed[j], x_send.at[j], x_recv.at[j], x_mate)
            add_rows(at[1], at[1], at[3], size)
        else:
            width = chunks[j][2]
            for which in range(2):
                window = landed[j].at[:, pl.ds(which * width, width)]
                add_rows(window, at[which], at[2 + which], size)

    def x_sum(j):
        at = staged(j)
        wait_bytes(at[0], x_send.at[j])
        wait_bytes(landed[j], x_recv.at[j])
        add_rows(landed[j], landed[j], at[1], shards * height(j))

    def block(j, t):
        rows = height(j)
        return landed[j].at[pl.ds(pl.multiple_of(t * rows, rows), rows), :]

    def inside(t):
        return (t >= 0) & (t < shards)

    def line(j, hop):
        for slot, way in enumerate((1, -1)):
            t = place + way * (shards - hop)
            target = passing[j].at[slot, hop - 1]
            sems = (line_send.at[j, slot, hop - 1], line_recv.at[j, slot, hop - 1])
            ahead = {"shard": place + way}
            own = block(j, jnp.clip(t, 0, shards - 1))
            if hop == 1:

                @pl.when(inside(t))
                def _():
                    start_remote(own, target, *sems, ahead)
            else:
                arrived = passing[j].at[slot, hop - 2]

                @pl.when(inside(t) & inside(place - way))
                def _():
                    wait_bytes(arrived, line_recv.at[j, slot, hop - 2])
                    add_rows(arrived, arrived, own, height(j))
                    start_remote(arrived, target, *sems, ahead)

                @pl.when(inside(t) & jnp.logical_not(inside(place - way)))
                def _():
                    start_remote(own, target, *sems, ahead)

    def sum_window(j, whose):
        return sums[chunks[j][0]].at[:, columns(j, whose)]

    def share(j):
        width = chunks[j][2]
        for which in range(1 if leading(j) else 2):
            rows = block(j, place).at[:, pl.ds(which * width, width)]
            target = sum_window(j, core * 2 + (side if leading(j) else which))
            pltpu.make_async_copy(rows, target, end_local.at[j, which]).start()
            start_remote(rows, target, end_core_send.at[j, which], end_core_recv.at[j, which], core_mate)

    def line_end(j):
        mine = block(j, place)
        for slot, way in enumerate((1, -1)):

            @pl.when(inside(place - way))
            def _():
                arrived = passing[j].at[slot, shards - 2]
                wait_bytes(arrived, line_recv.at[j, slot, shards - 2])
                add_rows(mine, mine, arrived, height(j))

        target = sum_window(j, core * 2 + side) if leading(j) else swapped[j - len(leads)]
        start_remote(mine, target, end_x_send.at[j], end_x_recv.at[j], x_mate)
        if leading(j):
            share(j)

    def finish(j):
        if leading(j):
            theirs = sum_window(j, core * 2 + (1 - side))
            wait_bytes(theirs, end_x_recv.at[j])
            start_remote(theirs, theirs, end_core_send.at[j, 1], end_core_recv.at[j, 1], core_mate)
        else:
            mine, other = block(j, place), swapped[j - len(leads)]
            wait_bytes(mine, end_x_send.at[j])
            wait_bytes(other, end_x_recv.at[j])
            add_rows(mine, mine, other, height(j))
            share(j)

    first, second = len(leads), len(trails)
    for j in range(max(first, second)):
        if j < first:
            send_near(j)
        if j < second:
            send_near(first + j)
    load(0)
    load(first)
    for step in range(max(first + shards + 2, second + shards + 1)):
        if step < first:
            near_sum(step)
        if step < second:
            near_sum(first + step)
            if step + 1 < second:
                load(first + step + 1)
            line(first + step, 1)
        for hop in range(2, shards):
            if 0 <= step - hop < first:
                line(step - hop, hop)
            if 0 <= step - hop + 1 < second:
                line(first + step - hop + 1, hop)
        if 0 <= step - shards < first:
            line_end(step - shards)
        if 0 <= step - shards + 1 < second:
            line_end(first + step - shards + 1)
        if 0 <= step - shards - 1 < first:
            finish(step - shards - 1)
        if 0 <= step - shards < second:
            finish(first + step - shards)
        if 1 <= step <= first:
            x_sum(step - 1)
            line(step - 1, 1)
        if step + 1 < first:
            load(step + 1)

    for j in range(total):
        for which in range(2):
            wait_bytes(near[chunks[j][0]].at[:, columns(j, which)], core_send.at[j, which])
        for slot, way in enumerate((1, -1)):
            for hop in range(1, shards):

                @pl.when(inside(place + way * (shards - hop)))
                def _():
                    wait_bytes(passing[j].at[slot, hop - 1], line_send.at[j, slot, hop - 1])

        if leading(j):
            wait_bytes(sum_window(j, 0), end_x_send.at[j])
        for which in range(2):
            if which == 0 or not leading(j):
                wait_bytes(sum_window(j, 0), end_local.at[j, which])
            wait_bytes(sum_window(j, 0), end_core_send.at[j, which])
            wait_bytes(sum_window(j, 0), end_core_recv.at[j, which])


def reduce_terms(leading, trailing, shards, lead_cells=1536 * 256):
    terms = list(leading) + list(trailing)
    count = len(terms)
    heights = tuple(t.shape[0] // shards for t in terms)
    leads, trails = [], []
    for index, term in enumerate(terms):
        part = term.shape[1] // PARTS
        if index < len(leading):
            width = part
            while width % (2 * LANES) == 0 and width * term.shape[0] > lead_cells:
                width //= 2
            if width * term.shape[0] > lead_cells and width % LANES == 0:
                width = LANES
            leads += [(index, first, width) for first in range(0, part, width)]
        else:
            trails += [(index, first, LANES) for first in range(0, part, LANES)]
    kinds = []
    for index, first, width in leads:
        if (heights[index], width) not in kinds:
            kinds.append((heights[index], width))
    chunks = leads + trails
    total = len(chunks)
    bf16, dma = jnp.bfloat16, pltpu.SemaphoreType.DMA

    def rows_and_width(j):
        index, first, width = chunks[j]
        return heights[index], width if j < len(leads) else 2 * width

    scratch = []
    for j in range(total):
        rows, width = rows_and_width(j)
        scratch.append(pltpu.VMEM((shards * rows, width), bf16))
    for j in range(total):
        rows, width = rows_and_width(j)
        scratch.append(pltpu.VMEM((2, shards - 1, rows, width), bf16))
    for j in range(len(leads), total):
        rows, width = rows_and_width(j)
        scratch.append(pltpu.VMEM((rows, width), bf16))
    for rows, width in kinds:
        scratch += [pltpu.VMEM((shards * rows, width), bf16)] * 6
    scratch += [pltpu.VMEM((shards * heights[-1], LANES), bf16)] * 4
    scratch += [
        dma((8,)),
        dma((total, 2)),
        dma((total, 2)),
        dma((total,)),
        dma((total,)),
        dma((total, 2, shards - 1)),
        dma((total, 2, shards - 1)),
        dma((total, 2)),
        dma((total,)),
        dma((total,)),
        dma((total, 2)),
        dma((total, 2)),
    ]
    outs = pl.pallas_call(
        functools.partial(reduce_kernel, shards, (tuple(leads), tuple(trails), heights, tuple(kinds)), count),
        out_shape=[jax.ShapeDtypeStruct((t.shape[0] // shards, t.shape[1]), bf16) for t in terms]
        + [jax.ShapeDtypeStruct((t.shape[0], t.shape[1] // 2), bf16) for t in terms],
        in_specs=[pl.BlockSpec(memory_space=pl.ANY)] * count,
        out_specs=[pl.BlockSpec(memory_space=pl.ANY)] * (2 * count),
        scratch_shapes=scratch,
        compiler_params=pltpu.CompilerParams(
            collective_id=1, has_side_effects=True, vmem_limit_bytes=62 * 1024 * 1024
        ),
        name="reduce_terms",
    )(*terms)
    return outs[:count]


def swap(x, bit):
    members = lax.axis_size("replica")
    return lax.ppermute(x, "replica", [(r, r ^ (1 << bit)) for r in range(members)])


def gain_width(rows):
    return -(-2 * rows // (PARTS * LANES)) * PARTS * LANES


def gather_layer(pieces):
    norm_attn, w_query, w_key, w_value, w_out, norm_ffn, w_gate, w_up, w_down = pieces
    rows = norm_attn.shape[0]
    gains = jnp.concatenate([norm_attn, norm_ffn])
    gains = jnp.pad(gains[None], ((0, 15), (0, gain_width(rows) - 2 * rows)))
    w_qkv = jnp.concatenate([w_query, w_key, w_value], axis=1)
    shards = lax.axis_size("shard")
    w_qkv, w_out, w_gate, w_up, w_down, gains = gather_weights(
        [w_qkv, w_out, w_gate, w_up, w_down, gains], shards
    )
    gains = gains.reshape(shards, 16, -1)[:, 0]
    norm_attn = gains[:, :rows].reshape(-1)
    norm_ffn = gains[:, rows : 2 * rows].reshape(-1)
    return norm_attn, w_qkv, w_out, norm_ffn, w_gate, w_up, w_down


def forward_layer(inputs, weights, segment, row_start):
    norm_attn, w_qkv, w_out, norm_ffn, w_gate, w_up, w_down = weights
    row_count = inputs.shape[0]
    seq_length = segment.shape[0]
    groups = QH // KVH
    half_dim = HD // 2
    local_segment = lax.dynamic_slice_in_dim(segment, row_start, row_count)
    query_index = row_start + jnp.arange(row_count, dtype=jnp.int32)
    starts = jnp.sum((segment[None, :] < local_segment[:, None]).astype(jnp.int32), axis=1)
    positions = query_index - starts
    frequency = ROPE_BASE ** (-(jnp.arange(half_dim, dtype=jnp.float32) * 2.0) / HD)
    angles = positions.astype(jnp.float32)[:, None, None] * frequency[None, None, :]
    cosine_table = jnp.cos(angles)
    sine_table = jnp.sin(angles)
    recip_one = lax.rsqrt(jnp.mean(inputs * inputs, axis=-1, keepdims=True) + EPSILON)
    scaled = inputs * recip_one
    normed = (scaled * norm_attn.astype(jnp.float32)).astype(jnp.bfloat16)
    raw = jnp.dot(normed, w_qkv, preferred_element_type=jnp.float32)
    raw_query, raw_key, raw_value = jnp.split(raw, [QH * HD, (QH + KVH) * HD], axis=1)
    raw_query = raw_query.reshape(row_count, KVH, groups, HD)
    queries = rotate(raw_query, cosine_table[:, :, None, :], sine_table[:, :, None, :], 1.0).astype(
        jnp.bfloat16
    )
    raw_key = raw_key.reshape(row_count, KVH, HD)
    key_rows = (
        rotate(raw_key, cosine_table, sine_table, 1.0)
        .astype(jnp.bfloat16)
        .reshape(row_count, KVH * HD)
    )
    value_rows = raw_value.astype(jnp.bfloat16)
    all_keys, all_values = (
        lax.all_gather(key_rows, "shard", axis=0, tiled=True),
        lax.all_gather(value_rows, "shard", axis=0, tiled=True),
    )
    all_keys = all_keys.reshape(seq_length, KVH, HD)
    all_values = all_values.reshape(seq_length, KVH, HD)
    key_index = jnp.arange(seq_length, dtype=jnp.int32)
    allowed = (key_index[None, :] <= query_index[:, None]) & (
        segment[None, :] == local_segment[:, None]
    )
    scores = jnp.einsum(
        "ihgd,jhd->hgij", queries, all_keys, preferred_element_type=jnp.float32
    ) * HD ** (-0.5)
    scores = jnp.where(allowed, scores, -1e30)
    row_top = jnp.max(scores, axis=-1, keepdims=True)
    exponent = jnp.exp(scores - row_top)
    row_total = jnp.sum(exponent, axis=-1, keepdims=True)
    probabilities = exponent / row_total
    log_total = row_top + jnp.log(row_total)
    attended = jnp.einsum(
        "hgij,jhd->ihgd",
        probabilities.astype(jnp.bfloat16),
        all_values,
        preferred_element_type=jnp.float32,
    )
    attended = attended.reshape(row_count, QH * HD).astype(jnp.bfloat16)
    middle = inputs + jnp.dot(attended, w_out, preferred_element_type=jnp.float32)
    recip_two = lax.rsqrt(jnp.mean(middle * middle, axis=-1, keepdims=True) + EPSILON)
    scaled_mid = middle * recip_two
    normed_mid = (scaled_mid * norm_ffn.astype(jnp.float32)).astype(jnp.bfloat16)
    gate_proj = jnp.dot(normed_mid, w_gate, preferred_element_type=jnp.float32)
    up_proj = jnp.dot(normed_mid, w_up, preferred_element_type=jnp.float32)
    hidden = (jax.nn.silu(gate_proj) * up_proj).astype(jnp.bfloat16)
    result = middle + jnp.dot(hidden, w_down, preferred_element_type=jnp.float32)
    saved = (
        scaled,
        recip_one,
        normed,
        queries,
        all_keys,
        all_values,
        allowed,
        log_total,
        attended,
        scaled_mid,
        recip_two,
        normed_mid,
        gate_proj,
        up_proj,
        hidden,
        cosine_table,
        sine_table,
    )
    return (result, saved)


def backward_layer(grad_result, weights, saved):
    norm_attn, w_qkv, w_out, norm_ffn, w_gate, w_up, w_down = weights
    (
        scaled,
        recip_one,
        normed,
        queries,
        all_keys,
        all_values,
        allowed,
        log_total,
        attended,
        scaled_mid,
        recip_two,
        normed_mid,
        gate_proj,
        up_proj,
        hidden,
        cosine_table,
        sine_table,
    ) = saved
    row_count = grad_result.shape[0]
    seq_length = all_keys.shape[0]
    groups = QH // KVH
    score_scale = HD ** (-0.5)
    branch_grad = grad_result.astype(jnp.bfloat16)
    grad_hidden = jnp.einsum("td,fd->tf", branch_grad, w_down, preferred_element_type=jnp.float32)
    sigmoid_gate = jax.nn.sigmoid(gate_proj)
    gate_low = (
        grad_hidden * up_proj * (sigmoid_gate * (1.0 + gate_proj * (1.0 - sigmoid_gate)))
    ).astype(jnp.bfloat16)
    up_low = (grad_hidden * jax.nn.silu(gate_proj)).astype(jnp.bfloat16)
    grad_normed_mid = jnp.einsum("tf,df->td", gate_low, w_gate, preferred_element_type=jnp.float32)
    grad_normed_mid = grad_normed_mid + jnp.einsum(
        "tf,df->td", up_low, w_up, preferred_element_type=jnp.float32
    )
    grad_norm_ffn = jnp.sum(grad_normed_mid * scaled_mid, axis=0)
    grad_scaled_mid = grad_normed_mid * norm_ffn.astype(jnp.float32)
    grad_middle = grad_result + recip_two * (
        grad_scaled_mid
        - scaled_mid * jnp.mean(grad_scaled_mid * scaled_mid, axis=-1, keepdims=True)
    )
    attn_grad = grad_middle.astype(jnp.bfloat16)
    grad_attended = jnp.einsum("td,qd->tq", attn_grad, w_out, preferred_element_type=jnp.float32)
    grad_attended = grad_attended.astype(jnp.bfloat16).reshape(row_count, KVH, groups, HD)
    scores = (
        jnp.einsum("ihgd,jhd->hgij", queries, all_keys, preferred_element_type=jnp.float32)
        * score_scale
    )
    scores = jnp.where(allowed, scores, -1e30)
    probabilities = jnp.exp(scores - log_total)
    grad_probs = jnp.einsum(
        "ihgd,jhd->hgij", grad_attended, all_values, preferred_element_type=jnp.float32
    )
    row_dot = jnp.sum(probabilities * grad_probs, axis=-1, keepdims=True)
    grad_scores = (probabilities * (grad_probs - row_dot)).astype(jnp.bfloat16)
    grad_queries = (
        jnp.einsum("hgij,jhd->ihgd", grad_scores, all_keys, preferred_element_type=jnp.float32)
        * score_scale
    )
    key_terms = (
        jnp.einsum("hgij,ihgd->jhd", grad_scores, queries, preferred_element_type=jnp.float32)
        * score_scale
    )
    value_terms = jnp.einsum(
        "hgij,ihgd->jhd",
        probabilities.astype(jnp.bfloat16),
        grad_attended,
        preferred_element_type=jnp.float32,
    )
    key_terms = key_terms.reshape(seq_length, KVH * HD)
    value_terms = value_terms.reshape(seq_length, KVH * HD)
    grad_keys, grad_values = (
        lax.psum_scatter(
            key_terms.astype(jnp.bfloat16), "shard", scatter_dimension=0, tiled=True
        ).astype(jnp.float32),
        lax.psum_scatter(
            value_terms.astype(jnp.bfloat16), "shard", scatter_dimension=0, tiled=True
        ).astype(jnp.float32),
    )
    query_low = rotate(grad_queries, cosine_table[:, :, None, :], sine_table[:, :, None, :], -1.0)
    query_low = query_low.reshape(row_count, QH * HD).astype(jnp.bfloat16)
    key_low = rotate(grad_keys.reshape(row_count, KVH, HD), cosine_table, sine_table, -1.0)
    key_low = key_low.reshape(row_count, KVH * HD).astype(jnp.bfloat16)
    value_low = grad_values.astype(jnp.bfloat16)
    qkv_low = jnp.concatenate([query_low, key_low, value_low], axis=1)
    grad_normed = jnp.einsum("tq,dq->td", qkv_low, w_qkv, preferred_element_type=jnp.float32)
    grad_norm_attn = jnp.sum(grad_normed * scaled, axis=0)
    grad_scaled = grad_normed * norm_attn.astype(jnp.float32)
    grad_inputs = grad_middle + recip_one * (
        grad_scaled - scaled * jnp.mean(grad_scaled * scaled, axis=-1, keepdims=True)
    )
    operands = (
        normed,
        qkv_low,
        attended,
        attn_grad,
        normed_mid,
        gate_low,
        up_low,
        hidden,
        branch_grad,
    )
    return (grad_inputs, (grad_norm_attn, grad_norm_ffn), operands)


def row_product(left, right):
    return jnp.einsum("td,tq->dq", left, right, preferred_element_type=jnp.float32)


def reduce_gradients(operand_pairs, gains):
    (
        normed,
        qkv_low,
        attended,
        attn_grad,
        normed_mid,
        gate_low,
        up_low,
        hidden,
        branch_grad,
    ) = zip(*operand_pairs)
    shards = lax.axis_size("shard")
    rows = gains[0].shape[0] // shards

    def product(lefts, rights):
        return sum(row_product(left, right) for left, right in zip(lefts, rights)).astype(
            jnp.bfloat16
        )

    gain_term = jnp.stack([gain.reshape(shards, rows) for gain in gains], axis=1)
    gain_term = gain_term.reshape(shards, 1, 2 * rows).astype(jnp.bfloat16)
    gain_term = jnp.pad(gain_term, ((0, 0), (0, 15), (0, gain_width(rows) - 2 * rows)))
    leading = [
        product(hidden, branch_grad),
        product(normed_mid, gate_low),
        product(normed_mid, up_low),
        gain_term.reshape(shards * 16, -1),
    ]
    trailing = [product(normed, qkv_low), product(attended, attn_grad)]
    totals = [total.astype(jnp.float32) for total in reduce_terms(leading, trailing, shards)]
    members = lax.axis_size("replica")
    for bit in range(PARTS.bit_length() - 1, members.bit_length() - 1):
        totals = [total + swap(total, bit) for total in totals]
    down, gate, up, own_gains, qkv, out = totals
    return (
        own_gains[0, :rows],
        qkv[:, : QH * HD],
        qkv[:, QH * HD : (QH + KVH) * HD],
        qkv[:, (QH + KVH) * HD :],
        out,
        own_gains[0, rows : 2 * rows],
        gate,
        up,
        down,
    )


def add_terms(earlier, later):
    if earlier is None:
        return later
    return tuple((left_term + right_term for left_term, right_term in zip(earlier, later)))


def body(
    tokens,
    segments,
    norm_attn,
    w_query,
    w_key,
    w_value,
    w_out,
    norm_ffn,
    w_gate,
    w_up,
    w_down,
    cotangent,
):
    micro_count = tokens.shape[0]
    row_count = tokens.shape[2]
    width = tokens.shape[3]
    first_section = lax.axis_index("section") == 0
    row_start = lax.axis_index("shard") * row_count
    pieces = (
        norm_attn[0],
        w_query[0],
        w_key[0],
        w_value[0],
        w_out[0],
        norm_ffn[0],
        w_gate[0],
        w_up[0],
        w_down[0],
    )
    held_weights = gather_layer(pieces)
    saved_ticks = []
    result_ticks = []
    arriving = jnp.zeros((row_count, width), jnp.bfloat16)
    for tick_index in range(micro_count + 1):
        weights = held_weights
        own_input = tokens[min(tick_index, micro_count - 1), 0].astype(jnp.float32)
        layer_input = jnp.where(first_section, own_input, arriving.astype(jnp.float32))
        segment = jnp.where(
            first_section,
            segments[min(tick_index, micro_count - 1), 0],
            segments[max(tick_index - 1, 0), 0],
        )
        result, saved = forward_layer(layer_input, weights, segment, row_start)
        result_low = result.astype(jnp.bfloat16)
        result_ticks.append(result_low)
        saved_ticks.append(saved)
        if tick_index < micro_count:
            arriving = from_behind(result_low, "section", 1)
    flow_ticks = []
    gain_sums = None
    operand_ticks = []
    returning = jnp.zeros((row_count, width), jnp.bfloat16)
    for tick_index in range(micro_count + 1):
        weights = held_weights
        later_grad = cotangent[min(tick_index, micro_count - 1), 0].astype(jnp.float32)
        incoming = jnp.where(first_section, returning.astype(jnp.float32), later_grad)
        active = jnp.where(first_section, tick_index >= 1, tick_index < micro_count)
        incoming = jnp.where(active, incoming, 0.0)
        if 0 < tick_index < micro_count:
            saved = jax.tree.map(
                lambda early_value, late_value: jnp.where(first_section, early_value, late_value),
                saved_ticks[tick_index - 1],
                saved_ticks[tick_index + 1],
            )
        else:
            saved = saved_ticks[1 if tick_index == 0 else micro_count - 1]
        grad_inputs, gains, operands = backward_layer(incoming, weights, saved)
        flow_ticks.append(grad_inputs)
        if tick_index < micro_count:
            returning = from_behind(grad_inputs.astype(jnp.bfloat16), "section", -1)
        gain_sums = add_terms(gain_sums, gains)
        operand_ticks.append(operands)
    first_ops, last_ops = operand_ticks[0], operand_ticks[micro_count]
    edge_ops = jax.tree.map(
        lambda early_value, late_value: jnp.where(first_section, late_value, early_value),
        first_ops,
        last_ops,
    )
    totals = reduce_gradients(operand_ticks[1:micro_count] + [edge_ops], gain_sums)
    section_outputs = jnp.stack(
        [
            jnp.where(first_section, result_ticks[index_micro], result_ticks[index_micro + 1])
            for index_micro in range(micro_count)
        ]
    )
    input_grads = jnp.stack(
        [
            jnp.where(first_section, flow_ticks[index_micro + 1], flow_ticks[index_micro])
            for index_micro in range(micro_count)
        ]
    )
    return (
        section_outputs[None, :, None],
        input_grads[None, :, None],
        totals[0][None],
        totals[1][None],
        totals[2][None],
        totals[3][None],
        totals[4][None],
        totals[5][None],
        totals[6][None],
        totals[7][None],
        totals[8][None],
    )


def solution(mesh):
    in_specs = (
        P(None, "replica", "shard", None),
        P(None, "replica", None),
        P("section", "shard"),
        P("section", "shard", None),
        P("section", "shard", None),
        P("section", "shard", None),
        P("section", "shard", None),
        P("section", "shard"),
        P("section", "shard", None),
        P("section", "shard", None),
        P("section", "shard", None),
        P(None, "replica", "shard", None),
    )
    out_specs = (
        P("section", None, "replica", "shard", None),
        P("section", None, "replica", "shard", None),
        P("section", "shard"),
        P("section", "shard", None),
        P("section", "shard", None),
        P("section", "shard", None),
        P("section", "shard", None),
        P("section", "shard"),
        P("section", "shard", None),
        P("section", "shard", None),
        P("section", "shard", None),
    )
    return jax.shard_map(body, mesh=mesh, in_specs=in_specs, out_specs=out_specs, check_vma=False)
```

```python
import functools

import jax
import jax.numpy as jnp
import numpy as np
from jax import lax
from jax.experimental import pallas as pl
from jax.experimental.pallas import tpu as pltpu
from jax.sharding import PartitionSpec as P

QH = 16
KVH = 8
HD = 96
PARTS = 4
LANES = 128


EPSILON = 1e-05
ROPE_BASE = 100000.0


def start_remote(source, target, send_sem, recv_sem, device):
    pltpu.make_async_remote_copy(
        src_ref=source,
        dst_ref=target,
        send_sem=send_sem,
        recv_sem=recv_sem,
        device_id=device,
        device_id_type=pl.DeviceIdType.MESH,
    ).start()


def wait_bytes(ref, sem):
    pltpu.make_async_copy(ref, ref, sem).wait()


def greet(shards):
    place = lax.axis_index("shard")
    member = lax.axis_index("replica")
    barrier = pltpu.get_barrier_semaphore()
    pl.semaphore_signal(barrier, inc=1, device_id={"replica": member ^ 1}, device_id_type=pl.DeviceIdType.MESH)
    pl.semaphore_signal(barrier, inc=1, device_id={"replica": member ^ 2}, device_id_type=pl.DeviceIdType.MESH)

    @pl.when(place > 0)
    def _():
        pl.semaphore_signal(barrier, inc=1, device_id={"shard": place - 1}, device_id_type=pl.DeviceIdType.MESH)

    @pl.when(place < shards - 1)
    def _():
        pl.semaphore_signal(barrier, inc=1, device_id={"shard": place + 1}, device_id_type=pl.DeviceIdType.MESH)

    pl.semaphore_wait(barrier, 2 + (place > 0).astype(jnp.int32) + (place < shards - 1).astype(jnp.int32))


def gather_kernel(shards, chunks, count, *refs):
    pieces, wholes = refs[:count], refs[count : 2 * count]
    held = refs[2 * count : 3 * count]
    (local_sem, own_send, pass_send, line_recv, x_send, x_recv, core_send, core_recv) = refs[
        3 * count :
    ]
    place = lax.axis_index("shard")
    member = lax.axis_index("replica")
    part = member % PARTS
    greet(shards)

    def loads(index):
        return pltpu.make_async_copy(pieces[index], held[index], local_sem.at[index])

    def stores(index):
        rows = pieces[index].shape[0]
        target = wholes[index].at[pl.ds(pl.multiple_of(place * rows, rows), rows), :]
        return pltpu.make_async_copy(held[index], target, local_sem.at[index])

    for index in range(count):
        loads(index).start()

    def window(chunk, block, whose):
        index, first, length = chunk
        rows = pieces[index].shape[0]
        width = pieces[index].shape[1] // PARTS
        return wholes[index].at[
            pl.ds(pl.multiple_of(block * rows + first, length), length),
            pl.ds(pl.multiple_of(whose * width, width), width),
        ]

    def own(j):
        index, first, length = chunks[j]
        width = pieces[index].shape[1] // PARTS
        source = pieces[index].at[
            pl.ds(first, length), pl.ds(pl.multiple_of(part * width, width), width)
        ]
        for slot, way in enumerate((1, -1)):
            @pl.when((place + way >= 0) & (place + way < shards))
            def _():
                start_remote(
                    source,
                    window(chunks[j], place, part),
                    own_send.at[j, slot],
                    line_recv.at[j, place],
                    {"shard": place + way},
                )

    def hop(j, k):
        for way in (1, -1):
            block = place - way * k

            @pl.when((block >= 0) & (block < shards))
            def _():
                mine = window(chunks[j], block, part)
                wait_bytes(mine, line_recv.at[j, block])

                @pl.when((place + way >= 0) & (place + way < shards))
                def _():
                    start_remote(
                        mine, mine, pass_send.at[j, block], line_recv.at[j, block], {"shard": place + way}
                    )

                start_remote(mine, mine, x_send.at[j, block], x_recv.at[j, block], {"replica": member ^ 2})
                start_remote(
                    mine, mine, core_send.at[j, block, 0], core_recv.at[j, block, 0], {"replica": member ^ 1}
                )

    def across(j, k):
        for way in (1, -1):
            block = place - way * k

            @pl.when((block >= 0) & (block < shards))
            def _():
                theirs = window(chunks[j], block, part ^ 2)
                wait_bytes(theirs, x_recv.at[j, block])
                start_remote(
                    theirs, theirs, core_send.at[j, block, 1], core_recv.at[j, block, 1], {"replica": member ^ 1}
                )

    total = len(chunks)
    for step in range(total + shards + 1):
        if step < total:
            own(step)
        if 1 <= step <= count:
            loads(step - 1).wait()
            stores(step - 1).start()
        for k in range(1, shards):
            if 0 <= step - k < total:
                hop(step - k, k)
        for k in range(1, shards):
            if 0 <= step - k - 1 < total:
                across(step - k - 1, k)

    for j in range(total):
        for slot, way in enumerate((1, -1)):
            @pl.when((place + way >= 0) & (place + way < shards))
            def _():
                wait_bytes(window(chunks[j], place, part), own_send.at[j, slot])

        for k in range(1, shards):
            for way in (1, -1):
                block = place - way * k

                @pl.when((block >= 0) & (block < shards))
                def _():
                    mine = window(chunks[j], block, part)

                    @pl.when((place + way >= 0) & (place + way < shards))
                    def _():
                        wait_bytes(mine, pass_send.at[j, block])

                    wait_bytes(mine, x_send.at[j, block])
                    for which in range(2):
                        wait_bytes(mine, core_send.at[j, block, which])
                        wait_bytes(mine, core_recv.at[j, block, which])
    for index in range(count):
        stores(index).wait()


def gather_weights(pieces, shards, pace=192 * 1024):
    chunks = []
    for index, piece in enumerate(pieces):
        rows, width = piece.shape
        cuts = 1
        while rows % (2 * cuts * 16) == 0 and rows // cuts * (width // PARTS) > pace:
            cuts *= 2
        for cut in range(cuts):
            chunks.append((index, cut * (rows // cuts), rows // cuts))
    count, total = len(pieces), len(chunks)
    dma = pltpu.SemaphoreType.DMA
    return pl.pallas_call(
        functools.partial(gather_kernel, shards, tuple(chunks), count),
        out_shape=[jax.ShapeDtypeStruct((shards * p.shape[0], p.shape[1]), p.dtype) for p in pieces],
        in_specs=[pl.BlockSpec(memory_space=pl.ANY)] * count,
        out_specs=[pl.BlockSpec(memory_space=pl.ANY)] * count,
        scratch_shapes=[pltpu.VMEM(p.shape, p.dtype) for p in pieces]
        + [
            dma((count,)),
            dma((total, 2)),
            dma((total, shards)),
            dma((total, shards)),
            dma((total, shards)),
            dma((total, shards)),
            dma((total, shards, 2)),
            dma((total, shards, 2)),
        ],
        compiler_params=pltpu.CompilerParams(collective_id=0, has_side_effects=True, vmem_limit_bytes=24 * 1024 * 1024),
        name="gather_weights",
    )(*pieces)


def add_rows(target, left, right, rows):
    step = next(size for size in (128, 64, 16) if rows % size == 0)

    def body(i, carry):
        window = pl.ds(pl.multiple_of(i * step, step), step)
        target[window, :] = (
            left[window, :].astype(jnp.float32) + right[window, :].astype(jnp.float32)
        ).astype(target.dtype)
        return carry

    lax.fori_loop(0, rows // step, body, 0)


def reduce_kernel(shards, plan, count, *refs):
    leads, trails, heights, kinds = plan
    chunks = leads + trails
    total = len(chunks)
    terms, refs = refs[:count], refs[count:]
    sums, refs = refs[:count], refs[count:]
    near, refs = refs[:count], refs[count:]
    landed, refs = refs[:total], refs[total:]
    passing, refs = refs[:total], refs[total:]
    swapped, refs = refs[: len(trails)], refs[len(trails) :]
    stages = []
    for kind in range(len(kinds)):
        stages.append(refs[:6])
        refs = refs[6:]
    trail_stage, refs = refs[:4], refs[4:]
    (load_sem, core_send, core_recv, x_send, x_recv, line_send, line_recv) = refs[:7]
    (end_local, end_x_send, end_x_recv, end_core_send, end_core_recv) = refs[7:]
    place = lax.axis_index("shard")
    member = lax.axis_index("replica")
    core = member % 2
    side = (member // 2) % 2
    x_mate = {"replica": member ^ 2}
    core_mate = {"replica": member ^ 1}
    greet(shards)

    def leading(j):
        return j < len(leads)

    def height(j):
        return heights[chunks[j][0]]

    def columns(j, whose):
        index, first, width = chunks[j]
        part = terms[index].shape[1] // PARTS
        return pl.ds(pl.multiple_of(whose * part + first, LANES), width)

    def send_near(j):
        index = chunks[j][0]
        for which in range(2):
            start_remote(
                terms[index].at[:, columns(j, (1 - core) * 2 + which)],
                near[index].at[:, columns(j, which)],
                core_send.at[j, which],
                core_recv.at[j, which],
                core_mate,
            )

    def staged(j):
        if leading(j):
            a0, a1, b0, b1, c, d = stages[kinds.index((height(j), chunks[j][2]))]
            return (b0, b1, c, d) if j % 2 else (a0, a1, c, d)
        return trail_stage

    def load_copies(j):
        index = chunks[j][0]
        whose = (1 - side, side) if leading(j) else (0, 1)
        at = staged(j)
        sem = 0 if leading(j) else 4
        sources = [terms[index].at[:, columns(j, core * 2 + w)] for w in whose]
        sources += [near[index].at[:, columns(j, w)] for w in whose]
        return [pltpu.make_async_copy(s, at[i], load_sem.at[sem + i]) for i, s in enumerate(sources)]

    def load(j):
        for which in range(2):
            wait_bytes(near[chunks[j][0]].at[:, columns(j, which)], core_recv.at[j, which])
        for copy in load_copies(j):
            copy.start()

    def near_sum(j):
        size = shards * height(j)
        at = staged(j)
        for copy in load_copies(j):
            copy.wait()
        if leading(j):
            add_rows(at[0], at[0], at[2], size)
            start_remote(at[0], landed[j], x_send.at[j], x_recv.at[j], x_mate)
            add_rows(at[1], at[1], at[3], size)
        else:
            width = chunks[j][2]
            for which in range(2):
                window = landed[j].at[:, pl.ds(which * width, width)]
                add_rows(window, at[which], at[2 + which], size)

    def x_sum(j):
        at = staged(j)
        wait_bytes(at[0], x_send.at[j])
        wait_bytes(landed[j], x_recv.at[j])
        add_rows(landed[j], landed[j], at[1], shards * height(j))

    def block(j, t):
        rows = height(j)
        return landed[j].at[pl.ds(pl.multiple_of(t * rows, rows), rows), :]

    def inside(t):
        return (t >= 0) & (t < shards)

    def line(j, hop):
        for slot, way in enumerate((1, -1)):
            t = place + way * (shards - hop)
            target = passing[j].at[slot, hop - 1]
            sems = (line_send.at[j, slot, hop - 1], line_recv.at[j, slot, hop - 1])
            ahead = {"shard": place + way}
            own = block(j, jnp.clip(t, 0, shards - 1))
            if hop == 1:

                @pl.when(inside(t))
                def _():
                    start_remote(own, target, *sems, ahead)
            else:
                arrived = passing[j].at[slot, hop - 2]

                @pl.when(inside(t) & inside(place - way))
                def _():
                    wait_bytes(arrived, line_recv.at[j, slot, hop - 2])
                    add_rows(arrived, arrived, own, height(j))
                    start_remote(arrived, target, *sems, ahead)

                @pl.when(inside(t) & jnp.logical_not(inside(place - way)))
                def _():
                    start_remote(own, target, *sems, ahead)

    def sum_window(j, whose):
        return sums[chunks[j][0]].at[:, columns(j, whose)]

    def share(j):
        width = chunks[j][2]
        for which in range(1 if leading(j) else 2):
            rows = block(j, place).at[:, pl.ds(which * width, width)]
            target = sum_window(j, core * 2 + (side if leading(j) else which))
            pltpu.make_async_copy(rows, target, end_local.at[j, which]).start()
            start_remote(rows, target, end_core_send.at[j, which], end_core_recv.at[j, which], core_mate)

    def line_end(j):
        mine = block(j, place)
        for slot, way in enumerate((1, -1)):

            @pl.when(inside(place - way))
            def _():
                arrived = passing[j].at[slot, shards - 2]
                wait_bytes(arrived, line_recv.at[j, slot, shards - 2])
                add_rows(mine, mine, arrived, height(j))

        target = sum_window(j, core * 2 + side) if leading(j) else swapped[j - len(leads)]
        start_remote(mine, target, end_x_send.at[j], end_x_recv.at[j], x_mate)
        if leading(j):
            share(j)

    def finish(j):
        if leading(j):
            theirs = sum_window(j, core * 2 + (1 - side))
            wait_bytes(theirs, end_x_recv.at[j])
            start_remote(theirs, theirs, end_core_send.at[j, 1], end_core_recv.at[j, 1], core_mate)
        else:
            mine, other = block(j, place), swapped[j - len(leads)]
            wait_bytes(mine, end_x_send.at[j])
            wait_bytes(other, end_x_recv.at[j])
            add_rows(mine, mine, other, height(j))
            share(j)

    first, second = len(leads), len(trails)
    for j in range(max(first, second)):
        if j < first:
            send_near(j)
        if j < second:
            send_near(first + j)
    load(0)
    load(first)
    for step in range(max(first + shards + 2, second + shards + 1)):
        if step < first:
            near_sum(step)
        if step < second:
            near_sum(first + step)
            if step + 1 < second:
                load(first + step + 1)
            line(first + step, 1)
        for hop in range(2, shards):
            if 0 <= step - hop < first:
                line(step - hop, hop)
            if 0 <= step - hop + 1 < second:
                line(first + step - hop + 1, hop)
        if 0 <= step - shards < first:
            line_end(step - shards)
        if 0 <= step - shards + 1 < second:
            line_end(first + step - shards + 1)
        if 0 <= step - shards - 1 < first:
            finish(step - shards - 1)
        if 0 <= step - shards < second:
            finish(first + step - shards)
        if 1 <= step <= first:
            x_sum(step - 1)
            line(step - 1, 1)
        if step + 1 < first:
            load(step + 1)

    for j in range(total):
        for which in range(2):
            wait_bytes(near[chunks[j][0]].at[:, columns(j, which)], core_send.at[j, which])
        for slot, way in enumerate((1, -1)):
            for hop in range(1, shards):

                @pl.when(inside(place + way * (shards - hop)))
                def _():
                    wait_bytes(passing[j].at[slot, hop - 1], line_send.at[j, slot, hop - 1])

        if leading(j):
            wait_bytes(sum_window(j, 0), end_x_send.at[j])
        for which in range(2):
            if which == 0 or not leading(j):
                wait_bytes(sum_window(j, 0), end_local.at[j, which])
            wait_bytes(sum_window(j, 0), end_core_send.at[j, which])
            wait_bytes(sum_window(j, 0), end_core_recv.at[j, which])


def reduce_terms(leading, trailing, shards, lead_cells=1536 * 256):
    terms = list(leading) + list(trailing)
    count = len(terms)
    heights = tuple(t.shape[0] // shards for t in terms)
    leads, trails = [], []
    for index, term in enumerate(terms):
        part = term.shape[1] // PARTS
        if index < len(leading):
            width = part
            while width % (2 * LANES) == 0 and width * term.shape[0] > lead_cells:
                width //= 2
            if width * term.shape[0] > lead_cells and width % LANES == 0:
                width = LANES
            leads += [(index, first, width) for first in range(0, part, width)]
        else:
            trails += [(index, first, LANES) for first in range(0, part, LANES)]
    kinds = []
    for index, first, width in leads:
        if (heights[index], width) not in kinds:
            kinds.append((heights[index], width))
    chunks = leads + trails
    total = len(chunks)
    bf16, dma = jnp.bfloat16, pltpu.SemaphoreType.DMA

    def rows_and_width(j):
        index, first, width = chunks[j]
        return heights[index], width if j < len(leads) else 2 * width

    scratch = []
    for j in range(total):
        rows, width = rows_and_width(j)
        scratch.append(pltpu.VMEM((shards * rows, width), bf16))
    for j in range(total):
        rows, width = rows_and_width(j)
        scratch.append(pltpu.VMEM((2, shards - 1, rows, width), bf16))
    for j in range(len(leads), total):
        rows, width = rows_and_width(j)
        scratch.append(pltpu.VMEM((rows, width), bf16))
    for rows, width in kinds:
        scratch += [pltpu.VMEM((shards * rows, width), bf16)] * 6
    scratch += [pltpu.VMEM((shards * heights[-1], LANES), bf16)] * 4
    scratch += [
        dma((8,)),
        dma((total, 2)),
        dma((total, 2)),
        dma((total,)),
        dma((total,)),
        dma((total, 2, shards - 1)),
        dma((total, 2, shards - 1)),
        dma((total, 2)),
        dma((total,)),
        dma((total,)),
        dma((total, 2)),
        dma((total, 2)),
    ]
    outs = pl.pallas_call(
        functools.partial(reduce_kernel, shards, (tuple(leads), tuple(trails), heights, tuple(kinds)), count),
        out_shape=[jax.ShapeDtypeStruct((t.shape[0] // shards, t.shape[1]), bf16) for t in terms]
        + [jax.ShapeDtypeStruct((t.shape[0], t.shape[1] // 2), bf16) for t in terms],
        in_specs=[pl.BlockSpec(memory_space=pl.ANY)] * count,
        out_specs=[pl.BlockSpec(memory_space=pl.ANY)] * (2 * count),
        scratch_shapes=scratch,
        compiler_params=pltpu.CompilerParams(
            collective_id=1, has_side_effects=True, vmem_limit_bytes=62 * 1024 * 1024
        ),
        name="reduce_terms",
    )(*terms)
    return outs[:count]


def tile_order():
    order = np.zeros(4 * HD, np.int32)
    for tile in range(3):
        for lane in range(LANES):
            upper, low = divmod(lane, LANES // 2)
            if low < HD // 2:
                head, item = tile, low
            else:
                head, item = 3, 16 * tile + low - HD // 2
            order[tile * LANES + lane] = head * HD + upper * (HD // 2) + item
    return order


def tile_matrix():
    order = tile_order()
    return (np.arange(4 * HD)[:, None] == order[None, :]).astype(np.float32)


def to_tiles(x):
    matrix = jnp.asarray(tile_matrix(), jnp.bfloat16)
    span = 4 * HD
    return jnp.concatenate(
        [
            jnp.dot(x[:, i : i + span], matrix, preferred_element_type=jnp.float32).astype(x.dtype)
            for i in range(0, x.shape[1], span)
        ],
        axis=1,
    )


def from_tiles(x):
    matrix = jnp.asarray(tile_matrix().T, jnp.bfloat16)
    span = 4 * HD
    return jnp.concatenate(
        [
            jnp.dot(x[:, i : i + span], matrix, preferred_element_type=jnp.float32).astype(x.dtype)
            for i in range(0, x.shape[1], span)
        ],
        axis=1,
    )


def rows_to_tiles(x):
    matrix = jnp.asarray(tile_matrix().T, jnp.bfloat16)
    groups = x.reshape(-1, 4 * HD, x.shape[1])
    moved = jnp.einsum("lk,gkn->gln", matrix, groups, preferred_element_type=jnp.float32)
    return moved.astype(x.dtype).reshape(x.shape)


def rope_tables(positions):
    item = tile_order() % (HD // 2)
    frequency = ROPE_BASE ** (-(jnp.asarray(item, jnp.float32) * 2.0) / HD)
    angles = positions.astype(jnp.float32)[:, None] * frequency[None, :]
    upper = (np.arange(3 * LANES) // (LANES // 2)) % 2 == 1
    sign = jnp.asarray(np.where(upper, 1.0, -1.0), jnp.float32)
    return jnp.cos(angles), jnp.sin(angles) * sign[None, :]


def spare_lanes(shape):
    return lax.broadcasted_iota(jnp.int32, shape, 1) % (LANES // 2) >= HD // 2


def last_head(tiles):
    spare = spare_lanes(tiles[0].shape)
    return sum(
        pltpu.roll(jnp.where(spare, tiles[i], 0.0), LANES - HD // 2 + 16 * i, 1) for i in range(3)
    )


def merge_heads(heads):
    spare = spare_lanes(heads[0].shape)
    return [
        jnp.where(spare, pltpu.roll(heads[3], HD // 2 - 16 * i, 1), heads[i])
        for i in range(3)
    ]


def tile(ref, index):
    return ref[:, index * LANES : (index + 1) * LANES]


def put(ref, index, value):
    ref[:, index * LANES : (index + 1) * LANES] = value


def turn(value, cosine, sine):
    return value * cosine + pltpu.roll(value, LANES // 2, 1) * sine


def key_tile(group, i):
    return group * 6 + i


def value_tile(group, i):
    return group * 6 + 3 + i


def fill_bias(bias, own_segment, key_segments, rows):
    size = key_segments.shape[1]
    same = own_segment[...] == key_segments[...]
    query = lax.broadcasted_iota(jnp.int32, (rows, size), 0)
    key = lax.broadcasted_iota(jnp.int32, (rows, size), 1)
    bias[...] = jnp.where(same & ((key >= rows) | (key <= query)), 0.0, -1e30)


def inside(place, shards):
    return (place >= 0) & (place < shards)


def greet_line(shards, way):
    place = lax.axis_index("shard")
    barrier = pltpu.get_barrier_semaphore()

    @pl.when(inside(place - way, shards))
    def _():
        pl.semaphore_signal(
            barrier, inc=1, device_id={"shard": place - way}, device_id_type=pl.DeviceIdType.MESH
        )

    @pl.when(inside(place + way, shards))
    def _():
        pl.semaphore_wait(barrier, 1)


def dot(left, right, dims):
    return lax.dot_general(left, right, (dims, ((), ())), preferred_element_type=jnp.float32)


NT = ((1,), (1,))
NN = ((1,), (0,))
TN = ((0,), (0,))


def attend_kernel(
    shards, hops, rows, raw, cosine, sine, own_segment, key_segments,
    queries, window, attended, log_total,
    held, last, bias, query_heads, send_sem, recv_sem, keep_sem,
):
    place = lax.axis_index("shard")
    greet_line(shards, 1)

    def slot(distance):
        return held.at[pl.ds(distance * rows, rows), :]

    first_key, first_value = QH * 3 // 4, QH * 3 // 4 + KVH * 3 // 4
    for group in range(KVH // 4):
        for i in range(3):
            value = turn(tile(raw, first_key + group * 3 + i), tile(cosine, i), tile(sine, i))
            held[pl.ds(0, rows), key_tile(group, i) * LANES : (key_tile(group, i) + 1) * LANES] = value.astype(
                jnp.bfloat16
            )
            value = tile(raw, first_value + group * 3 + i)
            held[pl.ds(0, rows), value_tile(group, i) * LANES : (value_tile(group, i) + 1) * LANES] = (
                value.astype(jnp.bfloat16)
            )

    def send(distance):
        @pl.when((place + 1 < shards) & (place - distance >= 0))
        def _():
            start_remote(
                slot(distance), slot(distance + 1), send_sem.at[distance], recv_sem.at[distance], {"shard": place + 1}
            )

    send(0)
    fill_bias(bias, own_segment, key_segments, rows)
    for group in range(QH // 4):
        tiles = []
        for i in range(3):
            value = turn(tile(raw, group * 3 + i), tile(cosine, i), tile(sine, i))
            put(queries, group * 3 + i, value.astype(jnp.bfloat16))
            tiles.append(value)
        spare = spare_lanes(tiles[0].shape)
        for i in range(3):
            query_heads[group * 4 + i] = jnp.where(spare, 0.0, tiles[i]).astype(jnp.bfloat16)
        query_heads[group * 4 + 3] = last_head(tiles).astype(jnp.bfloat16)

    for distance in range(1, hops + 1):
        @pl.when(place - distance >= 0)
        def _():
            wait_bytes(slot(distance), recv_sem.at[distance - 1])

        @pl.when(place - distance < 0)
        def _():
            held[pl.ds(distance * rows, rows), :] = jnp.zeros((rows, held.shape[1]), held.dtype)

        if distance < hops:
            send(distance)

    keep = pltpu.make_async_copy(held, window, keep_sem)
    keep.start()
    for group in range(KVH // 4):
        for which, first in enumerate((key_tile(group, 0), value_tile(group, 0))):
            tiles = [tile(held, first + i).astype(jnp.float32) for i in range(3)]
            last[group * 2 + which] = last_head(tiles).astype(jnp.bfloat16)

    lane = lax.broadcasted_iota(jnp.int32, (rows, LANES), 1)
    totals = jnp.zeros((rows, LANES), jnp.float32)
    for group in range(QH // 4):
        outs = []
        for i in range(4):
            head = group * 4 + i
            key_head = head // 2
            wide, item = divmod(key_head, 4)
            keys = last[wide * 2] if item == 3 else tile(held, key_tile(wide, item))
            values = last[wide * 2 + 1] if item == 3 else tile(held, value_tile(wide, item))
            scores = dot(query_heads[head], keys, NT) * HD ** (-0.5) + bias[...]
            top = jnp.max(scores, axis=1, keepdims=True)
            exponent = jnp.exp(scores - top)
            total = jnp.sum(exponent, axis=1, keepdims=True)
            out = dot(exponent.astype(jnp.bfloat16), values, NN) * (1.0 / total)
            outs.append(out)
            totals = jnp.where(lane == head, top + jnp.log(total), totals)
        for i, merged in enumerate(merge_heads(outs)):
            put(attended, group * 3 + i, merged.astype(jnp.bfloat16))
    log_total[...] = totals
    keep.wait()
    for distance in range(hops):
        @pl.when((place + 1 < shards) & (place - distance >= 0))
        def _():
            wait_bytes(slot(distance), send_sem.at[distance])


def line_hops(shards, rows, longest):
    return min(shards - 1, -(-(longest - 1) // rows))


def attend(raw, cosine, sine, own_segment, key_segments, shards, hops):
    rows = raw.shape[0]
    width = QH * HD
    size = (hops + 1) * rows
    bf16, f32, dma = jnp.bfloat16, jnp.float32, pltpu.SemaphoreType.DMA
    vmem = pl.BlockSpec(memory_space=pltpu.VMEM)
    return pl.pallas_call(
        functools.partial(attend_kernel, shards, hops, rows),
        out_shape=[
            jax.ShapeDtypeStruct((rows, width), bf16),
            jax.ShapeDtypeStruct((size, width), bf16),
            jax.ShapeDtypeStruct((rows, width), bf16),
            jax.ShapeDtypeStruct((rows, LANES), f32),
        ],
        in_specs=[vmem] * 5,
        out_specs=[vmem, pl.BlockSpec(memory_space=pl.ANY), vmem, vmem],
        scratch_shapes=[
            pltpu.VMEM((size, width), bf16),
            pltpu.VMEM((KVH // 2, size, LANES), bf16),
            pltpu.VMEM((rows, size), f32),
            pltpu.VMEM((QH, rows, LANES), bf16),
            dma((hops,)),
            dma((hops,)),
            dma,
        ],
        compiler_params=pltpu.CompilerParams(
            collective_id=2, has_side_effects=True, vmem_limit_bytes=40 * 1024 * 1024
        ),
        name="attend",
    )(raw, cosine, sine, own_segment, key_segments)


def attend_back_kernel(
    shards, hops, rows, queries, window, log_total, grads, cosine, sine, own_segment, key_segments,
    lows,
    bias, own_part, parts, landing, query_grads, send_sem, recv_sem,
):
    place = lax.axis_index("shard")
    greet_line(shards, -1)
    fill_bias(bias, own_segment, key_segments, rows)
    span = 6 * LANES

    def heads_of(ref, group):
        tiles = [tile(ref, group * 3 + i).astype(jnp.float32) for i in range(3)]
        spare = spare_lanes(tiles[0].shape)
        heads = [jnp.where(spare, 0.0, t).astype(jnp.bfloat16) for t in tiles]
        return heads + [last_head(tiles).astype(jnp.bfloat16)]

    def column(head):
        lane = lax.broadcasted_iota(jnp.int32, (rows, LANES), 1)
        return jnp.sum(jnp.where(lane == head, log_total[...], 0.0), axis=1, keepdims=True)

    def wide_group(wide):
        heads = heads_of(queries, 2 * wide) + heads_of(queries, 2 * wide + 1)
        grad_heads = heads_of(grads, 2 * wide) + heads_of(grads, 2 * wide + 1)
        key_grads, value_grads = [], []
        query_out = []
        key_tiles = [tile(window, key_tile(wide, i)) for i in range(3)]
        value_tiles = [tile(window, value_tile(wide, i)) for i in range(3)]
        key_tiles.append(last_head([t.astype(jnp.float32) for t in key_tiles]).astype(jnp.bfloat16))
        value_tiles.append(last_head([t.astype(jnp.float32) for t in value_tiles]).astype(jnp.bfloat16))
        for item in range(4):
            keys, values = key_tiles[item], value_tiles[item]
            key_grad = value_grad = None
            for one in (2 * item, 2 * item + 1):
                query, grad = heads[one], grad_heads[one]
                scores = dot(query, keys, NT) * HD ** (-0.5) + bias[...]
                probs = jnp.exp(scores - column(wide * 8 + one))
                grad_probs = dot(grad, values, NT)
                along = jnp.sum(probs * grad_probs, axis=1, keepdims=True)
                grad_scores = (probs * (grad_probs - along)).astype(jnp.bfloat16)
                query_out.append(dot(grad_scores, keys, NN) * HD ** (-0.5))
                key_one = dot(grad_scores, query, TN)
                value_one = dot(probs.astype(jnp.bfloat16), grad, TN)
                key_grad = key_one if key_grad is None else key_grad + key_one
                value_grad = value_one if value_grad is None else value_grad + value_one
            key_grads.append(key_grad * HD ** (-0.5))
            value_grads.append(value_grad)
        for which, grads_of in enumerate((key_grads, value_grads)):
            for i, merged in enumerate(merge_heads(grads_of)):
                at = which * 3 + i
                own_part[:, (wide * 6 + at) * LANES : (wide * 6 + at + 1) * LANES] = merged[:rows]
                for distance in range(1, hops + 1):
                    parts[wide, distance - 1, :, at * LANES : (at + 1) * LANES] = merged[
                        distance * rows : (distance + 1) * rows
                    ].astype(jnp.bfloat16)
        for half in range(2):
            for i, merged in enumerate(merge_heads(query_out[half * 4 : half * 4 + 4])):
                put(query_grads, (2 * wide + half) * 3 + i, merged)

    def step(wide, k):
        distance = hops - k + 1
        source = parts.at[wide, distance - 1]
        target = landing.at[wide, k - 1]
        sems = (send_sem.at[wide, k - 1], recv_sem.at[wide, k - 1])

        @pl.when(place - distance >= 0)
        def _():
            if k > 1:
                @pl.when(place + 1 < shards)
                def _():
                    arrived = landing.at[wide, k - 2]
                    wait_bytes(arrived, recv_sem.at[wide, k - 2])
                    source[...] = (
                        source[...].astype(jnp.float32) + arrived[...].astype(jnp.float32)
                    ).astype(jnp.bfloat16)

            start_remote(source, target, *sems, {"shard": place - 1})

    def finish(wide):
        @pl.when(place + 1 < shards)
        def _():
            arrived = landing.at[wide, hops - 1]
            wait_bytes(arrived, recv_sem.at[wide, hops - 1])
            own_part[:, wide * span : (wide + 1) * span] += arrived[...].astype(jnp.float32)

        first_key, first_value = QH * 3 // 4, QH * 3 // 4 + KVH * 3 // 4
        for i in range(3):
            value = turn(tile(own_part, key_tile(wide, i)), tile(cosine, i), -tile(sine, i))
            put(lows, first_key + wide * 3 + i, value.astype(jnp.bfloat16))
            put(lows, first_value + wide * 3 + i, tile(own_part, value_tile(wide, i)).astype(jnp.bfloat16))

    for wide in range(KVH // 4):
        wide_group(wide)
        step(wide, 1)
    for group in range(QH // 4):
        for i in range(3):
            value = turn(tile(query_grads, group * 3 + i), tile(cosine, i), -tile(sine, i))
            put(lows, group * 3 + i, value.astype(jnp.bfloat16))
    for k in range(2, hops + 1):
        for wide in range(KVH // 4):
            step(wide, k)
    for wide in range(KVH // 4):
        finish(wide)
    for wide in range(KVH // 4):
        for k in range(1, hops + 1):
            @pl.when(place - (hops - k + 1) >= 0)
            def _():
                wait_bytes(parts.at[wide, hops - k], send_sem.at[wide, k - 1])


def attend_back(queries, window, log_total, grads, cosine, sine, own_segment, key_segments, shards, hops):
    rows = queries.shape[0]
    width = QH * HD
    size = (hops + 1) * rows
    bf16, f32, dma = jnp.bfloat16, jnp.float32, pltpu.SemaphoreType.DMA
    vmem = pl.BlockSpec(memory_space=pltpu.VMEM)
    wides = KVH // 4
    return pl.pallas_call(
        functools.partial(attend_back_kernel, shards, hops, rows),
        out_shape=jax.ShapeDtypeStruct((rows, 2 * width), bf16),
        in_specs=[vmem] * 8,
        out_specs=vmem,
        scratch_shapes=[
            pltpu.VMEM((rows, size), f32),
            pltpu.VMEM((rows, width), f32),
            pltpu.VMEM((wides, hops, rows, 6 * LANES), bf16),
            pltpu.VMEM((wides, hops, rows, 6 * LANES), bf16),
            pltpu.VMEM((rows, width), f32),
            dma((wides, hops)),
            dma((wides, hops)),
        ],
        compiler_params=pltpu.CompilerParams(
            collective_id=3, has_side_effects=True, vmem_limit_bytes=48 * 1024 * 1024
        ),
        name="attend_back",
    )(queries, window, log_total, grads, cosine, sine, own_segment, key_segments)


def from_behind(x, axis, by):
    devices = lax.axis_size(axis)
    pairs = [(i, i + by) for i in range(devices) if 0 <= i + by < devices]
    return lax.ppermute(x, axis, pairs)


def swap(x, bit):
    members = lax.axis_size("replica")
    return lax.ppermute(x, "replica", [(r, r ^ (1 << bit)) for r in range(members)])


def gain_width(rows):
    return -(-2 * rows // (PARTS * LANES)) * PARTS * LANES


def gather_layer(pieces):
    norm_attn, w_query, w_key, w_value, w_out, norm_ffn, w_gate, w_up, w_down = pieces
    rows = norm_attn.shape[0]
    shards = lax.axis_size("shard")
    gains = jnp.concatenate([norm_attn, norm_ffn])
    gains = jnp.pad(gains[None], ((0, 15), (0, gain_width(rows) - 2 * rows)))
    w_qkv = to_tiles(jnp.concatenate([w_query, w_key, w_value], axis=1))
    w_qkv, w_out, w_gate, w_up, w_down, gains = gather_weights(
        [w_qkv, w_out, w_gate, w_up, w_down, gains], shards
    )
    gains = gains.reshape(shards, 16, -1)[:, 0].astype(jnp.float32)
    norm_attn = gains[:, :rows].reshape(-1)
    norm_ffn = gains[:, rows : 2 * rows].reshape(-1)
    return norm_attn, w_qkv, rows_to_tiles(w_out), norm_ffn, w_gate, w_up, w_down


def sequence_tables(segment, rows, hops):
    place = lax.axis_index("shard")
    local_segment = lax.dynamic_slice_in_dim(segment, place * rows, rows)
    starts = jnp.sum((segment[None, :] < local_segment[:, None]).astype(jnp.int32), axis=1)
    cosine, sine = rope_tables(place * rows + jnp.arange(rows, dtype=jnp.int32) - starts)
    padded = jnp.concatenate([jnp.full((hops * rows,), -1, jnp.int32), segment])
    key_segments = jnp.concatenate(
        [lax.dynamic_slice_in_dim(padded, (place + hops - d) * rows, rows) for d in range(hops + 1)]
    )
    return cosine, sine, local_segment[:, None], key_segments[None, :]


def matmul(left, right):
    return jnp.dot(left, right, preferred_element_type=jnp.float32)


def matmul_back(left, right):
    return jnp.einsum("tq,dq->td", left, right, preferred_element_type=jnp.float32)


def row_product(left, right):
    return jnp.einsum("td,tq->dq", left, right, preferred_element_type=jnp.float32)


def forward_layer(inputs, weights, tables, shards, hops):
    norm_attn, w_qkv, w_out, norm_ffn, w_gate, w_up, w_down = weights
    recip_one = lax.rsqrt(jnp.mean(inputs * inputs, axis=-1, keepdims=True) + EPSILON)
    scaled = inputs * recip_one
    normed = (scaled * norm_attn).astype(jnp.bfloat16)
    queries, window, attended, log_total = attend(matmul(normed, w_qkv), *tables, shards, hops)
    middle = inputs + matmul(attended, w_out)
    recip_two = lax.rsqrt(jnp.mean(middle * middle, axis=-1, keepdims=True) + EPSILON)
    scaled_mid = middle * recip_two
    normed_mid = (scaled_mid * norm_ffn).astype(jnp.bfloat16)
    gate_proj = matmul(normed_mid, w_gate)
    up_proj = matmul(normed_mid, w_up)
    hidden = (jax.nn.silu(gate_proj) * up_proj).astype(jnp.bfloat16)
    result = middle + matmul(hidden, w_down)
    saved = (
        scaled,
        recip_one,
        normed,
        queries,
        window,
        log_total,
        attended,
        scaled_mid,
        recip_two,
        normed_mid,
        gate_proj,
        up_proj,
        hidden,
        tables,
    )
    return (result, saved)


def backward_layer(grad_result, weights, saved, shards, hops):
    norm_attn, w_qkv, w_out, norm_ffn, w_gate, w_up, w_down = weights
    (
        scaled,
        recip_one,
        normed,
        queries,
        window,
        log_total,
        attended,
        scaled_mid,
        recip_two,
        normed_mid,
        gate_proj,
        up_proj,
        hidden,
        tables,
    ) = saved
    branch_grad = grad_result.astype(jnp.bfloat16)
    grad_hidden = matmul_back(branch_grad, w_down)
    sigmoid_gate = jax.nn.sigmoid(gate_proj)
    gate_low = (
        grad_hidden * up_proj * (sigmoid_gate * (1.0 + gate_proj * (1.0 - sigmoid_gate)))
    ).astype(jnp.bfloat16)
    up_low = (grad_hidden * jax.nn.silu(gate_proj)).astype(jnp.bfloat16)
    grad_normed_mid = matmul_back(gate_low, w_gate) + matmul_back(up_low, w_up)
    grad_norm_ffn = jnp.sum(grad_normed_mid * scaled_mid, axis=0)
    grad_scaled_mid = grad_normed_mid * norm_ffn
    grad_middle = grad_result + recip_two * (
        grad_scaled_mid
        - scaled_mid * jnp.mean(grad_scaled_mid * scaled_mid, axis=-1, keepdims=True)
    )
    attn_grad = grad_middle.astype(jnp.bfloat16)
    grad_attended = matmul_back(attn_grad, w_out).astype(jnp.bfloat16)
    qkv_low = attend_back(queries, window, log_total, grad_attended, *tables, shards, hops)
    grad_normed = matmul_back(qkv_low, w_qkv)
    grad_norm_attn = jnp.sum(grad_normed * scaled, axis=0)
    grad_scaled = grad_normed * norm_attn
    grad_inputs = grad_middle + recip_one * (
        grad_scaled - scaled * jnp.mean(grad_scaled * scaled, axis=-1, keepdims=True)
    )
    operands = (
        normed,
        qkv_low,
        attended,
        attn_grad,
        normed_mid,
        gate_low,
        up_low,
        hidden,
        branch_grad,
    )
    return (grad_inputs, (grad_norm_attn, grad_norm_ffn), operands)


def reduce_gradients(operand_pairs, gains):
    (
        normed,
        qkv_low,
        attended,
        attn_grad,
        normed_mid,
        gate_low,
        up_low,
        hidden,
        branch_grad,
    ) = (jnp.concatenate(parts, axis=0) for parts in zip(*operand_pairs))
    shards = lax.axis_size("shard")
    rows = gains[0].shape[0] // shards

    def product(left, right):
        return row_product(left, right).astype(jnp.bfloat16)

    gain_term = jnp.stack([gain.reshape(shards, rows) for gain in gains], axis=1)
    gain_term = gain_term.reshape(shards, 1, 2 * rows).astype(jnp.bfloat16)
    gain_term = jnp.pad(gain_term, ((0, 0), (0, 15), (0, gain_width(rows) - 2 * rows)))
    leading = [
        product(hidden, branch_grad),
        product(normed_mid, gate_low),
        product(normed_mid, up_low),
        gain_term.reshape(shards * 16, -1),
    ]
    trailing = [product(normed, from_tiles(qkv_low)), product(from_tiles(attended), attn_grad)]
    totals = [total.astype(jnp.float32) for total in reduce_terms(leading, trailing, shards)]
    members = lax.axis_size("replica")
    for bit in range(PARTS.bit_length() - 1, members.bit_length() - 1):
        totals = [total + swap(total, bit) for total in totals]
    down, gate, up, own_gains, qkv, out = totals
    return (
        own_gains[0, :rows],
        qkv[:, : QH * HD],
        qkv[:, QH * HD : (QH + KVH) * HD],
        qkv[:, (QH + KVH) * HD :],
        out,
        own_gains[0, rows : 2 * rows],
        gate,
        up,
        down,
    )


def body(
    tokens,
    segments,
    norm_attn,
    w_query,
    w_key,
    w_value,
    w_out,
    norm_ffn,
    w_gate,
    w_up,
    w_down,
    cotangent,
):
    micro_count = tokens.shape[0]
    row_count = tokens.shape[2]
    width = tokens.shape[3]
    seq_length = segments.shape[2]
    shards = lax.axis_size("shard")
    hops = line_hops(shards, row_count, seq_length // 2)
    first_section = lax.axis_index("section") == 0

    def choose(early, late):
        return jax.tree.map(lambda a, b: jnp.where(first_section, a, b), early, late)

    weights = gather_layer(
        (
            norm_attn[0],
            w_query[0],
            w_key[0],
            w_value[0],
            w_out[0],
            norm_ffn[0],
            w_gate[0],
            w_up[0],
            w_down[0],
        )
    )
    all_tables = [sequence_tables(segments[m, 0], row_count, hops) for m in range(micro_count)]
    saved_ticks = []
    result_ticks = []
    arriving = jnp.zeros((row_count, width), jnp.bfloat16)
    for tick_index in range(micro_count + 1):
        own_input = tokens[min(tick_index, micro_count - 1), 0].astype(jnp.float32)
        layer_input = jnp.where(first_section, own_input, arriving.astype(jnp.float32))
        tables = choose(
            all_tables[min(tick_index, micro_count - 1)], all_tables[max(tick_index - 1, 0)]
        )
        result, saved = forward_layer(layer_input, weights, tables, shards, hops)
        result_low = result.astype(jnp.bfloat16)
        result_ticks.append(result_low)
        saved_ticks.append(saved)
        if tick_index < micro_count:
            arriving = from_behind(result_low, "section", 1)
    flow_ticks = []
    gain_sums = None
    operand_ticks = []
    returning = jnp.zeros((row_count, width), jnp.bfloat16)
    for tick_index in range(micro_count + 1):
        later_grad = cotangent[min(tick_index, micro_count - 1), 0].astype(jnp.float32)
        incoming = jnp.where(first_section, returning.astype(jnp.float32), later_grad)
        active = jnp.where(first_section, tick_index >= 1, tick_index < micro_count)
        incoming = jnp.where(active, incoming, 0.0)
        if 0 < tick_index < micro_count:
            saved = choose(saved_ticks[tick_index - 1], saved_ticks[tick_index + 1])
        else:
            saved = saved_ticks[1 if tick_index == 0 else micro_count - 1]
        grad_inputs, gains, operands = backward_layer(incoming, weights, saved, shards, hops)
        flow_ticks.append(grad_inputs)
        if tick_index < micro_count:
            returning = from_behind(grad_inputs.astype(jnp.bfloat16), "section", -1)
        gain_sums = gains if gain_sums is None else jax.tree.map(jnp.add, gain_sums, gains)
        operand_ticks.append(operands)
    edge_operands = choose(operand_ticks[micro_count], operand_ticks[0])
    totals = reduce_gradients(operand_ticks[1:micro_count] + [edge_operands], gain_sums)
    section_outputs = jnp.stack(
        [
            jnp.where(first_section, result_ticks[index_micro], result_ticks[index_micro + 1])
            for index_micro in range(micro_count)
        ]
    )
    input_grads = jnp.stack(
        [
            jnp.where(first_section, flow_ticks[index_micro + 1], flow_ticks[index_micro])
            for index_micro in range(micro_count)
        ]
    )
    return (section_outputs[None, :, None], input_grads[None, :, None]) + tuple(
        total[None] for total in totals
    )


def solution(mesh):
    in_specs = (
        P(None, "replica", "shard", None),
        P(None, "replica", None),
        P("section", "shard"),
        P("section", "shard", None),
        P("section", "shard", None),
        P("section", "shard", None),
        P("section", "shard", None),
        P("section", "shard"),
        P("section", "shard", None),
        P("section", "shard", None),
        P("section", "shard", None),
        P(None, "replica", "shard", None),
    )
    out_specs = (
        P("section", None, "replica", "shard", None),
        P("section", None, "replica", "shard", None),
        P("section", "shard"),
        P("section", "shard", None),
        P("section", "shard", None),
        P("section", "shard", None),
        P("section", "shard", None),
        P("section", "shard"),
        P("section", "shard", None),
        P("section", "shard", None),
        P("section", "shard", None),
    )
    return jax.shard_map(body, mesh=mesh, in_specs=in_specs, out_specs=out_specs, check_vma=False)
```

```python
import functools

import jax
import jax.numpy as jnp
import numpy as np
from jax import lax
from jax.experimental import pallas as pl
from jax.experimental.pallas import tpu as pltpu
from jax.sharding import PartitionSpec as P

QH = 16
KVH = 8
HD = 96
PARTS = 4
LANES = 128


EPSILON = 1e-05
ROPE_BASE = 100000.0


def start_remote(source, target, send_sem, recv_sem, device):
    pltpu.make_async_remote_copy(
        src_ref=source,
        dst_ref=target,
        send_sem=send_sem,
        recv_sem=recv_sem,
        device_id=device,
        device_id_type=pl.DeviceIdType.MESH,
    ).start()


def wait_bytes(ref, sem):
    pltpu.make_async_copy(ref, ref, sem).wait()


def greet(shards):
    place = lax.axis_index("shard")
    member = lax.axis_index("replica")
    barrier = pltpu.get_barrier_semaphore()
    pl.semaphore_signal(barrier, inc=1, device_id={"replica": member ^ 1}, device_id_type=pl.DeviceIdType.MESH)
    pl.semaphore_signal(barrier, inc=1, device_id={"replica": member ^ 2}, device_id_type=pl.DeviceIdType.MESH)

    @pl.when(place > 0)
    def _():
        pl.semaphore_signal(barrier, inc=1, device_id={"shard": place - 1}, device_id_type=pl.DeviceIdType.MESH)

    @pl.when(place < shards - 1)
    def _():
        pl.semaphore_signal(barrier, inc=1, device_id={"shard": place + 1}, device_id_type=pl.DeviceIdType.MESH)

    pl.semaphore_wait(barrier, 2 + (place > 0).astype(jnp.int32) + (place < shards - 1).astype(jnp.int32))


def gather_kernel(shards, chunks, count, *refs):
    pieces, wholes = refs[:count], refs[count : 2 * count]
    held = refs[2 * count : 3 * count]
    (local_sem, own_send, pass_send, line_recv, x_send, x_recv, core_send, core_recv) = refs[
        3 * count :
    ]
    place = lax.axis_index("shard")
    member = lax.axis_index("replica")
    part = member % PARTS
    greet(shards)

    def loads(index):
        return pltpu.make_async_copy(pieces[index], held[index], local_sem.at[index])

    def stores(index):
        rows = pieces[index].shape[0]
        target = wholes[index].at[pl.ds(pl.multiple_of(place * rows, rows), rows), :]
        return pltpu.make_async_copy(held[index], target, local_sem.at[index])

    for index in range(count):
        loads(index).start()

    def window(chunk, block, whose):
        index, first, length = chunk
        rows = pieces[index].shape[0]
        width = pieces[index].shape[1] // PARTS
        return wholes[index].at[
            pl.ds(pl.multiple_of(block * rows + first, length), length),
            pl.ds(pl.multiple_of(whose * width, width), width),
        ]

    def own(j):
        index, first, length = chunks[j]
        width = pieces[index].shape[1] // PARTS
        source = pieces[index].at[
            pl.ds(first, length), pl.ds(pl.multiple_of(part * width, width), width)
        ]
        for slot, way in enumerate((1, -1)):
            @pl.when((place + way >= 0) & (place + way < shards))
            def _():
                start_remote(
                    source,
                    window(chunks[j], place, part),
                    own_send.at[j, slot],
                    line_recv.at[j, place],
                    {"shard": place + way},
                )

    def hop(j, k):
        for way in (1, -1):
            block = place - way * k

            @pl.when((block >= 0) & (block < shards))
            def _():
                mine = window(chunks[j], block, part)
                wait_bytes(mine, line_recv.at[j, block])

                @pl.when((place + way >= 0) & (place + way < shards))
                def _():
                    start_remote(
                        mine, mine, pass_send.at[j, block], line_recv.at[j, block], {"shard": place + way}
                    )

                start_remote(mine, mine, x_send.at[j, block], x_recv.at[j, block], {"replica": member ^ 2})
                start_remote(
                    mine, mine, core_send.at[j, block, 0], core_recv.at[j, block, 0], {"replica": member ^ 1}
                )

    def across(j, k):
        for way in (1, -1):
            block = place - way * k

            @pl.when((block >= 0) & (block < shards))
            def _():
                theirs = window(chunks[j], block, part ^ 2)
                wait_bytes(theirs, x_recv.at[j, block])
                start_remote(
                    theirs, theirs, core_send.at[j, block, 1], core_recv.at[j, block, 1], {"replica": member ^ 1}
                )

    total = len(chunks)
    for step in range(total + shards + 1):
        if step < total:
            own(step)
        if 1 <= step <= count:
            loads(step - 1).wait()
            stores(step - 1).start()
        for k in range(1, shards):
            if 0 <= step - k < total:
                hop(step - k, k)
        for k in range(1, shards):
            if 0 <= step - k - 1 < total:
                across(step - k - 1, k)

    for j in range(total):
        for slot, way in enumerate((1, -1)):
            @pl.when((place + way >= 0) & (place + way < shards))
            def _():
                wait_bytes(window(chunks[j], place, part), own_send.at[j, slot])

        for k in range(1, shards):
            for way in (1, -1):
                block = place - way * k

                @pl.when((block >= 0) & (block < shards))
                def _():
                    mine = window(chunks[j], block, part)

                    @pl.when((place + way >= 0) & (place + way < shards))
                    def _():
                        wait_bytes(mine, pass_send.at[j, block])

                    wait_bytes(mine, x_send.at[j, block])
                    for which in range(2):
                        wait_bytes(mine, core_send.at[j, block, which])
                        wait_bytes(mine, core_recv.at[j, block, which])
    for index in range(count):
        stores(index).wait()


def gather_weights(pieces, shards, pace=192 * 1024):
    chunks = []
    for index, piece in enumerate(pieces):
        rows, width = piece.shape
        cuts = 1
        while rows % (2 * cuts * 16) == 0 and rows // cuts * (width // PARTS) > pace:
            cuts *= 2
        for cut in range(cuts):
            chunks.append((index, cut * (rows // cuts), rows // cuts))
    count, total = len(pieces), len(chunks)
    dma = pltpu.SemaphoreType.DMA
    return pl.pallas_call(
        functools.partial(gather_kernel, shards, tuple(chunks), count),
        out_shape=[jax.ShapeDtypeStruct((shards * p.shape[0], p.shape[1]), p.dtype) for p in pieces],
        in_specs=[pl.BlockSpec(memory_space=pl.ANY)] * count,
        out_specs=[pl.BlockSpec(memory_space=pl.ANY)] * count,
        scratch_shapes=[pltpu.VMEM(p.shape, p.dtype) for p in pieces]
        + [
            dma((count,)),
            dma((total, 2)),
            dma((total, shards)),
            dma((total, shards)),
            dma((total, shards)),
            dma((total, shards)),
            dma((total, shards, 2)),
            dma((total, shards, 2)),
        ],
        compiler_params=pltpu.CompilerParams(collective_id=0, has_side_effects=True, vmem_limit_bytes=24 * 1024 * 1024),
        name="gather_weights",
    )(*pieces)


def add_rows(target, left, right, rows):
    step = next(size for size in (128, 64, 16) if rows % size == 0)

    def body(i, carry):
        window = pl.ds(pl.multiple_of(i * step, step), step)
        target[window, :] = (
            left[window, :].astype(jnp.float32) + right[window, :].astype(jnp.float32)
        ).astype(target.dtype)
        return carry

    lax.fori_loop(0, rows // step, body, 0)


def reduce_kernel(shards, plan, count, *refs):
    leads, trails, heights, kinds = plan
    chunks = leads + trails
    total = len(chunks)
    terms, refs = refs[:count], refs[count:]
    sums, refs = refs[:count], refs[count:]
    near, refs = refs[:count], refs[count:]
    landed, refs = refs[:total], refs[total:]
    passing, refs = refs[:total], refs[total:]
    swapped, refs = refs[: len(trails)], refs[len(trails) :]
    stages = []
    for kind in range(len(kinds)):
        stages.append(refs[:6])
        refs = refs[6:]
    trail_stage, refs = refs[:4], refs[4:]
    (load_sem, core_send, core_recv, x_send, x_recv, line_send, line_recv) = refs[:7]
    (end_local, end_x_send, end_x_recv, end_core_send, end_core_recv) = refs[7:]
    place = lax.axis_index("shard")
    member = lax.axis_index("replica")
    core = member % 2
    side = (member // 2) % 2
    x_mate = {"replica": member ^ 2}
    core_mate = {"replica": member ^ 1}
    greet(shards)

    def leading(j):
        return j < len(leads)

    def height(j):
        return heights[chunks[j][0]]

    def columns(j, whose):
        index, first, width = chunks[j]
        part = terms[index].shape[1] // PARTS
        return pl.ds(pl.multiple_of(whose * part + first, LANES), width)

    def send_near(j):
        index = chunks[j][0]
        for which in range(2):
            start_remote(
                terms[index].at[:, columns(j, (1 - core) * 2 + which)],
                near[index].at[:, columns(j, which)],
                core_send.at[j, which],
                core_recv.at[j, which],
                core_mate,
            )

    def staged(j):
        if leading(j):
            a0, a1, b0, b1, c, d = stages[kinds.index((height(j), chunks[j][2]))]
            return (b0, b1, c, d) if j % 2 else (a0, a1, c, d)
        return trail_stage

    def load_copies(j):
        index = chunks[j][0]
        whose = (1 - side, side) if leading(j) else (0, 1)
        at = staged(j)
        sem = 0 if leading(j) else 4
        sources = [terms[index].at[:, columns(j, core * 2 + w)] for w in whose]
        sources += [near[index].at[:, columns(j, w)] for w in whose]
        return [pltpu.make_async_copy(s, at[i], load_sem.at[sem + i]) for i, s in enumerate(sources)]

    def load(j):
        for which in range(2):
            wait_bytes(near[chunks[j][0]].at[:, columns(j, which)], core_recv.at[j, which])
        for copy in load_copies(j):
            copy.start()

    def near_sum(j):
        size = shards * height(j)
        at = staged(j)
        for copy in load_copies(j):
            copy.wait()
        if leading(j):
            add_rows(at[0], at[0], at[2], size)
            start_remote(at[0], landed[j], x_send.at[j], x_recv.at[j], x_mate)
            add_rows(at[1], at[1], at[3], size)
        else:
            width = chunks[j][2]
            for which in range(2):
                window = landed[j].at[:, pl.ds(which * width, width)]
                add_rows(window, at[which], at[2 + which], size)

    def x_sum(j):
        at = staged(j)
        wait_bytes(at[0], x_send.at[j])
        wait_bytes(landed[j], x_recv.at[j])
        add_rows(landed[j], landed[j], at[1], shards * height(j))

    def block(j, t):
        rows = height(j)
        return landed[j].at[pl.ds(pl.multiple_of(t * rows, rows), rows), :]

    def inside(t):
        return (t >= 0) & (t < shards)

    def line(j, hop):
        for slot, way in enumerate((1, -1)):
            t = place + way * (shards - hop)
            target = passing[j].at[slot, hop - 1]
            sems = (line_send.at[j, slot, hop - 1], line_recv.at[j, slot, hop - 1])
            ahead = {"shard": place + way}
            own = block(j, jnp.clip(t, 0, shards - 1))
            if hop == 1:

                @pl.when(inside(t))
                def _():
                    start_remote(own, target, *sems, ahead)
            else:
                arrived = passing[j].at[slot, hop - 2]

                @pl.when(inside(t) & inside(place - way))
                def _():
                    wait_bytes(arrived, line_recv.at[j, slot, hop - 2])
                    add_rows(arrived, arrived, own, height(j))
                    start_remote(arrived, target, *sems, ahead)

                @pl.when(inside(t) & jnp.logical_not(inside(place - way)))
                def _():
                    start_remote(own, target, *sems, ahead)

    def sum_window(j, whose):
        return sums[chunks[j][0]].at[:, columns(j, whose)]

    def share(j):
        width = chunks[j][2]
        for which in range(1 if leading(j) else 2):
            rows = block(j, place).at[:, pl.ds(which * width, width)]
            target = sum_window(j, core * 2 + (side if leading(j) else which))
            pltpu.make_async_copy(rows, target, end_local.at[j, which]).start()
            start_remote(rows, target, end_core_send.at[j, which], end_core_recv.at[j, which], core_mate)

    def line_end(j):
        mine = block(j, place)
        for slot, way in enumerate((1, -1)):

            @pl.when(inside(place - way))
            def _():
                arrived = passing[j].at[slot, shards - 2]
                wait_bytes(arrived, line_recv.at[j, slot, shards - 2])
                add_rows(mine, mine, arrived, height(j))

        target = sum_window(j, core * 2 + side) if leading(j) else swapped[j - len(leads)]
        start_remote(mine, target, end_x_send.at[j], end_x_recv.at[j], x_mate)
        if leading(j):
            share(j)

    def finish(j):
        if leading(j):
            theirs = sum_window(j, core * 2 + (1 - side))
            wait_bytes(theirs, end_x_recv.at[j])
            start_remote(theirs, theirs, end_core_send.at[j, 1], end_core_recv.at[j, 1], core_mate)
        else:
            mine, other = block(j, place), swapped[j - len(leads)]
            wait_bytes(mine, end_x_send.at[j])
            wait_bytes(other, end_x_recv.at[j])
            add_rows(mine, mine, other, height(j))
            share(j)

    first, second = len(leads), len(trails)
    for j in range(max(first, second)):
        if j < first:
            send_near(j)
        if j < second:
            send_near(first + j)
    load(0)
    load(first)
    for step in range(max(first + shards + 2, second + shards + 1)):
        if step < first:
            near_sum(step)
        if step < second:
            near_sum(first + step)
            if step + 1 < second:
                load(first + step + 1)
            line(first + step, 1)
        for hop in range(2, shards):
            if 0 <= step - hop < first:
                line(step - hop, hop)
            if 0 <= step - hop + 1 < second:
                line(first + step - hop + 1, hop)
        if 0 <= step - shards < first:
            line_end(step - shards)
        if 0 <= step - shards + 1 < second:
            line_end(first + step - shards + 1)
        if 0 <= step - shards - 1 < first:
            finish(step - shards - 1)
        if 0 <= step - shards < second:
            finish(first + step - shards)
        if 1 <= step <= first:
            x_sum(step - 1)
            line(step - 1, 1)
        if step + 1 < first:
            load(step + 1)

    for j in range(total):
        for which in range(2):
            wait_bytes(near[chunks[j][0]].at[:, columns(j, which)], core_send.at[j, which])
        for slot, way in enumerate((1, -1)):
            for hop in range(1, shards):

                @pl.when(inside(place + way * (shards - hop)))
                def _():
                    wait_bytes(passing[j].at[slot, hop - 1], line_send.at[j, slot, hop - 1])

        if leading(j):
            wait_bytes(sum_window(j, 0), end_x_send.at[j])
        for which in range(2):
            if which == 0 or not leading(j):
                wait_bytes(sum_window(j, 0), end_local.at[j, which])
            wait_bytes(sum_window(j, 0), end_core_send.at[j, which])
            wait_bytes(sum_window(j, 0), end_core_recv.at[j, which])


def reduce_terms(leading, trailing, shards, lead_cells=1536 * 256):
    terms = list(leading) + list(trailing)
    count = len(terms)
    heights = tuple(t.shape[0] // shards for t in terms)
    leads, trails = [], []
    for index, term in enumerate(terms):
        part = term.shape[1] // PARTS
        if index < len(leading):
            width = part
            while width % (2 * LANES) == 0 and width * term.shape[0] > lead_cells:
                width //= 2
            if width * term.shape[0] > lead_cells and width % LANES == 0:
                width = LANES
            leads += [(index, first, width) for first in range(0, part, width)]
        else:
            trails += [(index, first, LANES) for first in range(0, part, LANES)]
    kinds = []
    for index, first, width in leads:
        if (heights[index], width) not in kinds:
            kinds.append((heights[index], width))
    chunks = leads + trails
    total = len(chunks)
    bf16, dma = jnp.bfloat16, pltpu.SemaphoreType.DMA

    def rows_and_width(j):
        index, first, width = chunks[j]
        return heights[index], width if j < len(leads) else 2 * width

    scratch = []
    for j in range(total):
        rows, width = rows_and_width(j)
        scratch.append(pltpu.VMEM((shards * rows, width), bf16))
    for j in range(total):
        rows, width = rows_and_width(j)
        scratch.append(pltpu.VMEM((2, shards - 1, rows, width), bf16))
    for j in range(len(leads), total):
        rows, width = rows_and_width(j)
        scratch.append(pltpu.VMEM((rows, width), bf16))
    for rows, width in kinds:
        scratch += [pltpu.VMEM((shards * rows, width), bf16)] * 6
    scratch += [pltpu.VMEM((shards * heights[-1], LANES), bf16)] * 4
    scratch += [
        dma((8,)),
        dma((total, 2)),
        dma((total, 2)),
        dma((total,)),
        dma((total,)),
        dma((total, 2, shards - 1)),
        dma((total, 2, shards - 1)),
        dma((total, 2)),
        dma((total,)),
        dma((total,)),
        dma((total, 2)),
        dma((total, 2)),
    ]
    outs = pl.pallas_call(
        functools.partial(reduce_kernel, shards, (tuple(leads), tuple(trails), heights, tuple(kinds)), count),
        out_shape=[jax.ShapeDtypeStruct((t.shape[0] // shards, t.shape[1]), bf16) for t in terms]
        + [jax.ShapeDtypeStruct((t.shape[0], t.shape[1] // 2), bf16) for t in terms],
        in_specs=[pl.BlockSpec(memory_space=pl.ANY)] * count,
        out_specs=[pl.BlockSpec(memory_space=pl.ANY)] * (2 * count),
        scratch_shapes=scratch,
        compiler_params=pltpu.CompilerParams(
            collective_id=1, has_side_effects=True, vmem_limit_bytes=62 * 1024 * 1024
        ),
        name="reduce_terms",
    )(*terms)
    return outs[:count]


def tile_order():
    order = np.zeros(4 * HD, np.int32)
    for tile in range(3):
        for lane in range(LANES):
            upper, low = divmod(lane, LANES // 2)
            if low < HD // 2:
                head, item = tile, low
            else:
                head, item = 3, 16 * tile + low - HD // 2
            order[tile * LANES + lane] = head * HD + upper * (HD // 2) + item
    return order


def tile_matrix():
    order = tile_order()
    return (np.arange(4 * HD)[:, None] == order[None, :]).astype(np.float32)


def to_tiles(x):
    matrix = jnp.asarray(tile_matrix(), jnp.bfloat16)
    span = 4 * HD
    return jnp.concatenate(
        [
            jnp.dot(x[:, i : i + span], matrix, preferred_element_type=jnp.float32).astype(x.dtype)
            for i in range(0, x.shape[1], span)
        ],
        axis=1,
    )


def from_tiles(x):
    matrix = jnp.asarray(tile_matrix().T, jnp.bfloat16)
    span = 4 * HD
    return jnp.concatenate(
        [
            jnp.dot(x[:, i : i + span], matrix, preferred_element_type=jnp.float32).astype(x.dtype)
            for i in range(0, x.shape[1], span)
        ],
        axis=1,
    )


def rows_to_tiles(x):
    matrix = jnp.asarray(tile_matrix().T, jnp.bfloat16)
    groups = x.reshape(-1, 4 * HD, x.shape[1])
    moved = jnp.einsum("lk,gkn->gln", matrix, groups, preferred_element_type=jnp.float32)
    return moved.astype(x.dtype).reshape(x.shape)


def rope_tables(positions):
    item = tile_order() % (HD // 2)
    frequency = ROPE_BASE ** (-(jnp.asarray(item, jnp.float32) * 2.0) / HD)
    angles = positions.astype(jnp.float32)[:, None] * frequency[None, :]
    upper = (np.arange(3 * LANES) // (LANES // 2)) % 2 == 1
    sign = jnp.asarray(np.where(upper, 1.0, -1.0), jnp.float32)
    return jnp.cos(angles), jnp.sin(angles) * sign[None, :]


def spare_lanes(shape):
    return lax.broadcasted_iota(jnp.int32, shape, 1) % (LANES // 2) >= HD // 2


def last_head(tiles):
    spare = spare_lanes(tiles[0].shape)
    return sum(
        pltpu.roll(jnp.where(spare, tiles[i], 0.0), LANES - HD // 2 + 16 * i, 1) for i in range(3)
    )


def merge_heads(heads):
    spare = spare_lanes(heads[0].shape)
    return [
        jnp.where(spare, pltpu.roll(heads[3], HD // 2 - 16 * i, 1), heads[i])
        for i in range(3)
    ]


def tile(ref, index):
    return ref[:, index * LANES : (index + 1) * LANES]


def put(ref, index, value):
    ref[:, index * LANES : (index + 1) * LANES] = value


def turn(value, cosine, sine):
    return value * cosine + pltpu.roll(value, LANES // 2, 1) * sine


def key_tile(group, i):
    return group * 6 + i


def value_tile(group, i):
    return group * 6 + 3 + i


def fill_bias(bias, own_segment, key_segments, rows):
    size = key_segments.shape[1]
    same = own_segment[...] == key_segments[...]
    query = lax.broadcasted_iota(jnp.int32, (rows, size), 0)
    key = lax.broadcasted_iota(jnp.int32, (rows, size), 1)
    bias[...] = jnp.where(same & ((key >= rows) | (key <= query)), 0.0, -1e30)


def inside(place, shards):
    return (place >= 0) & (place < shards)


def line_place(shards):
    place = lax.axis_index("shard")
    mirrored = lax.axis_index("replica") % 2 == 1
    return jnp.where(mirrored, shards - 1 - place, place)


def line_device(place, shards):
    mirrored = lax.axis_index("replica") % 2 == 1
    return {"shard": jnp.where(mirrored, shards - 1 - place, place)}


def greet_line(shards, way):
    place = line_place(shards)
    barrier = pltpu.get_barrier_semaphore()

    @pl.when(inside(place - way, shards))
    def _():
        pl.semaphore_signal(
            barrier,
            inc=1,
            device_id=line_device(place - way, shards),
            device_id_type=pl.DeviceIdType.MESH,
        )

    @pl.when(inside(place + way, shards))
    def _():
        pl.semaphore_wait(barrier, 1)


def dot(left, right, dims):
    return lax.dot_general(left, right, (dims, ((), ())), preferred_element_type=jnp.float32)


NT = ((1,), (1,))
NN = ((1,), (0,))
TN = ((0,), (0,))


def attend_kernel(
    shards, hops, rows, raw, cosine, sine, own_segment, key_segments,
    queries, window, attended, log_total,
    held, last, bias, query_heads, send_sem, recv_sem, keep_sem,
):
    place = line_place(shards)
    greet_line(shards, 1)

    def slot(distance):
        return held.at[pl.ds(distance * rows, rows), :]

    first_key, first_value = QH * 3 // 4, QH * 3 // 4 + KVH * 3 // 4
    for group in range(KVH // 4):
        for i in range(3):
            value = turn(tile(raw, first_key + group * 3 + i), tile(cosine, i), tile(sine, i))
            held[pl.ds(0, rows), key_tile(group, i) * LANES : (key_tile(group, i) + 1) * LANES] = value.astype(
                jnp.bfloat16
            )
            value = tile(raw, first_value + group * 3 + i)
            held[pl.ds(0, rows), value_tile(group, i) * LANES : (value_tile(group, i) + 1) * LANES] = (
                value.astype(jnp.bfloat16)
            )

    def send(distance):
        @pl.when((place + 1 < shards) & (place - distance >= 0))
        def _():
            start_remote(
                slot(distance),
                slot(distance + 1),
                send_sem.at[distance],
                recv_sem.at[distance],
                line_device(place + 1, shards),
            )

    send(0)
    fill_bias(bias, own_segment, key_segments, rows)
    for group in range(QH // 4):
        tiles = []
        for i in range(3):
            value = turn(tile(raw, group * 3 + i), tile(cosine, i), tile(sine, i))
            put(queries, group * 3 + i, value.astype(jnp.bfloat16))
            tiles.append(value)
        spare = spare_lanes(tiles[0].shape)
        for i in range(3):
            query_heads[group * 4 + i] = jnp.where(spare, 0.0, tiles[i]).astype(jnp.bfloat16)
        query_heads[group * 4 + 3] = last_head(tiles).astype(jnp.bfloat16)

    def receive(distance):
        @pl.when(place - distance >= 0)
        def _():
            wait_bytes(slot(distance), recv_sem.at[distance - 1])

        @pl.when(place - distance < 0)
        def _():
            held[pl.ds(distance * rows, rows), :] = jnp.zeros((rows, held.shape[1]), held.dtype)

        if distance < hops:
            send(distance)

    def scores_values(head, first, size):
        wide, item = divmod(head // 2, 4)
        span = pl.ds(first, size)
        if item == 3:
            keys, values = last[wide * 2, span], last[wide * 2 + 1, span]
        else:
            at = [spot(wide, item) * LANES for spot in (key_tile, value_tile)]
            keys, values = (held[span, lane : lane + LANES] for lane in at)
        return dot(query_heads[head], keys, NT) * HD ** (-0.5) + bias[:, first : first + size], values

    def fill_last(first, size):
        for wide in range(KVH // 4):
            for which, at in enumerate((key_tile(wide, 0), value_tile(wide, 0))):
                tiles = [
                    held[pl.ds(first, size), (at + i) * LANES : (at + i + 1) * LANES].astype(jnp.float32)
                    for i in range(3)
                ]
                last[wide * 2 + which, pl.ds(first, size)] = last_head(tiles).astype(jnp.bfloat16)

    for distance in range(1, hops):
        receive(distance)
    near = hops * rows
    fill_last(0, near)
    state = []
    for head in range(QH):
        scores, values = scores_values(head, 0, near)
        top = jnp.max(scores, axis=1, keepdims=True)
        exponent = jnp.exp(scores - top)
        total = jnp.sum(exponent, axis=1, keepdims=True)
        state.append((top, total, dot(exponent.astype(jnp.bfloat16), values, NN)))
    receive(hops)
    keep = pltpu.make_async_copy(held, window, keep_sem)
    keep.start()
    fill_last(near, rows)
    lane = lax.broadcasted_iota(jnp.int32, (rows, LANES), 1)
    totals = jnp.zeros((rows, LANES), jnp.float32)
    for group in range(QH // 4):
        outs = []
        for head in range(group * 4, group * 4 + 4):
            before, total, out = state[head]
            scores, values = scores_values(head, near, rows)
            top = jnp.maximum(before, jnp.max(scores, axis=1, keepdims=True))
            exponent = jnp.exp(scores - top)
            shrink = jnp.exp(before - top)
            total = total * shrink + jnp.sum(exponent, axis=1, keepdims=True)
            out = out * shrink + dot(exponent.astype(jnp.bfloat16), values, NN)
            outs.append(out * (1.0 / total))
            totals = jnp.where(lane == head, top + jnp.log(total), totals)
        for i, merged in enumerate(merge_heads(outs)):
            put(attended, group * 3 + i, merged.astype(jnp.bfloat16))
    log_total[...] = totals
    keep.wait()
    for distance in range(hops):
        @pl.when((place + 1 < shards) & (place - distance >= 0))
        def _():
            wait_bytes(slot(distance), send_sem.at[distance])


def line_hops(shards, rows, longest):
    return min(shards - 1, -(-(longest - 1) // rows))


def attend(raw, cosine, sine, own_segment, key_segments, shards, hops):
    rows = raw.shape[0]
    width = QH * HD
    size = (hops + 1) * rows
    bf16, f32, dma = jnp.bfloat16, jnp.float32, pltpu.SemaphoreType.DMA
    vmem = pl.BlockSpec(memory_space=pltpu.VMEM)
    return pl.pallas_call(
        functools.partial(attend_kernel, shards, hops, rows),
        out_shape=[
            jax.ShapeDtypeStruct((rows, width), bf16),
            jax.ShapeDtypeStruct((size, width), bf16),
            jax.ShapeDtypeStruct((rows, width), bf16),
            jax.ShapeDtypeStruct((rows, LANES), f32),
        ],
        in_specs=[vmem] * 5,
        out_specs=[vmem, pl.BlockSpec(memory_space=pl.ANY), vmem, vmem],
        scratch_shapes=[
            pltpu.VMEM((size, width), bf16),
            pltpu.VMEM((KVH // 2, size, LANES), bf16),
            pltpu.VMEM((rows, size), f32),
            pltpu.VMEM((QH, rows, LANES), bf16),
            dma((hops,)),
            dma((hops,)),
            dma,
        ],
        compiler_params=pltpu.CompilerParams(
            collective_id=2, has_side_effects=True, vmem_limit_bytes=40 * 1024 * 1024
        ),
        name="attend",
    )(raw, cosine, sine, own_segment, key_segments)


def attend_back_kernel(
    shards, hops, rows, queries, window, log_total, grads, cosine, sine, own_segment, key_segments,
    lows,
    bias, own_part, parts, landing, query_grads, send_sem, recv_sem,
):
    place = line_place(shards)
    greet_line(shards, -1)
    fill_bias(bias, own_segment, key_segments, rows)
    span = 6 * LANES

    def heads_of(ref, group):
        tiles = [tile(ref, group * 3 + i).astype(jnp.float32) for i in range(3)]
        spare = spare_lanes(tiles[0].shape)
        heads = [jnp.where(spare, 0.0, t).astype(jnp.bfloat16) for t in tiles]
        return heads + [last_head(tiles).astype(jnp.bfloat16)]

    def column(head):
        lane = lax.broadcasted_iota(jnp.int32, (rows, LANES), 1)
        return jnp.sum(jnp.where(lane == head, log_total[...], 0.0), axis=1, keepdims=True)

    def wide_group(wide):
        heads = heads_of(queries, 2 * wide) + heads_of(queries, 2 * wide + 1)
        grad_heads = heads_of(grads, 2 * wide) + heads_of(grads, 2 * wide + 1)
        key_grads, value_grads = [], []
        query_out = []
        key_tiles = [tile(window, key_tile(wide, i)) for i in range(3)]
        value_tiles = [tile(window, value_tile(wide, i)) for i in range(3)]
        key_tiles.append(last_head([t.astype(jnp.float32) for t in key_tiles]).astype(jnp.bfloat16))
        value_tiles.append(last_head([t.astype(jnp.float32) for t in value_tiles]).astype(jnp.bfloat16))
        for item in range(4):
            keys, values = key_tiles[item], value_tiles[item]
            key_grad = value_grad = None
            for one in (2 * item, 2 * item + 1):
                query, grad = heads[one], grad_heads[one]
                scores = dot(query, keys, NT) * HD ** (-0.5) + bias[...]
                probs = jnp.exp(scores - column(wide * 8 + one))
                grad_probs = dot(grad, values, NT)
                along = jnp.sum(probs * grad_probs, axis=1, keepdims=True)
                grad_scores = (probs * (grad_probs - along)).astype(jnp.bfloat16)
                query_out.append(dot(grad_scores, keys, NN) * HD ** (-0.5))
                key_one = dot(grad_scores, query, TN)
                value_one = dot(probs.astype(jnp.bfloat16), grad, TN)
                key_grad = key_one if key_grad is None else key_grad + key_one
                value_grad = value_one if value_grad is None else value_grad + value_one
            key_grads.append(key_grad * HD ** (-0.5))
            value_grads.append(value_grad)
        for which, grads_of in enumerate((key_grads, value_grads)):
            for i, merged in enumerate(merge_heads(grads_of)):
                at = which * 3 + i
                own_part[:, (wide * 6 + at) * LANES : (wide * 6 + at + 1) * LANES] = merged[:rows]
                for distance in range(1, hops + 1):
                    parts[wide, distance - 1, :, at * LANES : (at + 1) * LANES] = merged[
                        distance * rows : (distance + 1) * rows
                    ].astype(jnp.bfloat16)
        for half in range(2):
            for i, merged in enumerate(merge_heads(query_out[half * 4 : half * 4 + 4])):
                put(query_grads, (2 * wide + half) * 3 + i, merged)

    def step(wide, k):
        distance = hops - k + 1
        source = parts.at[wide, distance - 1]
        target = landing.at[wide, k - 1]
        sems = (send_sem.at[wide, k - 1], recv_sem.at[wide, k - 1])

        @pl.when(place - distance >= 0)
        def _():
            if k > 1:
                @pl.when(place + 1 < shards)
                def _():
                    arrived = landing.at[wide, k - 2]
                    wait_bytes(arrived, recv_sem.at[wide, k - 2])
                    source[...] = (
                        source[...].astype(jnp.float32) + arrived[...].astype(jnp.float32)
                    ).astype(jnp.bfloat16)

            start_remote(source, target, *sems, line_device(place - 1, shards))

    def finish(wide):
        @pl.when(place + 1 < shards)
        def _():
            arrived = landing.at[wide, hops - 1]
            wait_bytes(arrived, recv_sem.at[wide, hops - 1])
            own_part[:, wide * span : (wide + 1) * span] += arrived[...].astype(jnp.float32)

        first_key, first_value = QH * 3 // 4, QH * 3 // 4 + KVH * 3 // 4
        for i in range(3):
            value = turn(tile(own_part, key_tile(wide, i)), tile(cosine, i), -tile(sine, i))
            put(lows, first_key + wide * 3 + i, value.astype(jnp.bfloat16))
            put(lows, first_value + wide * 3 + i, tile(own_part, value_tile(wide, i)).astype(jnp.bfloat16))

    for wide in range(KVH // 4):
        wide_group(wide)
        step(wide, 1)
    for group in range(QH // 4):
        for i in range(3):
            value = turn(tile(query_grads, group * 3 + i), tile(cosine, i), -tile(sine, i))
            put(lows, group * 3 + i, value.astype(jnp.bfloat16))
    for k in range(2, hops + 1):
        for wide in range(KVH // 4):
            step(wide, k)
    for wide in range(KVH // 4):
        finish(wide)
    for wide in range(KVH // 4):
        for k in range(1, hops + 1):
            @pl.when(place - (hops - k + 1) >= 0)
            def _():
                wait_bytes(parts.at[wide, hops - k], send_sem.at[wide, k - 1])


def attend_back(queries, window, log_total, grads, cosine, sine, own_segment, key_segments, shards, hops):
    rows = queries.shape[0]
    width = QH * HD
    size = (hops + 1) * rows
    bf16, f32, dma = jnp.bfloat16, jnp.float32, pltpu.SemaphoreType.DMA
    vmem = pl.BlockSpec(memory_space=pltpu.VMEM)
    wides = KVH // 4
    return pl.pallas_call(
        functools.partial(attend_back_kernel, shards, hops, rows),
        out_shape=jax.ShapeDtypeStruct((rows, 2 * width), bf16),
        in_specs=[vmem] * 8,
        out_specs=vmem,
        scratch_shapes=[
            pltpu.VMEM((rows, size), f32),
            pltpu.VMEM((rows, width), f32),
            pltpu.VMEM((wides, hops, rows, 6 * LANES), bf16),
            pltpu.VMEM((wides, hops, rows, 6 * LANES), bf16),
            pltpu.VMEM((rows, width), f32),
            dma((wides, hops)),
            dma((wides, hops)),
        ],
        compiler_params=pltpu.CompilerParams(
            collective_id=3, has_side_effects=True, vmem_limit_bytes=48 * 1024 * 1024
        ),
        name="attend_back",
    )(queries, window, log_total, grads, cosine, sine, own_segment, key_segments)


def from_behind(x, axis, by):
    devices = lax.axis_size(axis)
    pairs = [(i, i + by) for i in range(devices) if 0 <= i + by < devices]
    return lax.ppermute(x, axis, pairs)


def swap(x, bit):
    members = lax.axis_size("replica")
    return lax.ppermute(x, "replica", [(r, r ^ (1 << bit)) for r in range(members)])


def mirror(x):
    members, shards = lax.axis_size("replica"), lax.axis_size("shard")
    pairs = [
        (r * shards + s, r * shards + shards - 1 - s)
        for r in range(1, members, 2)
        for s in range(shards)
        if 2 * s != shards - 1
    ]
    moved = lax.ppermute(x, ("replica", "shard"), pairs)
    return jnp.where(lax.axis_index("replica") % 2 == 1, moved, x)


def gain_width(rows):
    return -(-2 * rows // (PARTS * LANES)) * PARTS * LANES


def gather_layer(pieces):
    norm_attn, w_query, w_key, w_value, w_out, norm_ffn, w_gate, w_up, w_down = pieces
    rows = norm_attn.shape[0]
    shards = lax.axis_size("shard")
    gains = jnp.concatenate([norm_attn, norm_ffn])
    gains = jnp.pad(gains[None], ((0, 15), (0, gain_width(rows) - 2 * rows)))
    w_qkv = to_tiles(jnp.concatenate([w_query, w_key, w_value], axis=1))
    w_qkv, w_out, w_gate, w_up, w_down, gains = gather_weights(
        [w_qkv, w_out, w_gate, w_up, w_down, gains], shards
    )
    gains = gains.reshape(shards, 16, -1)[:, 0].astype(jnp.float32)
    norm_attn = gains[:, :rows].reshape(-1)
    norm_ffn = gains[:, rows : 2 * rows].reshape(-1)
    return norm_attn, w_qkv, rows_to_tiles(w_out), norm_ffn, w_gate, w_up, w_down


def sequence_tables(segment, rows, hops):
    place = line_place(lax.axis_size("shard"))
    local_segment = lax.dynamic_slice_in_dim(segment, place * rows, rows)
    starts = jnp.sum((segment[None, :] < local_segment[:, None]).astype(jnp.int32), axis=1)
    cosine, sine = rope_tables(place * rows + jnp.arange(rows, dtype=jnp.int32) - starts)
    padded = jnp.concatenate([jnp.full((hops * rows,), -1, jnp.int32), segment])
    key_segments = jnp.concatenate(
        [lax.dynamic_slice_in_dim(padded, (place + hops - d) * rows, rows) for d in range(hops + 1)]
    )
    return cosine, sine, local_segment[:, None], key_segments[None, :]


def matmul(left, right):
    return jnp.dot(left, right, preferred_element_type=jnp.float32)


def matmul_back(left, right):
    return jnp.einsum("tq,dq->td", left, right, preferred_element_type=jnp.float32)


def row_product(left, right):
    return jnp.einsum("td,tq->dq", left, right, preferred_element_type=jnp.float32)


def forward_layer(inputs, weights, tables, shards, hops):
    norm_attn, w_qkv, w_out, norm_ffn, w_gate, w_up, w_down = weights
    recip_one = lax.rsqrt(jnp.mean(inputs * inputs, axis=-1, keepdims=True) + EPSILON)
    scaled = inputs * recip_one
    normed = (scaled * norm_attn).astype(jnp.bfloat16)
    queries, window, attended, log_total = attend(matmul(normed, w_qkv), *tables, shards, hops)
    middle = inputs + matmul(attended, w_out)
    recip_two = lax.rsqrt(jnp.mean(middle * middle, axis=-1, keepdims=True) + EPSILON)
    scaled_mid = middle * recip_two
    normed_mid = (scaled_mid * norm_ffn).astype(jnp.bfloat16)
    gate_proj = matmul(normed_mid, w_gate)
    up_proj = matmul(normed_mid, w_up)
    hidden = (jax.nn.silu(gate_proj) * up_proj).astype(jnp.bfloat16)
    result = middle + matmul(hidden, w_down)
    saved = (
        scaled,
        recip_one,
        normed,
        queries,
        window,
        log_total,
        attended,
        scaled_mid,
        recip_two,
        normed_mid,
        gate_proj,
        up_proj,
        hidden,
        tables,
    )
    return (result, saved)


def backward_layer(grad_result, weights, saved, shards, hops):
    norm_attn, w_qkv, w_out, norm_ffn, w_gate, w_up, w_down = weights
    (
        scaled,
        recip_one,
        normed,
        queries,
        window,
        log_total,
        attended,
        scaled_mid,
        recip_two,
        normed_mid,
        gate_proj,
        up_proj,
        hidden,
        tables,
    ) = saved
    branch_grad = grad_result.astype(jnp.bfloat16)
    grad_hidden = matmul_back(branch_grad, w_down)
    sigmoid_gate = jax.nn.sigmoid(gate_proj)
    gate_low = (
        grad_hidden * up_proj * (sigmoid_gate * (1.0 + gate_proj * (1.0 - sigmoid_gate)))
    ).astype(jnp.bfloat16)
    up_low = (grad_hidden * jax.nn.silu(gate_proj)).astype(jnp.bfloat16)
    grad_normed_mid = matmul_back(gate_low, w_gate) + matmul_back(up_low, w_up)
    grad_norm_ffn = jnp.sum(grad_normed_mid * scaled_mid, axis=0)
    grad_scaled_mid = grad_normed_mid * norm_ffn
    grad_middle = grad_result + recip_two * (
        grad_scaled_mid
        - scaled_mid * jnp.mean(grad_scaled_mid * scaled_mid, axis=-1, keepdims=True)
    )
    attn_grad = grad_middle.astype(jnp.bfloat16)
    grad_attended = matmul_back(attn_grad, w_out).astype(jnp.bfloat16)
    qkv_low = attend_back(queries, window, log_total, grad_attended, *tables, shards, hops)
    grad_normed = matmul_back(qkv_low, w_qkv)
    grad_norm_attn = jnp.sum(grad_normed * scaled, axis=0)
    grad_scaled = grad_normed * norm_attn
    grad_inputs = grad_middle + recip_one * (
        grad_scaled - scaled * jnp.mean(grad_scaled * scaled, axis=-1, keepdims=True)
    )
    operands = (
        normed,
        qkv_low,
        attended,
        attn_grad,
        normed_mid,
        gate_low,
        up_low,
        hidden,
        branch_grad,
    )
    return (grad_inputs, (grad_norm_attn, grad_norm_ffn), operands)


def reduce_gradients(operand_pairs, gains):
    (
        normed,
        qkv_low,
        attended,
        attn_grad,
        normed_mid,
        gate_low,
        up_low,
        hidden,
        branch_grad,
    ) = (jnp.concatenate(parts, axis=0) for parts in zip(*operand_pairs))
    shards = lax.axis_size("shard")
    rows = gains[0].shape[0] // shards

    def product(left, right):
        return row_product(left, right).astype(jnp.bfloat16)

    gain_term = jnp.stack([gain.reshape(shards, rows) for gain in gains], axis=1)
    gain_term = gain_term.reshape(shards, 1, 2 * rows).astype(jnp.bfloat16)
    gain_term = jnp.pad(gain_term, ((0, 0), (0, 15), (0, gain_width(rows) - 2 * rows)))
    leading = [
        product(hidden, branch_grad),
        product(normed_mid, gate_low),
        product(normed_mid, up_low),
        gain_term.reshape(shards * 16, -1),
    ]
    trailing = [product(normed, from_tiles(qkv_low)), product(from_tiles(attended), attn_grad)]
    totals = [total.astype(jnp.float32) for total in reduce_terms(leading, trailing, shards)]
    members = lax.axis_size("replica")
    for bit in range(PARTS.bit_length() - 1, members.bit_length() - 1):
        totals = [total + swap(total, bit) for total in totals]
    down, gate, up, own_gains, qkv, out = totals
    return (
        own_gains[0, :rows],
        qkv[:, : QH * HD],
        qkv[:, QH * HD : (QH + KVH) * HD],
        qkv[:, (QH + KVH) * HD :],
        out,
        own_gains[0, rows : 2 * rows],
        gate,
        up,
        down,
    )


def body(
    tokens,
    segments,
    norm_attn,
    w_query,
    w_key,
    w_value,
    w_out,
    norm_ffn,
    w_gate,
    w_up,
    w_down,
    cotangent,
):
    micro_count = tokens.shape[0]
    row_count = tokens.shape[2]
    width = tokens.shape[3]
    seq_length = segments.shape[2]
    shards = lax.axis_size("shard")
    hops = line_hops(shards, row_count, seq_length // 2)
    first_section = lax.axis_index("section") == 0

    def choose(early, late):
        return jax.tree.map(lambda a, b: jnp.where(first_section, a, b), early, late)

    tokens, cotangent = mirror(tokens), mirror(cotangent)
    weights = gather_layer(
        (
            norm_attn[0],
            w_query[0],
            w_key[0],
            w_value[0],
            w_out[0],
            norm_ffn[0],
            w_gate[0],
            w_up[0],
            w_down[0],
        )
    )
    all_tables = [sequence_tables(segments[m, 0], row_count, hops) for m in range(micro_count)]
    saved_ticks = []
    result_ticks = []
    arriving = jnp.zeros((row_count, width), jnp.bfloat16)
    for tick_index in range(micro_count + 1):
        own_input = tokens[min(tick_index, micro_count - 1), 0].astype(jnp.float32)
        layer_input = jnp.where(first_section, own_input, arriving.astype(jnp.float32))
        tables = choose(
            all_tables[min(tick_index, micro_count - 1)], all_tables[max(tick_index - 1, 0)]
        )
        result, saved = forward_layer(layer_input, weights, tables, shards, hops)
        result_low = result.astype(jnp.bfloat16)
        result_ticks.append(result_low)
        saved_ticks.append(saved)
        if tick_index < micro_count:
            arriving = from_behind(result_low, "section", 1)
    flow_ticks = []
    gain_sums = None
    operand_ticks = []
    returning = jnp.zeros((row_count, width), jnp.bfloat16)
    for tick_index in range(micro_count + 1):
        later_grad = cotangent[min(tick_index, micro_count - 1), 0].astype(jnp.float32)
        incoming = jnp.where(first_section, returning.astype(jnp.float32), later_grad)
        active = jnp.where(first_section, tick_index >= 1, tick_index < micro_count)
        incoming = jnp.where(active, incoming, 0.0)
        if 0 < tick_index < micro_count:
            saved = choose(saved_ticks[tick_index - 1], saved_ticks[tick_index + 1])
        else:
            saved = saved_ticks[1 if tick_index == 0 else micro_count - 1]
        grad_inputs, gains, operands = backward_layer(incoming, weights, saved, shards, hops)
        flow_ticks.append(grad_inputs)
        if tick_index < micro_count:
            returning = from_behind(grad_inputs.astype(jnp.bfloat16), "section", -1)
        gain_sums = gains if gain_sums is None else jax.tree.map(jnp.add, gain_sums, gains)
        operand_ticks.append(operands)
    edge_operands = choose(operand_ticks[micro_count], operand_ticks[0])
    totals = reduce_gradients(operand_ticks[1:micro_count] + [edge_operands], gain_sums)
    section_outputs = mirror(
        jnp.stack(
            [choose(result_ticks[index], result_ticks[index + 1]) for index in range(micro_count)]
        )
    )
    input_grads = jnp.stack(
        [
            mirror(choose(flow_ticks[index + 1], flow_ticks[index]))
            for index in range(micro_count)
        ]
    )
    return (section_outputs[None, :, None], input_grads[None, :, None]) + tuple(
        total[None] for total in totals
    )


def solution(mesh):
    in_specs = (
        P(None, "replica", "shard", None),
        P(None, "replica", None),
        P("section", "shard"),
        P("section", "shard", None),
        P("section", "shard", None),
        P("section", "shard", None),
        P("section", "shard", None),
        P("section", "shard"),
        P("section", "shard", None),
        P("section", "shard", None),
        P("section", "shard", None),
        P(None, "replica", "shard", None),
    )
    out_specs = (
        P("section", None, "replica", "shard", None),
        P("section", None, "replica", "shard", None),
        P("section", "shard"),
        P("section", "shard", None),
        P("section", "shard", None),
        P("section", "shard", None),
        P("section", "shard", None),
        P("section", "shard"),
        P("section", "shard", None),
        P("section", "shard", None),
        P("section", "shard", None),
    )
    return jax.shard_map(body, mesh=mesh, in_specs=in_specs, out_specs=out_specs, check_vma=False)
```

```python
import functools

import jax
import jax.numpy as jnp
import numpy as np
from jax import lax
from jax.experimental import pallas as pl
from jax.experimental.pallas import tpu as pltpu
from jax.sharding import PartitionSpec as P

QH = 16
KVH = 8
HD = 96
PARTS = 4
LANES = 128


EPSILON = 1e-05
ROPE_BASE = 100000.0


def start_remote(source, target, send_sem, recv_sem, device):
    pltpu.make_async_remote_copy(
        src_ref=source,
        dst_ref=target,
        send_sem=send_sem,
        recv_sem=recv_sem,
        device_id=device,
        device_id_type=pl.DeviceIdType.MESH,
    ).start()


def wait_bytes(ref, sem):
    pltpu.make_async_copy(ref, ref, sem).wait()


def greet(shards):
    place = lax.axis_index("shard")
    member = lax.axis_index("replica")
    barrier = pltpu.get_barrier_semaphore()
    pl.semaphore_signal(barrier, inc=1, device_id={"replica": member ^ 1}, device_id_type=pl.DeviceIdType.MESH)
    pl.semaphore_signal(barrier, inc=1, device_id={"replica": member ^ 2}, device_id_type=pl.DeviceIdType.MESH)

    @pl.when(place > 0)
    def _():
        pl.semaphore_signal(barrier, inc=1, device_id={"shard": place - 1}, device_id_type=pl.DeviceIdType.MESH)

    @pl.when(place < shards - 1)
    def _():
        pl.semaphore_signal(barrier, inc=1, device_id={"shard": place + 1}, device_id_type=pl.DeviceIdType.MESH)

    pl.semaphore_wait(barrier, 2 + (place > 0).astype(jnp.int32) + (place < shards - 1).astype(jnp.int32))


def gather_kernel(shards, chunks, count, *refs):
    pieces, wholes = refs[:count], refs[count : 2 * count]
    held = refs[2 * count : 3 * count]
    (local_sem, own_send, pass_send, line_recv, x_send, x_recv, core_send, core_recv) = refs[
        3 * count :
    ]
    place = lax.axis_index("shard")
    member = lax.axis_index("replica")
    part = member % PARTS
    greet(shards)

    def loads(index):
        return pltpu.make_async_copy(pieces[index], held[index], local_sem.at[index])

    def stores(index):
        rows = pieces[index].shape[0]
        target = wholes[index].at[pl.ds(pl.multiple_of(place * rows, rows), rows), :]
        return pltpu.make_async_copy(held[index], target, local_sem.at[index])

    for index in range(count):
        loads(index).start()

    def window(chunk, block, whose):
        index, first, length = chunk
        rows = pieces[index].shape[0]
        width = pieces[index].shape[1] // PARTS
        return wholes[index].at[
            pl.ds(pl.multiple_of(block * rows + first, length), length),
            pl.ds(pl.multiple_of(whose * width, width), width),
        ]

    def own(j):
        index, first, length = chunks[j]
        width = pieces[index].shape[1] // PARTS
        source = pieces[index].at[
            pl.ds(first, length), pl.ds(pl.multiple_of(part * width, width), width)
        ]
        for slot, way in enumerate((1, -1)):
            @pl.when((place + way >= 0) & (place + way < shards))
            def _():
                start_remote(
                    source,
                    window(chunks[j], place, part),
                    own_send.at[j, slot],
                    line_recv.at[j, place],
                    {"shard": place + way},
                )

    def hop(j, k):
        for way in (1, -1):
            block = place - way * k

            @pl.when((block >= 0) & (block < shards))
            def _():
                mine = window(chunks[j], block, part)
                wait_bytes(mine, line_recv.at[j, block])

                @pl.when((place + way >= 0) & (place + way < shards))
                def _():
                    start_remote(
                        mine, mine, pass_send.at[j, block], line_recv.at[j, block], {"shard": place + way}
                    )

                start_remote(mine, mine, x_send.at[j, block], x_recv.at[j, block], {"replica": member ^ 2})
                start_remote(
                    mine, mine, core_send.at[j, block, 0], core_recv.at[j, block, 0], {"replica": member ^ 1}
                )

    def across(j, k):
        for way in (1, -1):
            block = place - way * k

            @pl.when((block >= 0) & (block < shards))
            def _():
                theirs = window(chunks[j], block, part ^ 2)
                wait_bytes(theirs, x_recv.at[j, block])
                start_remote(
                    theirs, theirs, core_send.at[j, block, 1], core_recv.at[j, block, 1], {"replica": member ^ 1}
                )

    total = len(chunks)
    for step in range(total + shards + 1):
        if step < total:
            own(step)
        if 1 <= step <= count:
            loads(step - 1).wait()
            stores(step - 1).start()
        for k in range(1, shards):
            if 0 <= step - k < total:
                hop(step - k, k)
        for k in range(1, shards):
            if 0 <= step - k - 1 < total:
                across(step - k - 1, k)

    for j in range(total):
        for slot, way in enumerate((1, -1)):
            @pl.when((place + way >= 0) & (place + way < shards))
            def _():
                wait_bytes(window(chunks[j], place, part), own_send.at[j, slot])

        for k in range(1, shards):
            for way in (1, -1):
                block = place - way * k

                @pl.when((block >= 0) & (block < shards))
                def _():
                    mine = window(chunks[j], block, part)

                    @pl.when((place + way >= 0) & (place + way < shards))
                    def _():
                        wait_bytes(mine, pass_send.at[j, block])

                    wait_bytes(mine, x_send.at[j, block])
                    for which in range(2):
                        wait_bytes(mine, core_send.at[j, block, which])
                        wait_bytes(mine, core_recv.at[j, block, which])
    for index in range(count):
        stores(index).wait()


def gather_weights(pieces, shards, pace=192 * 1024):
    chunks = []
    for index, piece in enumerate(pieces):
        rows, width = piece.shape
        cuts = 1
        while rows % (2 * cuts * 16) == 0 and rows // cuts * (width // PARTS) > pace:
            cuts *= 2
        for cut in range(cuts):
            chunks.append((index, cut * (rows // cuts), rows // cuts))
    count, total = len(pieces), len(chunks)
    dma = pltpu.SemaphoreType.DMA
    return pl.pallas_call(
        functools.partial(gather_kernel, shards, tuple(chunks), count),
        out_shape=[jax.ShapeDtypeStruct((shards * p.shape[0], p.shape[1]), p.dtype) for p in pieces],
        in_specs=[pl.BlockSpec(memory_space=pl.ANY)] * count,
        out_specs=[pl.BlockSpec(memory_space=pl.ANY)] * count,
        scratch_shapes=[pltpu.VMEM(p.shape, p.dtype) for p in pieces]
        + [
            dma((count,)),
            dma((total, 2)),
            dma((total, shards)),
            dma((total, shards)),
            dma((total, shards)),
            dma((total, shards)),
            dma((total, shards, 2)),
            dma((total, shards, 2)),
        ],
        compiler_params=pltpu.CompilerParams(collective_id=0, has_side_effects=True, vmem_limit_bytes=24 * 1024 * 1024),
        name="gather_weights",
    )(*pieces)


def add_rows(target, left, right, rows):
    step = next(size for size in (128, 64, 16) if rows % size == 0)

    def body(i, carry):
        window = pl.ds(pl.multiple_of(i * step, step), step)
        target[window, :] = (
            left[window, :].astype(jnp.float32) + right[window, :].astype(jnp.float32)
        ).astype(target.dtype)
        return carry

    lax.fori_loop(0, rows // step, body, 0)


def reduce_kernel(shards, plan, count, *refs):
    leads, trails, heights, kinds = plan
    chunks = leads + trails
    total = len(chunks)
    terms, refs = refs[:count], refs[count:]
    sums, refs = refs[:count], refs[count:]
    near, refs = refs[:count], refs[count:]
    landed, refs = refs[:total], refs[total:]
    passing, refs = refs[:total], refs[total:]
    swapped, refs = refs[: len(trails)], refs[len(trails) :]
    stages = []
    for kind in range(len(kinds)):
        stages.append(refs[:6])
        refs = refs[6:]
    trail_stage, refs = refs[:4], refs[4:]
    (load_sem, core_send, core_recv, x_send, x_recv, line_send, line_recv) = refs[:7]
    (end_local, end_x_send, end_x_recv, end_core_send, end_core_recv) = refs[7:]
    place = lax.axis_index("shard")
    member = lax.axis_index("replica")
    core = member % 2
    side = (member // 2) % 2
    x_mate = {"replica": member ^ 2}
    core_mate = {"replica": member ^ 1}
    greet(shards)

    def leading(j):
        return j < len(leads)

    def height(j):
        return heights[chunks[j][0]]

    def columns(j, whose):
        index, first, width = chunks[j]
        part = terms[index].shape[1] // PARTS
        return pl.ds(pl.multiple_of(whose * part + first, LANES), width)

    def send_near(j):
        index = chunks[j][0]
        for which in range(2):
            start_remote(
                terms[index].at[:, columns(j, (1 - core) * 2 + which)],
                near[index].at[:, columns(j, which)],
                core_send.at[j, which],
                core_recv.at[j, which],
                core_mate,
            )

    def staged(j):
        if leading(j):
            a0, a1, b0, b1, c, d = stages[kinds.index((height(j), chunks[j][2]))]
            return (b0, b1, c, d) if j % 2 else (a0, a1, c, d)
        return trail_stage

    def load_copies(j):
        index = chunks[j][0]
        whose = (1 - side, side) if leading(j) else (0, 1)
        at = staged(j)
        sem = 0 if leading(j) else 4
        sources = [terms[index].at[:, columns(j, core * 2 + w)] for w in whose]
        sources += [near[index].at[:, columns(j, w)] for w in whose]
        return [pltpu.make_async_copy(s, at[i], load_sem.at[sem + i]) for i, s in enumerate(sources)]

    def load(j):
        for which in range(2):
            wait_bytes(near[chunks[j][0]].at[:, columns(j, which)], core_recv.at[j, which])
        for copy in load_copies(j):
            copy.start()

    def near_sum(j):
        size = shards * height(j)
        at = staged(j)
        for copy in load_copies(j):
            copy.wait()
        if leading(j):
            add_rows(at[0], at[0], at[2], size)
            start_remote(at[0], landed[j], x_send.at[j], x_recv.at[j], x_mate)
            add_rows(at[1], at[1], at[3], size)
        else:
            width = chunks[j][2]
            for which in range(2):
                window = landed[j].at[:, pl.ds(which * width, width)]
                add_rows(window, at[which], at[2 + which], size)

    def x_sum(j):
        at = staged(j)
        wait_bytes(at[0], x_send.at[j])
        wait_bytes(landed[j], x_recv.at[j])
        add_rows(landed[j], landed[j], at[1], shards * height(j))

    def block(j, t):
        rows = height(j)
        return landed[j].at[pl.ds(pl.multiple_of(t * rows, rows), rows), :]

    def inside(t):
        return (t >= 0) & (t < shards)

    def line(j, hop):
        for slot, way in enumerate((1, -1)):
            t = place + way * (shards - hop)
            target = passing[j].at[slot, hop - 1]
            sems = (line_send.at[j, slot, hop - 1], line_recv.at[j, slot, hop - 1])
            ahead = {"shard": place + way}
            own = block(j, jnp.clip(t, 0, shards - 1))
            if hop == 1:

                @pl.when(inside(t))
                def _():
                    start_remote(own, target, *sems, ahead)
            else:
                arrived = passing[j].at[slot, hop - 2]

                @pl.when(inside(t) & inside(place - way))
                def _():
                    wait_bytes(arrived, line_recv.at[j, slot, hop - 2])
                    add_rows(arrived, arrived, own, height(j))
                    start_remote(arrived, target, *sems, ahead)

                @pl.when(inside(t) & jnp.logical_not(inside(place - way)))
                def _():
                    start_remote(own, target, *sems, ahead)

    def sum_window(j, whose):
        return sums[chunks[j][0]].at[:, columns(j, whose)]

    def share(j):
        width = chunks[j][2]
        for which in range(1 if leading(j) else 2):
            rows = block(j, place).at[:, pl.ds(which * width, width)]
            target = sum_window(j, core * 2 + (side if leading(j) else which))
            pltpu.make_async_copy(rows, target, end_local.at[j, which]).start()
            start_remote(rows, target, end_core_send.at[j, which], end_core_recv.at[j, which], core_mate)

    def line_end(j):
        mine = block(j, place)
        for slot, way in enumerate((1, -1)):

            @pl.when(inside(place - way))
            def _():
                arrived = passing[j].at[slot, shards - 2]
                wait_bytes(arrived, line_recv.at[j, slot, shards - 2])
                add_rows(mine, mine, arrived, height(j))

        target = sum_window(j, core * 2 + side) if leading(j) else swapped[j - len(leads)]
        start_remote(mine, target, end_x_send.at[j], end_x_recv.at[j], x_mate)
        if leading(j):
            share(j)

    def finish(j):
        if leading(j):
            theirs = sum_window(j, core * 2 + (1 - side))
            wait_bytes(theirs, end_x_recv.at[j])
            start_remote(theirs, theirs, end_core_send.at[j, 1], end_core_recv.at[j, 1], core_mate)
        else:
            mine, other = block(j, place), swapped[j - len(leads)]
            wait_bytes(mine, end_x_send.at[j])
            wait_bytes(other, end_x_recv.at[j])
            add_rows(mine, mine, other, height(j))
            share(j)

    first, second = len(leads), len(trails)
    for j in range(max(first, second)):
        if j < first:
            send_near(j)
        if j < second:
            send_near(first + j)
    load(0)
    load(first)
    for step in range(max(first + shards + 2, second + shards + 1)):
        if step < first:
            near_sum(step)
        if step < second:
            near_sum(first + step)
            if step + 1 < second:
                load(first + step + 1)
            line(first + step, 1)
        for hop in range(2, shards):
            if 0 <= step - hop < first:
                line(step - hop, hop)
            if 0 <= step - hop + 1 < second:
                line(first + step - hop + 1, hop)
        if 0 <= step - shards < first:
            line_end(step - shards)
        if 0 <= step - shards + 1 < second:
            line_end(first + step - shards + 1)
        if 0 <= step - shards - 1 < first:
            finish(step - shards - 1)
        if 0 <= step - shards < second:
            finish(first + step - shards)
        if 1 <= step <= first:
            x_sum(step - 1)
            line(step - 1, 1)
        if step + 1 < first:
            load(step + 1)

    for j in range(total):
        for which in range(2):
            wait_bytes(near[chunks[j][0]].at[:, columns(j, which)], core_send.at[j, which])
        for slot, way in enumerate((1, -1)):
            for hop in range(1, shards):

                @pl.when(inside(place + way * (shards - hop)))
                def _():
                    wait_bytes(passing[j].at[slot, hop - 1], line_send.at[j, slot, hop - 1])

        if leading(j):
            wait_bytes(sum_window(j, 0), end_x_send.at[j])
        for which in range(2):
            if which == 0 or not leading(j):
                wait_bytes(sum_window(j, 0), end_local.at[j, which])
            wait_bytes(sum_window(j, 0), end_core_send.at[j, which])
            wait_bytes(sum_window(j, 0), end_core_recv.at[j, which])


def reduce_terms(leading, trailing, shards, lead_cells=1536 * 256):
    terms = list(leading) + list(trailing)
    count = len(terms)
    heights = tuple(t.shape[0] // shards for t in terms)
    leads, trails = [], []
    for index, term in enumerate(terms):
        part = term.shape[1] // PARTS
        if index < len(leading):
            width = part
            while width % (2 * LANES) == 0 and width * term.shape[0] > lead_cells:
                width //= 2
            if width * term.shape[0] > lead_cells and width % LANES == 0:
                width = LANES
            leads += [(index, first, width) for first in range(0, part, width)]
        else:
            trails += [(index, first, LANES) for first in range(0, part, LANES)]
    kinds = []
    for index, first, width in leads:
        if (heights[index], width) not in kinds:
            kinds.append((heights[index], width))
    chunks = leads + trails
    total = len(chunks)
    bf16, dma = jnp.bfloat16, pltpu.SemaphoreType.DMA

    def rows_and_width(j):
        index, first, width = chunks[j]
        return heights[index], width if j < len(leads) else 2 * width

    scratch = []
    for j in range(total):
        rows, width = rows_and_width(j)
        scratch.append(pltpu.VMEM((shards * rows, width), bf16))
    for j in range(total):
        rows, width = rows_and_width(j)
        scratch.append(pltpu.VMEM((2, shards - 1, rows, width), bf16))
    for j in range(len(leads), total):
        rows, width = rows_and_width(j)
        scratch.append(pltpu.VMEM((rows, width), bf16))
    for rows, width in kinds:
        scratch += [pltpu.VMEM((shards * rows, width), bf16)] * 6
    scratch += [pltpu.VMEM((shards * heights[-1], LANES), bf16)] * 4
    scratch += [
        dma((8,)),
        dma((total, 2)),
        dma((total, 2)),
        dma((total,)),
        dma((total,)),
        dma((total, 2, shards - 1)),
        dma((total, 2, shards - 1)),
        dma((total, 2)),
        dma((total,)),
        dma((total,)),
        dma((total, 2)),
        dma((total, 2)),
    ]
    outs = pl.pallas_call(
        functools.partial(reduce_kernel, shards, (tuple(leads), tuple(trails), heights, tuple(kinds)), count),
        out_shape=[jax.ShapeDtypeStruct((t.shape[0] // shards, t.shape[1]), bf16) for t in terms]
        + [jax.ShapeDtypeStruct((t.shape[0], t.shape[1] // 2), bf16) for t in terms],
        in_specs=[pl.BlockSpec(memory_space=pl.ANY)] * count,
        out_specs=[pl.BlockSpec(memory_space=pl.ANY)] * (2 * count),
        scratch_shapes=scratch,
        compiler_params=pltpu.CompilerParams(
            collective_id=1, has_side_effects=True, vmem_limit_bytes=62 * 1024 * 1024
        ),
        name="reduce_terms",
    )(*terms)
    return outs[:count]


def tile_order():
    order = np.zeros(4 * HD, np.int32)
    for tile in range(3):
        for lane in range(LANES):
            upper, low = divmod(lane, LANES // 2)
            if low < HD // 2:
                head, item = tile, low
            else:
                head, item = 3, 16 * tile + low - HD // 2
            order[tile * LANES + lane] = head * HD + upper * (HD // 2) + item
    return order


def tile_matrix():
    order = tile_order()
    return (np.arange(4 * HD)[:, None] == order[None, :]).astype(np.float32)


def to_tiles(x):
    matrix = jnp.asarray(tile_matrix(), jnp.bfloat16)
    span = 4 * HD
    return jnp.concatenate(
        [
            jnp.dot(x[:, i : i + span], matrix, preferred_element_type=jnp.float32).astype(x.dtype)
            for i in range(0, x.shape[1], span)
        ],
        axis=1,
    )


def from_tiles(x):
    matrix = jnp.asarray(tile_matrix().T, jnp.bfloat16)
    span = 4 * HD
    return jnp.concatenate(
        [
            jnp.dot(x[:, i : i + span], matrix, preferred_element_type=jnp.float32).astype(x.dtype)
            for i in range(0, x.shape[1], span)
        ],
        axis=1,
    )


def rows_to_tiles(x):
    matrix = jnp.asarray(tile_matrix().T, jnp.bfloat16)
    groups = x.reshape(-1, 4 * HD, x.shape[1])
    moved = jnp.einsum("lk,gkn->gln", matrix, groups, preferred_element_type=jnp.float32)
    return moved.astype(x.dtype).reshape(x.shape)


def rope_tables(positions):
    item = tile_order() % (HD // 2)
    frequency = ROPE_BASE ** (-(jnp.asarray(item, jnp.float32) * 2.0) / HD)
    angles = positions.astype(jnp.float32)[:, None] * frequency[None, :]
    upper = (np.arange(3 * LANES) // (LANES // 2)) % 2 == 1
    sign = jnp.asarray(np.where(upper, 1.0, -1.0), jnp.float32)
    return jnp.cos(angles), jnp.sin(angles) * sign[None, :]


def spare_lanes(shape):
    return lax.broadcasted_iota(jnp.int32, shape, 1) % (LANES // 2) >= HD // 2


def last_head(tiles):
    spare = spare_lanes(tiles[0].shape)
    return sum(
        pltpu.roll(jnp.where(spare, tiles[i], 0.0), LANES - HD // 2 + 16 * i, 1) for i in range(3)
    )


def merge_heads(heads):
    spare = spare_lanes(heads[0].shape)
    return [
        jnp.where(spare, pltpu.roll(heads[3], HD // 2 - 16 * i, 1), heads[i])
        for i in range(3)
    ]


def tile(ref, index):
    return ref[:, index * LANES : (index + 1) * LANES]


def put(ref, index, value):
    ref[:, index * LANES : (index + 1) * LANES] = value


def turn(value, cosine, sine):
    return value * cosine + pltpu.roll(value, LANES // 2, 1) * sine


def key_tile(group, i):
    return group * 6 + i


def value_tile(group, i):
    return group * 6 + 3 + i


def fill_bias(bias, own_segment, key_segments, rows):
    size = key_segments.shape[1]
    same = own_segment[...] == key_segments[...]
    query = lax.broadcasted_iota(jnp.int32, (rows, size), 0)
    key = lax.broadcasted_iota(jnp.int32, (rows, size), 1)
    bias[...] = jnp.where(same & ((key >= rows) | (key <= query)), 0.0, -1e30)


def inside(place, shards):
    return (place >= 0) & (place < shards)


def line_place(shards):
    place = lax.axis_index("shard")
    mirrored = lax.axis_index("replica") % 2 == 1
    return jnp.where(mirrored, shards - 1 - place, place)


def line_device(place, shards):
    mirrored = lax.axis_index("replica") % 2 == 1
    return {"shard": jnp.where(mirrored, shards - 1 - place, place)}


def greet_line(shards, way):
    place = line_place(shards)
    barrier = pltpu.get_barrier_semaphore()

    @pl.when(inside(place - way, shards))
    def _():
        pl.semaphore_signal(
            barrier,
            inc=1,
            device_id=line_device(place - way, shards),
            device_id_type=pl.DeviceIdType.MESH,
        )

    @pl.when(inside(place + way, shards))
    def _():
        pl.semaphore_wait(barrier, 1)


def dot(left, right, dims):
    return lax.dot_general(left, right, (dims, ((), ())), preferred_element_type=jnp.float32)


NT = ((1,), (1,))
NN = ((1,), (0,))
TN = ((0,), (0,))


def attend_kernel(
    shards, hops, rows, raw, cosine, sine, own_segment, key_segments,
    queries, window, attended, log_total,
    held, last, bias, query_heads, send_sem, recv_sem, keep_sem,
):
    place = line_place(shards)
    greet_line(shards, 1)

    def slot(distance):
        return held.at[pl.ds(distance * rows, rows), :]

    first_key, first_value = QH * 3 // 4, QH * 3 // 4 + KVH * 3 // 4
    for group in range(KVH // 4):
        for i in range(3):
            value = turn(tile(raw, first_key + group * 3 + i), tile(cosine, i), tile(sine, i))
            held[pl.ds(0, rows), key_tile(group, i) * LANES : (key_tile(group, i) + 1) * LANES] = value.astype(
                jnp.bfloat16
            )
            value = tile(raw, first_value + group * 3 + i)
            held[pl.ds(0, rows), value_tile(group, i) * LANES : (value_tile(group, i) + 1) * LANES] = (
                value.astype(jnp.bfloat16)
            )

    def send(distance):
        @pl.when((place + 1 < shards) & (place - distance >= 0))
        def _():
            start_remote(
                slot(distance),
                slot(distance + 1),
                send_sem.at[distance],
                recv_sem.at[distance],
                line_device(place + 1, shards),
            )

    send(0)
    fill_bias(bias, own_segment, key_segments, rows)
    for group in range(QH // 4):
        tiles = []
        for i in range(3):
            value = turn(tile(raw, group * 3 + i), tile(cosine, i), tile(sine, i))
            put(queries, group * 3 + i, value.astype(jnp.bfloat16))
            tiles.append(value)
        spare = spare_lanes(tiles[0].shape)
        for i in range(3):
            query_heads[group * 4 + i] = jnp.where(spare, 0.0, tiles[i]).astype(jnp.bfloat16)
        query_heads[group * 4 + 3] = last_head(tiles).astype(jnp.bfloat16)

    def receive(distance):
        @pl.when(place - distance >= 0)
        def _():
            wait_bytes(slot(distance), recv_sem.at[distance - 1])

        @pl.when(place - distance < 0)
        def _():
            held[pl.ds(distance * rows, rows), :] = jnp.zeros((rows, held.shape[1]), held.dtype)

        if distance < hops:
            send(distance)

    def scores_values(head, first, size):
        wide, item = divmod(head // 2, 4)
        span = pl.ds(first, size)
        if item == 3:
            keys, values = last[wide * 2, span], last[wide * 2 + 1, span]
        else:
            at = [spot(wide, item) * LANES for spot in (key_tile, value_tile)]
            keys, values = (held[span, lane : lane + LANES] for lane in at)
        return dot(query_heads[head], keys, NT) * HD ** (-0.5) + bias[:, first : first + size], values

    def fill_last(first, size):
        for wide in range(KVH // 4):
            for which, at in enumerate((key_tile(wide, 0), value_tile(wide, 0))):
                tiles = [
                    held[pl.ds(first, size), (at + i) * LANES : (at + i + 1) * LANES].astype(jnp.float32)
                    for i in range(3)
                ]
                last[wide * 2 + which, pl.ds(first, size)] = last_head(tiles).astype(jnp.bfloat16)

    for distance in range(1, hops):
        receive(distance)
    near = hops * rows
    fill_last(0, near)
    state = []
    for head in range(QH):
        scores, values = scores_values(head, 0, near)
        top = jnp.max(scores, axis=1, keepdims=True)
        exponent = jnp.exp(scores - top)
        total = jnp.sum(exponent, axis=1, keepdims=True)
        state.append((top, total, dot(exponent.astype(jnp.bfloat16), values, NN)))
    receive(hops)
    keep = pltpu.make_async_copy(held, window, keep_sem)
    keep.start()
    fill_last(near, rows)
    lane = lax.broadcasted_iota(jnp.int32, (rows, LANES), 1)
    totals = jnp.zeros((rows, LANES), jnp.float32)
    for group in range(QH // 4):
        outs = []
        for head in range(group * 4, group * 4 + 4):
            before, total, out = state[head]
            scores, values = scores_values(head, near, rows)
            top = jnp.maximum(before, jnp.max(scores, axis=1, keepdims=True))
            exponent = jnp.exp(scores - top)
            shrink = jnp.exp(before - top)
            total = total * shrink + jnp.sum(exponent, axis=1, keepdims=True)
            out = out * shrink + dot(exponent.astype(jnp.bfloat16), values, NN)
            outs.append(out * (1.0 / total))
            totals = jnp.where(lane == head, top + jnp.log(total), totals)
        for i, merged in enumerate(merge_heads(outs)):
            put(attended, group * 3 + i, merged.astype(jnp.bfloat16))
    log_total[...] = totals
    keep.wait()
    for distance in range(hops):
        @pl.when((place + 1 < shards) & (place - distance >= 0))
        def _():
            wait_bytes(slot(distance), send_sem.at[distance])


def line_hops(shards, rows, longest):
    return min(shards - 1, -(-(longest - 1) // rows))


def attend(raw, cosine, sine, own_segment, key_segments, shards, hops):
    rows = raw.shape[0]
    width = QH * HD
    size = (hops + 1) * rows
    bf16, f32, dma = jnp.bfloat16, jnp.float32, pltpu.SemaphoreType.DMA
    vmem = pl.BlockSpec(memory_space=pltpu.VMEM)
    return pl.pallas_call(
        functools.partial(attend_kernel, shards, hops, rows),
        out_shape=[
            jax.ShapeDtypeStruct((rows, width), bf16),
            jax.ShapeDtypeStruct((size, width), bf16),
            jax.ShapeDtypeStruct((rows, width), bf16),
            jax.ShapeDtypeStruct((rows, LANES), f32),
        ],
        in_specs=[vmem] * 5,
        out_specs=[vmem, pl.BlockSpec(memory_space=pl.ANY), vmem, vmem],
        scratch_shapes=[
            pltpu.VMEM((size, width), bf16),
            pltpu.VMEM((KVH // 2, size, LANES), bf16),
            pltpu.VMEM((rows, size), f32),
            pltpu.VMEM((QH, rows, LANES), bf16),
            dma((hops,)),
            dma((hops,)),
            dma,
        ],
        compiler_params=pltpu.CompilerParams(
            collective_id=2, has_side_effects=True, vmem_limit_bytes=62 * 1024 * 1024
        ),
        name="attend",
    )(raw, cosine, sine, own_segment, key_segments)


def attend_back_kernel(
    shards, hops, rows, queries, window, log_total, grads, cosine, sine, own_segment, key_segments,
    lows,
    bias, own_part, parts, landing, query_grads, send_sem, recv_sem,
):
    place = line_place(shards)
    greet_line(shards, -1)
    fill_bias(bias, own_segment, key_segments, rows)
    span = 6 * LANES

    def heads_of(ref, group):
        tiles = [tile(ref, group * 3 + i).astype(jnp.float32) for i in range(3)]
        spare = spare_lanes(tiles[0].shape)
        heads = [jnp.where(spare, 0.0, t).astype(jnp.bfloat16) for t in tiles]
        return heads + [last_head(tiles).astype(jnp.bfloat16)]

    def column(head):
        lane = lax.broadcasted_iota(jnp.int32, (rows, LANES), 1)
        return jnp.sum(jnp.where(lane == head, log_total[...], 0.0), axis=1, keepdims=True)

    def wide_group(wide):
        heads = heads_of(queries, 2 * wide) + heads_of(queries, 2 * wide + 1)
        grad_heads = heads_of(grads, 2 * wide) + heads_of(grads, 2 * wide + 1)
        key_grads, value_grads = [], []
        query_out = []
        key_tiles = [tile(window, key_tile(wide, i)) for i in range(3)]
        value_tiles = [tile(window, value_tile(wide, i)) for i in range(3)]
        key_tiles.append(last_head([t.astype(jnp.float32) for t in key_tiles]).astype(jnp.bfloat16))
        value_tiles.append(last_head([t.astype(jnp.float32) for t in value_tiles]).astype(jnp.bfloat16))
        for item in range(4):
            keys, values = key_tiles[item], value_tiles[item]
            key_grad = value_grad = None
            for one in (2 * item, 2 * item + 1):
                query, grad = heads[one], grad_heads[one]
                scores = dot(query, keys, NT) * HD ** (-0.5) + bias[...]
                probs = jnp.exp(scores - column(wide * 8 + one))
                grad_probs = dot(grad, values, NT)
                along = jnp.sum(probs * grad_probs, axis=1, keepdims=True)
                grad_scores = (probs * (grad_probs - along)).astype(jnp.bfloat16)
                query_out.append(dot(grad_scores, keys, NN) * HD ** (-0.5))
                key_one = dot(grad_scores, query, TN)
                value_one = dot(probs.astype(jnp.bfloat16), grad, TN)
                key_grad = key_one if key_grad is None else key_grad + key_one
                value_grad = value_one if value_grad is None else value_grad + value_one
            key_grads.append(key_grad * HD ** (-0.5))
            value_grads.append(value_grad)
        for which, grads_of in enumerate((key_grads, value_grads)):
            for i, merged in enumerate(merge_heads(grads_of)):
                at = which * 3 + i
                own_part[:, (wide * 6 + at) * LANES : (wide * 6 + at + 1) * LANES] = merged[:rows]
                for distance in range(1, hops + 1):
                    parts[wide, distance - 1, :, at * LANES : (at + 1) * LANES] = merged[
                        distance * rows : (distance + 1) * rows
                    ].astype(jnp.bfloat16)
        for half in range(2):
            for i, merged in enumerate(merge_heads(query_out[half * 4 : half * 4 + 4])):
                put(query_grads, (2 * wide + half) * 3 + i, merged)

    def step(wide, k):
        distance = hops - k + 1
        source = parts.at[wide, distance - 1]
        target = landing.at[wide, k - 1]
        sems = (send_sem.at[wide, k - 1], recv_sem.at[wide, k - 1])

        @pl.when(place - distance >= 0)
        def _():
            if k > 1:
                @pl.when(place + 1 < shards)
                def _():
                    arrived = landing.at[wide, k - 2]
                    wait_bytes(arrived, recv_sem.at[wide, k - 2])
                    source[...] = (
                        source[...].astype(jnp.float32) + arrived[...].astype(jnp.float32)
                    ).astype(jnp.bfloat16)

            start_remote(source, target, *sems, line_device(place - 1, shards))

    def finish(wide):
        @pl.when(place + 1 < shards)
        def _():
            arrived = landing.at[wide, hops - 1]
            wait_bytes(arrived, recv_sem.at[wide, hops - 1])
            own_part[:, wide * span : (wide + 1) * span] += arrived[...].astype(jnp.float32)

        first_key, first_value = QH * 3 // 4, QH * 3 // 4 + KVH * 3 // 4
        for i in range(3):
            value = turn(tile(own_part, key_tile(wide, i)), tile(cosine, i), -tile(sine, i))
            put(lows, first_key + wide * 3 + i, value.astype(jnp.bfloat16))
            put(lows, first_value + wide * 3 + i, tile(own_part, value_tile(wide, i)).astype(jnp.bfloat16))

    for wide in range(KVH // 4):
        wide_group(wide)
        step(wide, 1)
    for group in range(QH // 4):
        for i in range(3):
            value = turn(tile(query_grads, group * 3 + i), tile(cosine, i), -tile(sine, i))
            put(lows, group * 3 + i, value.astype(jnp.bfloat16))
    for k in range(2, hops + 1):
        for wide in range(KVH // 4):
            step(wide, k)
    for wide in range(KVH // 4):
        finish(wide)
    for wide in range(KVH // 4):
        for k in range(1, hops + 1):
            @pl.when(place - (hops - k + 1) >= 0)
            def _():
                wait_bytes(parts.at[wide, hops - k], send_sem.at[wide, k - 1])


def attend_back(queries, window, log_total, grads, cosine, sine, own_segment, key_segments, shards, hops):
    rows = queries.shape[0]
    width = QH * HD
    size = (hops + 1) * rows
    bf16, f32, dma = jnp.bfloat16, jnp.float32, pltpu.SemaphoreType.DMA
    vmem = pl.BlockSpec(memory_space=pltpu.VMEM)
    wides = KVH // 4
    return pl.pallas_call(
        functools.partial(attend_back_kernel, shards, hops, rows),
        out_shape=jax.ShapeDtypeStruct((rows, 2 * width), bf16),
        in_specs=[vmem] * 8,
        out_specs=vmem,
        scratch_shapes=[
            pltpu.VMEM((rows, size), f32),
            pltpu.VMEM((rows, width), f32),
            pltpu.VMEM((wides, hops, rows, 6 * LANES), bf16),
            pltpu.VMEM((wides, hops, rows, 6 * LANES), bf16),
            pltpu.VMEM((rows, width), f32),
            dma((wides, hops)),
            dma((wides, hops)),
        ],
        compiler_params=pltpu.CompilerParams(
            collective_id=3, has_side_effects=True, vmem_limit_bytes=62 * 1024 * 1024
        ),
        name="attend_back",
    )(queries, window, log_total, grads, cosine, sine, own_segment, key_segments)


def sigmoid(value):
    return 1.0 / (1.0 + jnp.exp(-value))


def feed_kernel(
    inputs,
    attended,
    w_out,
    gain,
    w_gate,
    w_up,
    w_down,
    middle,
    normed,
    gate,
    up,
    hidden,
    result,
    total,
):
    step = pl.program_id(0)

    @pl.when(step == 0)
    def _():
        value = inputs[...] + dot(attended[...], w_out[...], NN)
        middle[...] = value
        recip = lax.rsqrt(jnp.mean(value * value, axis=-1, keepdims=True) + EPSILON)
        normed[...] = (value * recip * gain[...]).astype(jnp.bfloat16)
        total[...] = value

    gate_value = dot(normed[...], w_gate[...], NN)
    up_value = dot(normed[...], w_up[...], NN)
    low = (gate_value * sigmoid(gate_value) * up_value).astype(jnp.bfloat16)
    gate[...] = gate_value.astype(jnp.bfloat16)
    up[...] = up_value.astype(jnp.bfloat16)
    hidden[...] = low
    total[...] += dot(low, w_down[...], NN)

    @pl.when(step == pl.num_programs(0) - 1)
    def _():
        result[...] = total[...].astype(jnp.bfloat16)


def whole(shape):
    return pl.BlockSpec(shape, lambda i: (0, 0), pipeline_mode=pl.Buffered(1))


def feed_forward(inputs, attended, w_out, gain, w_gate, w_up, w_down, block=1024):
    rows, width = inputs.shape
    units = w_gate.shape[1]
    f32, bf16 = jnp.float32, jnp.bfloat16
    columns = pl.BlockSpec((rows, block), lambda i: (0, i))
    weight = pl.BlockSpec((width, block), lambda i: (0, i))
    return pl.pallas_call(
        feed_kernel,
        grid=(units // block,),
        out_shape=[
            jax.ShapeDtypeStruct((rows, width), f32),
            jax.ShapeDtypeStruct((rows, width), bf16),
            jax.ShapeDtypeStruct((rows, units), bf16),
            jax.ShapeDtypeStruct((rows, units), bf16),
            jax.ShapeDtypeStruct((rows, units), bf16),
            jax.ShapeDtypeStruct((rows, width), bf16),
        ],
        in_specs=[
            whole((rows, width)),
            whole(attended.shape),
            whole(w_out.shape),
            whole((1, width)),
            weight,
            weight,
            pl.BlockSpec((block, width), lambda i: (i, 0)),
        ],
        out_specs=[
            whole((rows, width)),
            whole((rows, width)),
            columns,
            columns,
            columns,
            whole((rows, width)),
        ],
        scratch_shapes=[pltpu.VMEM((rows, width), f32)],
        compiler_params=pltpu.CompilerParams(vmem_limit_bytes=62 * 1024 * 1024),
        cost_estimate=pl.CostEstimate(
            flops=6 * rows * width * units + 2 * rows * width * width,
            bytes_accessed=6 * width * units + 2 * width * width + 6 * rows * units + 14 * rows * width,
            transcendentals=rows * units,
        ),
        name="feed_forward",
    )(inputs, attended, w_out, gain[None], w_gate, w_up, w_down)


def feed_back_kernel(
    grads,
    middle,
    gain,
    w_out,
    gate,
    up,
    w_gate,
    w_up,
    w_down,
    gate_low,
    up_low,
    grad_middle,
    attn_grad,
    grad_attended,
    gain_grad,
    branch,
    total,
):
    step = pl.program_id(0)

    @pl.when(step == 0)
    def _():
        branch[...] = grads[...].astype(jnp.bfloat16)
        total[...] = jnp.zeros_like(total)

    grad_hidden = dot(branch[...], w_down[...], NT)
    gate_value, up_value = gate[...].astype(jnp.float32), up[...].astype(jnp.float32)
    share = sigmoid(gate_value)
    one = (grad_hidden * up_value * (share * (1.0 + gate_value * (1.0 - share)))).astype(jnp.bfloat16)
    two = (grad_hidden * (gate_value * share)).astype(jnp.bfloat16)
    gate_low[...] = one
    up_low[...] = two
    total[...] += dot(one, w_gate[...], NT) + dot(two, w_up[...], NT)

    @pl.when(step == pl.num_programs(0) - 1)
    def _():
        value = middle[...]
        recip = lax.rsqrt(jnp.mean(value * value, axis=-1, keepdims=True) + EPSILON)
        scaled = value * recip
        grad = total[...]
        gain_grad[...] = jnp.sum(grad * scaled, axis=0, keepdims=True)
        grad = grad * gain[...]
        grad = grads[...] + recip * (
            grad - scaled * jnp.mean(grad * scaled, axis=-1, keepdims=True)
        )
        grad_middle[...] = grad
        attn_grad[...] = grad.astype(jnp.bfloat16)
        grad_attended[...] = dot(attn_grad[...], w_out[...], NT).astype(jnp.bfloat16)


def feed_back(grads, middle, gain, w_out, gate, up, w_gate, w_up, w_down, block=1024):
    rows, width = grads.shape
    units = w_gate.shape[1]
    f32, bf16 = jnp.float32, jnp.bfloat16
    columns = pl.BlockSpec((rows, block), lambda i: (0, i))
    weight = pl.BlockSpec((width, block), lambda i: (0, i))
    return pl.pallas_call(
        feed_back_kernel,
        grid=(units // block,),
        out_shape=[
            jax.ShapeDtypeStruct((rows, units), bf16),
            jax.ShapeDtypeStruct((rows, units), bf16),
            jax.ShapeDtypeStruct((rows, width), f32),
            jax.ShapeDtypeStruct((rows, width), bf16),
            jax.ShapeDtypeStruct((rows, w_out.shape[0]), bf16),
            jax.ShapeDtypeStruct((1, width), f32),
        ],
        in_specs=[
            whole((rows, width)),
            whole((rows, width)),
            whole((1, width)),
            whole(w_out.shape),
            columns,
            columns,
            weight,
            weight,
            pl.BlockSpec((block, width), lambda i: (i, 0)),
        ],
        out_specs=[
            columns,
            columns,
            whole((rows, width)),
            whole((rows, width)),
            whole((rows, w_out.shape[0])),
            whole((1, width)),
        ],
        scratch_shapes=[pltpu.VMEM((rows, width), bf16), pltpu.VMEM((rows, width), f32)],
        compiler_params=pltpu.CompilerParams(vmem_limit_bytes=62 * 1024 * 1024),
        cost_estimate=pl.CostEstimate(
            flops=6 * rows * width * units + 2 * rows * width * width,
            bytes_accessed=6 * width * units + 2 * width * width + 8 * rows * units + 16 * rows * width,
            transcendentals=rows * units,
        ),
        name="feed_back",
    )(grads, middle, gain[None], w_out, gate, up, w_gate, w_up, w_down)


def from_behind(x, axis, by):
    devices = lax.axis_size(axis)
    pairs = [(i, i + by) for i in range(devices) if 0 <= i + by < devices]
    return lax.ppermute(x, axis, pairs)


def swap(x, bit):
    members = lax.axis_size("replica")
    return lax.ppermute(x, "replica", [(r, r ^ (1 << bit)) for r in range(members)])


def mirror(x):
    members, shards = lax.axis_size("replica"), lax.axis_size("shard")
    pairs = [
        (r * shards + s, r * shards + shards - 1 - s)
        for r in range(1, members, 2)
        for s in range(shards)
        if 2 * s != shards - 1
    ]
    moved = lax.ppermute(x, ("replica", "shard"), pairs)
    return jnp.where(lax.axis_index("replica") % 2 == 1, moved, x)


def gain_width(rows):
    return -(-2 * rows // (PARTS * LANES)) * PARTS * LANES


def gather_layer(pieces):
    norm_attn, w_query, w_key, w_value, w_out, norm_ffn, w_gate, w_up, w_down = pieces
    rows = norm_attn.shape[0]
    shards = lax.axis_size("shard")
    gains = jnp.concatenate([norm_attn, norm_ffn])
    gains = jnp.pad(gains[None], ((0, 15), (0, gain_width(rows) - 2 * rows)))
    w_qkv = to_tiles(jnp.concatenate([w_query, w_key, w_value], axis=1))
    w_qkv, w_out, w_gate, w_up, w_down, gains = gather_weights(
        [w_qkv, w_out, w_gate, w_up, w_down, gains], shards
    )
    gains = gains.reshape(shards, 16, -1)[:, 0].astype(jnp.float32)
    norm_attn = gains[:, :rows].reshape(-1)
    norm_ffn = gains[:, rows : 2 * rows].reshape(-1)
    return norm_attn, w_qkv, rows_to_tiles(w_out), norm_ffn, w_gate, w_up, w_down


def sequence_tables(segment, rows, hops):
    place = line_place(lax.axis_size("shard"))
    local_segment = lax.dynamic_slice_in_dim(segment, place * rows, rows)
    starts = jnp.sum((segment[None, :] < local_segment[:, None]).astype(jnp.int32), axis=1)
    cosine, sine = rope_tables(place * rows + jnp.arange(rows, dtype=jnp.int32) - starts)
    padded = jnp.concatenate([jnp.full((hops * rows,), -1, jnp.int32), segment])
    key_segments = jnp.concatenate(
        [lax.dynamic_slice_in_dim(padded, (place + hops - d) * rows, rows) for d in range(hops + 1)]
    )
    return cosine, sine, local_segment[:, None], key_segments[None, :]


def matmul(left, right):
    return jnp.dot(left, right, preferred_element_type=jnp.float32)


def matmul_back(left, right):
    return jnp.einsum("tq,dq->td", left, right, preferred_element_type=jnp.float32)


def row_product(left, right):
    return jnp.einsum("td,tq->dq", left, right, preferred_element_type=jnp.float32)


def forward_layer(inputs, weights, tables, shards, hops):
    norm_attn, w_qkv, w_out, norm_ffn, w_gate, w_up, w_down = weights
    recip_one = lax.rsqrt(jnp.mean(inputs * inputs, axis=-1, keepdims=True) + EPSILON)
    scaled = inputs * recip_one
    normed = (scaled * norm_attn).astype(jnp.bfloat16)
    queries, window, attended, log_total = attend(matmul(normed, w_qkv), *tables, shards, hops)
    middle, normed_mid, gate, up, hidden, result = feed_forward(
        inputs, attended, w_out, norm_ffn, w_gate, w_up, w_down
    )
    saved = (
        scaled,
        recip_one,
        normed,
        queries,
        window,
        log_total,
        attended,
        middle,
        normed_mid,
        gate,
        up,
        hidden,
        tables,
    )
    return (result, saved)


def backward_layer(grad_result, weights, saved, shards, hops):
    norm_attn, w_qkv, w_out, norm_ffn, w_gate, w_up, w_down = weights
    (
        scaled,
        recip_one,
        normed,
        queries,
        window,
        log_total,
        attended,
        middle,
        normed_mid,
        gate,
        up,
        hidden,
        tables,
    ) = saved
    branch_grad = grad_result.astype(jnp.bfloat16)
    gate_low, up_low, grad_middle, attn_grad, grad_attended, grad_norm_ffn = feed_back(
        grad_result, middle, norm_ffn, w_out, gate, up, w_gate, w_up, w_down
    )
    qkv_low = attend_back(queries, window, log_total, grad_attended, *tables, shards, hops)
    grad_normed = matmul_back(qkv_low, w_qkv)
    grad_norm_attn = jnp.sum(grad_normed * scaled, axis=0)
    grad_scaled = grad_normed * norm_attn
    grad_inputs = grad_middle + recip_one * (
        grad_scaled - scaled * jnp.mean(grad_scaled * scaled, axis=-1, keepdims=True)
    )
    operands = (
        normed,
        qkv_low,
        attended,
        attn_grad,
        normed_mid,
        gate_low,
        up_low,
        hidden,
        branch_grad,
    )
    return (grad_inputs, (grad_norm_attn, grad_norm_ffn[0]), operands)


def reduce_gradients(operand_pairs, gains):
    (
        normed,
        qkv_low,
        attended,
        attn_grad,
        normed_mid,
        gate_low,
        up_low,
        hidden,
        branch_grad,
    ) = (jnp.concatenate(parts, axis=0) for parts in zip(*operand_pairs))
    shards = lax.axis_size("shard")
    rows = gains[0].shape[0] // shards

    def product(left, right):
        return row_product(left, right).astype(jnp.bfloat16)

    gain_term = jnp.stack([gain.reshape(shards, rows) for gain in gains], axis=1)
    gain_term = gain_term.reshape(shards, 1, 2 * rows).astype(jnp.bfloat16)
    gain_term = jnp.pad(gain_term, ((0, 0), (0, 15), (0, gain_width(rows) - 2 * rows)))
    leading = [
        product(hidden, branch_grad),
        product(normed_mid, gate_low),
        product(normed_mid, up_low),
        gain_term.reshape(shards * 16, -1),
    ]
    trailing = [product(normed, from_tiles(qkv_low)), product(from_tiles(attended), attn_grad)]
    totals = [total.astype(jnp.float32) for total in reduce_terms(leading, trailing, shards)]
    members = lax.axis_size("replica")
    for bit in range(PARTS.bit_length() - 1, members.bit_length() - 1):
        totals = [total + swap(total, bit) for total in totals]
    down, gate, up, own_gains, qkv, out = totals
    return (
        own_gains[0, :rows],
        qkv[:, : QH * HD],
        qkv[:, QH * HD : (QH + KVH) * HD],
        qkv[:, (QH + KVH) * HD :],
        out,
        own_gains[0, rows : 2 * rows],
        gate,
        up,
        down,
    )


def body(
    tokens,
    segments,
    norm_attn,
    w_query,
    w_key,
    w_value,
    w_out,
    norm_ffn,
    w_gate,
    w_up,
    w_down,
    cotangent,
):
    micro_count = tokens.shape[0]
    row_count = tokens.shape[2]
    width = tokens.shape[3]
    seq_length = segments.shape[2]
    shards = lax.axis_size("shard")
    hops = line_hops(shards, row_count, seq_length // 2)
    first_section = lax.axis_index("section") == 0

    def choose(early, late):
        return jax.tree.map(lambda a, b: jnp.where(first_section, a, b), early, late)

    weights = gather_layer(
        (
            norm_attn[0],
            w_query[0],
            w_key[0],
            w_value[0],
            w_out[0],
            norm_ffn[0],
            w_gate[0],
            w_up[0],
            w_down[0],
        )
    )
    later, gathered = lax.optimization_barrier((tokens[1:], weights[0]))
    weights = (gathered,) + weights[1:]
    tokens = jnp.concatenate([mirror(tokens[:1]), mirror(later)]) if micro_count > 1 else mirror(tokens)
    all_tables = [sequence_tables(segments[m, 0], row_count, hops) for m in range(micro_count)]
    saved_ticks = []
    result_ticks = []
    later_grads = []
    arriving = jnp.zeros((row_count, width), jnp.bfloat16)
    for tick_index in range(micro_count + 1):
        own_input = tokens[min(tick_index, micro_count - 1), 0].astype(jnp.float32)
        layer_input = jnp.where(first_section, own_input, arriving.astype(jnp.float32))
        if tick_index > 0:
            layer_input, later_grads[-1] = lax.optimization_barrier((layer_input, later_grads[-1]))
        tables = choose(
            all_tables[min(tick_index, micro_count - 1)], all_tables[max(tick_index - 1, 0)]
        )
        result_low, saved = forward_layer(layer_input, weights, tables, shards, hops)
        result_ticks.append(result_low)
        saved_ticks.append(saved)
        if tick_index < micro_count:
            grad, attended = lax.optimization_barrier((cotangent[tick_index, 0], saved[6]))
            later_grads.append(mirror(grad))
        if tick_index < micro_count:
            arriving = from_behind(result_low, "section", 1)
    flow_ticks = []
    gain_sums = None
    operand_ticks = []
    returning = jnp.zeros((row_count, width), jnp.bfloat16)
    for tick_index in range(micro_count + 1):
        later_grad = later_grads[min(tick_index, micro_count - 1)].astype(jnp.float32)
        incoming = jnp.where(first_section, returning.astype(jnp.float32), later_grad)
        active = jnp.where(first_section, tick_index >= 1, tick_index < micro_count)
        incoming = jnp.where(active, incoming, 0.0)
        if 0 < tick_index < micro_count:
            saved = choose(saved_ticks[tick_index - 1], saved_ticks[tick_index + 1])
        else:
            saved = saved_ticks[1 if tick_index == 0 else micro_count - 1]
        grad_inputs, gains, operands = backward_layer(incoming, weights, saved, shards, hops)
        flow_ticks.append(grad_inputs)
        if tick_index < micro_count:
            returning = from_behind(grad_inputs.astype(jnp.bfloat16), "section", -1)
        gain_sums = gains if gain_sums is None else jax.tree.map(jnp.add, gain_sums, gains)
        operand_ticks.append(operands)
    edge_operands = choose(operand_ticks[micro_count], operand_ticks[0])
    totals = reduce_gradients(operand_ticks[1:micro_count] + [edge_operands], gain_sums)
    section_outputs = mirror(
        jnp.stack(
            [choose(result_ticks[index], result_ticks[index + 1]) for index in range(micro_count)]
        )
    )
    input_grads = jnp.stack(
        [
            mirror(choose(flow_ticks[index + 1], flow_ticks[index]))
            for index in range(micro_count)
        ]
    )
    return (section_outputs[None, :, None], input_grads[None, :, None]) + tuple(
        total[None] for total in totals
    )


def solution(mesh):
    in_specs = (
        P(None, "replica", "shard", None),
        P(None, "replica", None),
        P("section", "shard"),
        P("section", "shard", None),
        P("section", "shard", None),
        P("section", "shard", None),
        P("section", "shard", None),
        P("section", "shard"),
        P("section", "shard", None),
        P("section", "shard", None),
        P("section", "shard", None),
        P(None, "replica", "shard", None),
    )
    out_specs = (
        P("section", None, "replica", "shard", None),
        P("section", None, "replica", "shard", None),
        P("section", "shard"),
        P("section", "shard", None),
        P("section", "shard", None),
        P("section", "shard", None),
        P("section", "shard", None),
        P("section", "shard"),
        P("section", "shard", None),
        P("section", "shard", None),
        P("section", "shard", None),
    )
    return jax.shard_map(body, mesh=mesh, in_specs=in_specs, out_specs=out_specs, check_vma=False)
```

```python
import functools

import jax
import jax.numpy as jnp
import numpy as np
from jax import lax
from jax.experimental import pallas as pl
from jax.experimental.pallas import tpu as pltpu
from jax.sharding import PartitionSpec as P

QH = 16
KVH = 8
HD = 96
PARTS = 4
LANES = 128


EPSILON = 1e-05
ROPE_BASE = 100000.0


def start_remote(source, target, send_sem, recv_sem, device):
    pltpu.make_async_remote_copy(
        src_ref=source,
        dst_ref=target,
        send_sem=send_sem,
        recv_sem=recv_sem,
        device_id=device,
        device_id_type=pl.DeviceIdType.MESH,
    ).start()


def wait_bytes(ref, sem):
    pltpu.make_async_copy(ref, ref, sem).wait()


def greet(shards):
    place = lax.axis_index("shard")
    member = lax.axis_index("replica")
    barrier = pltpu.get_barrier_semaphore()
    pl.semaphore_signal(barrier, inc=1, device_id={"replica": member ^ 1}, device_id_type=pl.DeviceIdType.MESH)
    pl.semaphore_signal(barrier, inc=1, device_id={"replica": member ^ 2}, device_id_type=pl.DeviceIdType.MESH)

    @pl.when(place > 0)
    def _():
        pl.semaphore_signal(barrier, inc=1, device_id={"shard": place - 1}, device_id_type=pl.DeviceIdType.MESH)

    @pl.when(place < shards - 1)
    def _():
        pl.semaphore_signal(barrier, inc=1, device_id={"shard": place + 1}, device_id_type=pl.DeviceIdType.MESH)

    pl.semaphore_wait(barrier, 2 + (place > 0).astype(jnp.int32) + (place < shards - 1).astype(jnp.int32))


def gather_kernel(shards, chunks, count, *refs):
    pieces, wholes = refs[:count], refs[count : 2 * count]
    held = refs[2 * count : 3 * count]
    (local_sem, own_send, pass_send, line_recv, x_send, x_recv, core_send, core_recv) = refs[
        3 * count :
    ]
    place = lax.axis_index("shard")
    member = lax.axis_index("replica")
    part = member % PARTS
    greet(shards)

    def loads(index):
        return pltpu.make_async_copy(pieces[index], held[index], local_sem.at[index])

    def stores(index):
        rows = pieces[index].shape[0]
        target = wholes[index].at[pl.ds(pl.multiple_of(place * rows, rows), rows), :]
        return pltpu.make_async_copy(held[index], target, local_sem.at[index])

    for index in range(count):
        loads(index).start()

    def window(chunk, block, whose):
        index, first, length = chunk
        rows = pieces[index].shape[0]
        width = pieces[index].shape[1] // PARTS
        return wholes[index].at[
            pl.ds(pl.multiple_of(block * rows + first, length), length),
            pl.ds(pl.multiple_of(whose * width, width), width),
        ]

    def own(j):
        index, first, length = chunks[j]
        width = pieces[index].shape[1] // PARTS
        source = pieces[index].at[
            pl.ds(first, length), pl.ds(pl.multiple_of(part * width, width), width)
        ]
        for slot, way in enumerate((1, -1)):
            @pl.when((place + way >= 0) & (place + way < shards))
            def _():
                start_remote(
                    source,
                    window(chunks[j], place, part),
                    own_send.at[j, slot],
                    line_recv.at[j, place],
                    {"shard": place + way},
                )

    def hop(j, k):
        for way in (1, -1):
            block = place - way * k

            @pl.when((block >= 0) & (block < shards))
            def _():
                mine = window(chunks[j], block, part)
                wait_bytes(mine, line_recv.at[j, block])

                @pl.when((place + way >= 0) & (place + way < shards))
                def _():
                    start_remote(
                        mine, mine, pass_send.at[j, block], line_recv.at[j, block], {"shard": place + way}
                    )

                start_remote(mine, mine, x_send.at[j, block], x_recv.at[j, block], {"replica": member ^ 2})
                start_remote(
                    mine, mine, core_send.at[j, block, 0], core_recv.at[j, block, 0], {"replica": member ^ 1}
                )

    def across(j, k):
        for way in (1, -1):
            block = place - way * k

            @pl.when((block >= 0) & (block < shards))
            def _():
                theirs = window(chunks[j], block, part ^ 2)
                wait_bytes(theirs, x_recv.at[j, block])
                start_remote(
                    theirs, theirs, core_send.at[j, block, 1], core_recv.at[j, block, 1], {"replica": member ^ 1}
                )

    total = len(chunks)
    for step in range(total + shards + 1):
        if step < total:
            own(step)
        if 1 <= step <= count:
            loads(step - 1).wait()
            stores(step - 1).start()
        for k in range(1, shards):
            if 0 <= step - k < total:
                hop(step - k, k)
        for k in range(1, shards):
            if 0 <= step - k - 1 < total:
                across(step - k - 1, k)

    for j in range(total):
        for slot, way in enumerate((1, -1)):
            @pl.when((place + way >= 0) & (place + way < shards))
            def _():
                wait_bytes(window(chunks[j], place, part), own_send.at[j, slot])

        for k in range(1, shards):
            for way in (1, -1):
                block = place - way * k

                @pl.when((block >= 0) & (block < shards))
                def _():
                    mine = window(chunks[j], block, part)

                    @pl.when((place + way >= 0) & (place + way < shards))
                    def _():
                        wait_bytes(mine, pass_send.at[j, block])

                    wait_bytes(mine, x_send.at[j, block])
                    for which in range(2):
                        wait_bytes(mine, core_send.at[j, block, which])
                        wait_bytes(mine, core_recv.at[j, block, which])
    for index in range(count):
        stores(index).wait()


def gather_weights(pieces, shards, pace=192 * 1024):
    chunks = []
    for index, piece in enumerate(pieces):
        rows, width = piece.shape
        cuts = 1
        while rows % (2 * cuts * 16) == 0 and rows // cuts * (width // PARTS) > pace:
            cuts *= 2
        for cut in range(cuts):
            chunks.append((index, cut * (rows // cuts), rows // cuts))
    count, total = len(pieces), len(chunks)
    dma = pltpu.SemaphoreType.DMA
    return pl.pallas_call(
        functools.partial(gather_kernel, shards, tuple(chunks), count),
        out_shape=[jax.ShapeDtypeStruct((shards * p.shape[0], p.shape[1]), p.dtype) for p in pieces],
        in_specs=[pl.BlockSpec(memory_space=pl.ANY)] * count,
        out_specs=[pl.BlockSpec(memory_space=pl.ANY)] * count,
        scratch_shapes=[pltpu.VMEM(p.shape, p.dtype) for p in pieces]
        + [
            dma((count,)),
            dma((total, 2)),
            dma((total, shards)),
            dma((total, shards)),
            dma((total, shards)),
            dma((total, shards)),
            dma((total, shards, 2)),
            dma((total, shards, 2)),
        ],
        compiler_params=pltpu.CompilerParams(collective_id=0, has_side_effects=True, vmem_limit_bytes=24 * 1024 * 1024),
        name="gather_weights",
    )(*pieces)


def add_rows(target, left, right, rows):
    step = next(size for size in (128, 64, 16) if rows % size == 0)

    def body(i, carry):
        window = pl.ds(pl.multiple_of(i * step, step), step)
        target[window, :] = (
            left[window, :].astype(jnp.float32) + right[window, :].astype(jnp.float32)
        ).astype(target.dtype)
        return carry

    lax.fori_loop(0, rows // step, body, 0)


def reduce_kernel(shards, plan, count, *refs):
    leads, trails, heights, kinds = plan
    chunks = leads + trails
    total = len(chunks)
    terms, refs = refs[:count], refs[count:]
    sums, refs = refs[:count], refs[count:]
    near, refs = refs[:count], refs[count:]
    landed, refs = refs[:total], refs[total:]
    passing, refs = refs[:total], refs[total:]
    swapped, refs = refs[: len(trails)], refs[len(trails) :]
    stages = []
    for kind in range(len(kinds)):
        stages.append(refs[:6])
        refs = refs[6:]
    trail_stage, refs = refs[:4], refs[4:]
    (load_sem, core_send, core_recv, x_send, x_recv, line_send, line_recv) = refs[:7]
    (end_local, end_x_send, end_x_recv, end_core_send, end_core_recv) = refs[7:]
    place = lax.axis_index("shard")
    member = lax.axis_index("replica")
    core = member % 2
    side = (member // 2) % 2
    x_mate = {"replica": member ^ 2}
    core_mate = {"replica": member ^ 1}
    greet(shards)

    def leading(j):
        return j < len(leads)

    def height(j):
        return heights[chunks[j][0]]

    def columns(j, whose):
        index, first, width = chunks[j]
        part = terms[index].shape[1] // PARTS
        return pl.ds(pl.multiple_of(whose * part + first, LANES), width)

    def send_near(j):
        index = chunks[j][0]
        for which in range(2):
            start_remote(
                terms[index].at[:, columns(j, (1 - core) * 2 + which)],
                near[index].at[:, columns(j, which)],
                core_send.at[j, which],
                core_recv.at[j, which],
                core_mate,
            )

    def staged(j):
        if leading(j):
            a0, a1, b0, b1, c, d = stages[kinds.index((height(j), chunks[j][2]))]
            return (b0, b1, c, d) if j % 2 else (a0, a1, c, d)
        return trail_stage

    def load_copies(j):
        index = chunks[j][0]
        whose = (1 - side, side) if leading(j) else (0, 1)
        at = staged(j)
        sem = 0 if leading(j) else 4
        sources = [terms[index].at[:, columns(j, core * 2 + w)] for w in whose]
        sources += [near[index].at[:, columns(j, w)] for w in whose]
        return [pltpu.make_async_copy(s, at[i], load_sem.at[sem + i]) for i, s in enumerate(sources)]

    def load(j):
        for which in range(2):
            wait_bytes(near[chunks[j][0]].at[:, columns(j, which)], core_recv.at[j, which])
        for copy in load_copies(j):
            copy.start()

    def near_sum(j):
        size = shards * height(j)
        at = staged(j)
        for copy in load_copies(j):
            copy.wait()
        if leading(j):
            add_rows(at[0], at[0], at[2], size)
            start_remote(at[0], landed[j], x_send.at[j], x_recv.at[j], x_mate)
            add_rows(at[1], at[1], at[3], size)
        else:
            width = chunks[j][2]
            for which in range(2):
                window = landed[j].at[:, pl.ds(which * width, width)]
                add_rows(window, at[which], at[2 + which], size)

    def x_sum(j):
        at = staged(j)
        wait_bytes(at[0], x_send.at[j])
        wait_bytes(landed[j], x_recv.at[j])
        add_rows(landed[j], landed[j], at[1], shards * height(j))

    def block(j, t):
        rows = height(j)
        return landed[j].at[pl.ds(pl.multiple_of(t * rows, rows), rows), :]

    def inside(t):
        return (t >= 0) & (t < shards)

    def line(j, hop):
        for slot, way in enumerate((1, -1)):
            t = place + way * (shards - hop)
            target = passing[j].at[slot, hop - 1]
            sems = (line_send.at[j, slot, hop - 1], line_recv.at[j, slot, hop - 1])
            ahead = {"shard": place + way}
            own = block(j, jnp.clip(t, 0, shards - 1))
            if hop == 1:

                @pl.when(inside(t))
                def _():
                    start_remote(own, target, *sems, ahead)
            else:
                arrived = passing[j].at[slot, hop - 2]

                @pl.when(inside(t) & inside(place - way))
                def _():
                    wait_bytes(arrived, line_recv.at[j, slot, hop - 2])
                    add_rows(arrived, arrived, own, height(j))
                    start_remote(arrived, target, *sems, ahead)

                @pl.when(inside(t) & jnp.logical_not(inside(place - way)))
                def _():
                    start_remote(own, target, *sems, ahead)

    def sum_window(j, whose):
        return sums[chunks[j][0]].at[:, columns(j, whose)]

    def share(j):
        width = chunks[j][2]
        for which in range(1 if leading(j) else 2):
            rows = block(j, place).at[:, pl.ds(which * width, width)]
            target = sum_window(j, core * 2 + (side if leading(j) else which))
            pltpu.make_async_copy(rows, target, end_local.at[j, which]).start()
            start_remote(rows, target, end_core_send.at[j, which], end_core_recv.at[j, which], core_mate)

    def line_end(j):
        mine = block(j, place)
        for slot, way in enumerate((1, -1)):

            @pl.when(inside(place - way))
            def _():
                arrived = passing[j].at[slot, shards - 2]
                wait_bytes(arrived, line_recv.at[j, slot, shards - 2])
                add_rows(mine, mine, arrived, height(j))

        target = sum_window(j, core * 2 + side) if leading(j) else swapped[j - len(leads)]
        start_remote(mine, target, end_x_send.at[j], end_x_recv.at[j], x_mate)
        if leading(j):
            share(j)

    def finish(j):
        if leading(j):
            theirs = sum_window(j, core * 2 + (1 - side))
            wait_bytes(theirs, end_x_recv.at[j])
            start_remote(theirs, theirs, end_core_send.at[j, 1], end_core_recv.at[j, 1], core_mate)
        else:
            mine, other = block(j, place), swapped[j - len(leads)]
            wait_bytes(mine, end_x_send.at[j])
            wait_bytes(other, end_x_recv.at[j])
            add_rows(mine, mine, other, height(j))
            share(j)

    first, second = len(leads), len(trails)
    for j in range(max(first, second)):
        if j < first:
            send_near(j)
        if j < second:
            send_near(first + j)
    load(0)
    load(first)
    for step in range(max(first + shards + 2, second + shards + 1)):
        if step < first:
            near_sum(step)
        if step < second:
            near_sum(first + step)
            if step + 1 < second:
                load(first + step + 1)
            line(first + step, 1)
        for hop in range(2, shards):
            if 0 <= step - hop < first:
                line(step - hop, hop)
            if 0 <= step - hop + 1 < second:
                line(first + step - hop + 1, hop)
        if 0 <= step - shards < first:
            line_end(step - shards)
        if 0 <= step - shards + 1 < second:
            line_end(first + step - shards + 1)
        if 0 <= step - shards - 1 < first:
            finish(step - shards - 1)
        if 0 <= step - shards < second:
            finish(first + step - shards)
        if 1 <= step <= first:
            x_sum(step - 1)
            line(step - 1, 1)
        if step + 1 < first:
            load(step + 1)

    for j in range(total):
        for which in range(2):
            wait_bytes(near[chunks[j][0]].at[:, columns(j, which)], core_send.at[j, which])
        for slot, way in enumerate((1, -1)):
            for hop in range(1, shards):

                @pl.when(inside(place + way * (shards - hop)))
                def _():
                    wait_bytes(passing[j].at[slot, hop - 1], line_send.at[j, slot, hop - 1])

        if leading(j):
            wait_bytes(sum_window(j, 0), end_x_send.at[j])
        for which in range(2):
            if which == 0 or not leading(j):
                wait_bytes(sum_window(j, 0), end_local.at[j, which])
            wait_bytes(sum_window(j, 0), end_core_send.at[j, which])
            wait_bytes(sum_window(j, 0), end_core_recv.at[j, which])


def reduce_terms(leading, trailing, shards, lead_cells=1536 * 256):
    terms = list(leading) + list(trailing)
    count = len(terms)
    heights = tuple(t.shape[0] // shards for t in terms)
    leads, trails = [], []
    for index, term in enumerate(terms):
        part = term.shape[1] // PARTS
        if index < len(leading):
            width = part
            while width % (2 * LANES) == 0 and width * term.shape[0] > lead_cells:
                width //= 2
            if width * term.shape[0] > lead_cells and width % LANES == 0:
                width = LANES
            leads += [(index, first, width) for first in range(0, part, width)]
        else:
            trails += [(index, first, LANES) for first in range(0, part, LANES)]
    kinds = []
    for index, first, width in leads:
        if (heights[index], width) not in kinds:
            kinds.append((heights[index], width))
    chunks = leads + trails
    total = len(chunks)
    bf16, dma = jnp.bfloat16, pltpu.SemaphoreType.DMA

    def rows_and_width(j):
        index, first, width = chunks[j]
        return heights[index], width if j < len(leads) else 2 * width

    scratch = []
    for j in range(total):
        rows, width = rows_and_width(j)
        scratch.append(pltpu.VMEM((shards * rows, width), bf16))
    for j in range(total):
        rows, width = rows_and_width(j)
        scratch.append(pltpu.VMEM((2, shards - 1, rows, width), bf16))
    for j in range(len(leads), total):
        rows, width = rows_and_width(j)
        scratch.append(pltpu.VMEM((rows, width), bf16))
    for rows, width in kinds:
        scratch += [pltpu.VMEM((shards * rows, width), bf16)] * 6
    scratch += [pltpu.VMEM((shards * heights[-1], LANES), bf16)] * 4
    scratch += [
        dma((8,)),
        dma((total, 2)),
        dma((total, 2)),
        dma((total,)),
        dma((total,)),
        dma((total, 2, shards - 1)),
        dma((total, 2, shards - 1)),
        dma((total, 2)),
        dma((total,)),
        dma((total,)),
        dma((total, 2)),
        dma((total, 2)),
    ]
    outs = pl.pallas_call(
        functools.partial(reduce_kernel, shards, (tuple(leads), tuple(trails), heights, tuple(kinds)), count),
        out_shape=[jax.ShapeDtypeStruct((t.shape[0] // shards, t.shape[1]), bf16) for t in terms]
        + [jax.ShapeDtypeStruct((t.shape[0], t.shape[1] // 2), bf16) for t in terms],
        in_specs=[pl.BlockSpec(memory_space=pl.ANY)] * count,
        out_specs=[pl.BlockSpec(memory_space=pl.ANY)] * (2 * count),
        scratch_shapes=scratch,
        compiler_params=pltpu.CompilerParams(
            collective_id=1, has_side_effects=True, vmem_limit_bytes=62 * 1024 * 1024
        ),
        name="reduce_terms",
    )(*terms)
    return outs[:count]


def tile_order():
    order = np.zeros(4 * HD, np.int32)
    for tile in range(3):
        for lane in range(LANES):
            upper, low = divmod(lane, LANES // 2)
            if low < HD // 2:
                head, item = tile, low
            else:
                head, item = 3, 16 * tile + low - HD // 2
            order[tile * LANES + lane] = head * HD + upper * (HD // 2) + item
    return order


def tile_matrix():
    order = tile_order()
    return (np.arange(4 * HD)[:, None] == order[None, :]).astype(np.float32)


def to_tiles(x):
    matrix = jnp.asarray(tile_matrix(), jnp.bfloat16)
    span = 4 * HD
    return jnp.concatenate(
        [
            jnp.dot(x[:, i : i + span], matrix, preferred_element_type=jnp.float32).astype(x.dtype)
            for i in range(0, x.shape[1], span)
        ],
        axis=1,
    )


def from_tiles(x):
    matrix = jnp.asarray(tile_matrix().T, jnp.bfloat16)
    span = 4 * HD
    return jnp.concatenate(
        [
            jnp.dot(x[:, i : i + span], matrix, preferred_element_type=jnp.float32).astype(x.dtype)
            for i in range(0, x.shape[1], span)
        ],
        axis=1,
    )


def rows_to_tiles(x):
    matrix = jnp.asarray(tile_matrix().T, jnp.bfloat16)
    groups = x.reshape(-1, 4 * HD, x.shape[1])
    moved = jnp.einsum("lk,gkn->gln", matrix, groups, preferred_element_type=jnp.float32)
    return moved.astype(x.dtype).reshape(x.shape)


def rope_tables(positions):
    item = tile_order() % (HD // 2)
    frequency = ROPE_BASE ** (-(jnp.asarray(item, jnp.float32) * 2.0) / HD)
    angles = positions.astype(jnp.float32)[:, None] * frequency[None, :]
    upper = (np.arange(3 * LANES) // (LANES // 2)) % 2 == 1
    sign = jnp.asarray(np.where(upper, 1.0, -1.0), jnp.float32)
    return jnp.cos(angles), jnp.sin(angles) * sign[None, :]


def spare_lanes(shape):
    return lax.broadcasted_iota(jnp.int32, shape, 1) % (LANES // 2) >= HD // 2


def last_head(tiles):
    spare = spare_lanes(tiles[0].shape)
    return sum(
        pltpu.roll(jnp.where(spare, tiles[i], 0.0), LANES - HD // 2 + 16 * i, 1) for i in range(3)
    )


def merge_heads(heads):
    spare = spare_lanes(heads[0].shape)
    return [
        jnp.where(spare, pltpu.roll(heads[3], HD // 2 - 16 * i, 1), heads[i])
        for i in range(3)
    ]


def tile(ref, index):
    return ref[:, index * LANES : (index + 1) * LANES]


def put(ref, index, value):
    ref[:, index * LANES : (index + 1) * LANES] = value


def turn(value, cosine, sine):
    return value * cosine + pltpu.roll(value, LANES // 2, 1) * sine


def key_tile(group, i):
    return group * 6 + i


def value_tile(group, i):
    return group * 6 + 3 + i


def fill_bias(bias, own_segment, key_segments, rows):
    size = key_segments.shape[1]
    same = own_segment[...] == key_segments[...]
    query = lax.broadcasted_iota(jnp.int32, (rows, size), 0)
    key = lax.broadcasted_iota(jnp.int32, (rows, size), 1)
    bias[...] = jnp.where(same & ((key >= rows) | (key <= query)), 0.0, -1e30)


def inside(place, shards):
    return (place >= 0) & (place < shards)


def line_place(shards):
    place = lax.axis_index("shard")
    mirrored = lax.axis_index("replica") % 2 == 1
    return jnp.where(mirrored, shards - 1 - place, place)


def line_device(place, shards):
    mirrored = lax.axis_index("replica") % 2 == 1
    return {"shard": jnp.where(mirrored, shards - 1 - place, place)}


def greet_line(shards, way):
    place = line_place(shards)
    barrier = pltpu.get_barrier_semaphore()

    @pl.when(inside(place - way, shards))
    def _():
        pl.semaphore_signal(
            barrier,
            inc=1,
            device_id=line_device(place - way, shards),
            device_id_type=pl.DeviceIdType.MESH,
        )

    @pl.when(inside(place + way, shards))
    def _():
        pl.semaphore_wait(barrier, 1)


def dot(left, right, dims):
    return lax.dot_general(left, right, (dims, ((), ())), preferred_element_type=jnp.float32)


NT = ((1,), (1,))
NN = ((1,), (0,))
TN = ((0,), (0,))


def attend_kernel(
    shards, hops, rows, raw, cosine, sine, own_segment, key_segments,
    queries, window, attended, log_total,
    held, last, bias, query_heads, send_sem, recv_sem, keep_sem,
):
    place = line_place(shards)
    greet_line(shards, 1)

    def slot(distance):
        return held.at[pl.ds(distance * rows, rows), :]

    first_key, first_value = QH * 3 // 4, QH * 3 // 4 + KVH * 3 // 4
    for group in range(KVH // 4):
        for i in range(3):
            value = turn(tile(raw, first_key + group * 3 + i), tile(cosine, i), tile(sine, i))
            held[pl.ds(0, rows), key_tile(group, i) * LANES : (key_tile(group, i) + 1) * LANES] = value.astype(
                jnp.bfloat16
            )
            value = tile(raw, first_value + group * 3 + i)
            held[pl.ds(0, rows), value_tile(group, i) * LANES : (value_tile(group, i) + 1) * LANES] = (
                value.astype(jnp.bfloat16)
            )

    def send(distance):
        @pl.when((place + 1 < shards) & (place - distance >= 0))
        def _():
            start_remote(
                slot(distance),
                slot(distance + 1),
                send_sem.at[distance],
                recv_sem.at[distance],
                line_device(place + 1, shards),
            )

    send(0)
    fill_bias(bias, own_segment, key_segments, rows)
    for group in range(QH // 4):
        tiles = []
        for i in range(3):
            value = turn(tile(raw, group * 3 + i), tile(cosine, i), tile(sine, i))
            put(queries, group * 3 + i, value.astype(jnp.bfloat16))
            tiles.append(value)
        spare = spare_lanes(tiles[0].shape)
        for i in range(3):
            query_heads[group * 4 + i] = jnp.where(spare, 0.0, tiles[i]).astype(jnp.bfloat16)
        query_heads[group * 4 + 3] = last_head(tiles).astype(jnp.bfloat16)

    def receive(distance):
        @pl.when(place - distance >= 0)
        def _():
            wait_bytes(slot(distance), recv_sem.at[distance - 1])

        @pl.when(place - distance < 0)
        def _():
            held[pl.ds(distance * rows, rows), :] = jnp.zeros((rows, held.shape[1]), held.dtype)

        if distance < hops:
            send(distance)

    def scores_values(head, first, size):
        wide, item = divmod(head // 2, 4)
        span = pl.ds(first, size)
        if item == 3:
            keys, values = last[wide * 2, span], last[wide * 2 + 1, span]
        else:
            at = [spot(wide, item) * LANES for spot in (key_tile, value_tile)]
            keys, values = (held[span, lane : lane + LANES] for lane in at)
        return dot(query_heads[head], keys, NT) * HD ** (-0.5) + bias[:, first : first + size], values

    def fill_last(first, size):
        for wide in range(KVH // 4):
            for which, at in enumerate((key_tile(wide, 0), value_tile(wide, 0))):
                tiles = [
                    held[pl.ds(first, size), (at + i) * LANES : (at + i + 1) * LANES].astype(jnp.float32)
                    for i in range(3)
                ]
                last[wide * 2 + which, pl.ds(first, size)] = last_head(tiles).astype(jnp.bfloat16)

    for distance in range(1, hops):
        receive(distance)
    near = hops * rows
    fill_last(0, near)
    state = []
    for head in range(QH):
        scores, values = scores_values(head, 0, near)
        top = jnp.max(scores, axis=1, keepdims=True)
        exponent = jnp.exp(scores - top)
        total = jnp.sum(exponent, axis=1, keepdims=True)
        state.append((top, total, dot(exponent.astype(jnp.bfloat16), values, NN)))
    receive(hops)
    keep = pltpu.make_async_copy(held, window, keep_sem)
    keep.start()
    fill_last(near, rows)
    lane = lax.broadcasted_iota(jnp.int32, (rows, LANES), 1)
    totals = jnp.zeros((rows, LANES), jnp.float32)
    for group in range(QH // 4):
        outs = []
        for head in range(group * 4, group * 4 + 4):
            before, total, out = state[head]
            scores, values = scores_values(head, near, rows)
            top = jnp.maximum(before, jnp.max(scores, axis=1, keepdims=True))
            exponent = jnp.exp(scores - top)
            shrink = jnp.exp(before - top)
            total = total * shrink + jnp.sum(exponent, axis=1, keepdims=True)
            out = out * shrink + dot(exponent.astype(jnp.bfloat16), values, NN)
            outs.append(out * (1.0 / total))
            totals = jnp.where(lane == head, top + jnp.log(total), totals)
        for i, merged in enumerate(merge_heads(outs)):
            put(attended, group * 3 + i, merged.astype(jnp.bfloat16))
    log_total[...] = totals
    keep.wait()
    for distance in range(hops):
        @pl.when((place + 1 < shards) & (place - distance >= 0))
        def _():
            wait_bytes(slot(distance), send_sem.at[distance])


def line_hops(shards, rows, longest):
    return min(shards - 1, -(-(longest - 1) // rows))


def attend(raw, cosine, sine, own_segment, key_segments, shards, hops):
    rows = raw.shape[0]
    width = QH * HD
    size = (hops + 1) * rows
    bf16, f32, dma = jnp.bfloat16, jnp.float32, pltpu.SemaphoreType.DMA
    vmem = pl.BlockSpec(memory_space=pltpu.VMEM)
    return pl.pallas_call(
        functools.partial(attend_kernel, shards, hops, rows),
        out_shape=[
            jax.ShapeDtypeStruct((rows, width), bf16),
            jax.ShapeDtypeStruct((size, width), bf16),
            jax.ShapeDtypeStruct((rows, width), bf16),
            jax.ShapeDtypeStruct((rows, LANES), f32),
        ],
        in_specs=[vmem] * 5,
        out_specs=[vmem, pl.BlockSpec(memory_space=pl.ANY), vmem, vmem],
        scratch_shapes=[
            pltpu.VMEM((size, width), bf16),
            pltpu.VMEM((KVH // 2, size, LANES), bf16),
            pltpu.VMEM((rows, size), f32),
            pltpu.VMEM((QH, rows, LANES), bf16),
            dma((hops,)),
            dma((hops,)),
            dma,
        ],
        compiler_params=pltpu.CompilerParams(
            collective_id=2, has_side_effects=True, vmem_limit_bytes=62 * 1024 * 1024
        ),
        name="attend",
    )(raw, cosine, sine, own_segment, key_segments)


def attend_back_kernel(
    shards, hops, rows, queries, window, log_total, grads, cosine, sine, own_segment, key_segments,
    lows,
    bias, own_part, parts, landing, query_grads, send_sem, recv_sem,
):
    place = line_place(shards)
    greet_line(shards, -1)
    fill_bias(bias, own_segment, key_segments, rows)
    span = 6 * LANES

    def heads_of(ref, group):
        tiles = [tile(ref, group * 3 + i).astype(jnp.float32) for i in range(3)]
        spare = spare_lanes(tiles[0].shape)
        heads = [jnp.where(spare, 0.0, t).astype(jnp.bfloat16) for t in tiles]
        return heads + [last_head(tiles).astype(jnp.bfloat16)]

    def column(head):
        lane = lax.broadcasted_iota(jnp.int32, (rows, LANES), 1)
        return jnp.sum(jnp.where(lane == head, log_total[...], 0.0), axis=1, keepdims=True)

    def wide_group(wide):
        heads = heads_of(queries, 2 * wide) + heads_of(queries, 2 * wide + 1)
        grad_heads = heads_of(grads, 2 * wide) + heads_of(grads, 2 * wide + 1)
        key_grads, value_grads = [], []
        query_out = []
        key_tiles = [tile(window, key_tile(wide, i)) for i in range(3)]
        value_tiles = [tile(window, value_tile(wide, i)) for i in range(3)]
        key_tiles.append(last_head([t.astype(jnp.float32) for t in key_tiles]).astype(jnp.bfloat16))
        value_tiles.append(last_head([t.astype(jnp.float32) for t in value_tiles]).astype(jnp.bfloat16))
        for item in range(4):
            keys, values = key_tiles[item], value_tiles[item]
            key_grad = value_grad = None
            for one in (2 * item, 2 * item + 1):
                query, grad = heads[one], grad_heads[one]
                scores = dot(query, keys, NT) * HD ** (-0.5) + bias[...]
                probs = jnp.exp(scores - column(wide * 8 + one))
                grad_probs = dot(grad, values, NT)
                along = jnp.sum(probs * grad_probs, axis=1, keepdims=True)
                grad_scores = (probs * (grad_probs - along)).astype(jnp.bfloat16)
                query_out.append(dot(grad_scores, keys, NN) * HD ** (-0.5))
                key_one = dot(grad_scores, query, TN)
                value_one = dot(probs.astype(jnp.bfloat16), grad, TN)
                key_grad = key_one if key_grad is None else key_grad + key_one
                value_grad = value_one if value_grad is None else value_grad + value_one
            key_grads.append(key_grad * HD ** (-0.5))
            value_grads.append(value_grad)
        for which, grads_of in enumerate((key_grads, value_grads)):
            for i, merged in enumerate(merge_heads(grads_of)):
                at = which * 3 + i
                own_part[:, (wide * 6 + at) * LANES : (wide * 6 + at + 1) * LANES] = merged[:rows]
                for distance in range(1, hops + 1):
                    parts[wide, distance - 1, :, at * LANES : (at + 1) * LANES] = merged[
                        distance * rows : (distance + 1) * rows
                    ].astype(jnp.bfloat16)
        for half in range(2):
            for i, merged in enumerate(merge_heads(query_out[half * 4 : half * 4 + 4])):
                put(query_grads, (2 * wide + half) * 3 + i, merged)

    def step(wide, k):
        distance = hops - k + 1
        source = parts.at[wide, distance - 1]
        target = landing.at[wide, k - 1]
        sems = (send_sem.at[wide, k - 1], recv_sem.at[wide, k - 1])

        @pl.when(place - distance >= 0)
        def _():
            if k > 1:
                @pl.when(place + 1 < shards)
                def _():
                    arrived = landing.at[wide, k - 2]
                    wait_bytes(arrived, recv_sem.at[wide, k - 2])
                    source[...] = (
                        source[...].astype(jnp.float32) + arrived[...].astype(jnp.float32)
                    ).astype(jnp.bfloat16)

            start_remote(source, target, *sems, line_device(place - 1, shards))

    def finish(wide):
        @pl.when(place + 1 < shards)
        def _():
            arrived = landing.at[wide, hops - 1]
            wait_bytes(arrived, recv_sem.at[wide, hops - 1])
            own_part[:, wide * span : (wide + 1) * span] += arrived[...].astype(jnp.float32)

        first_key, first_value = QH * 3 // 4, QH * 3 // 4 + KVH * 3 // 4
        for i in range(3):
            value = turn(tile(own_part, key_tile(wide, i)), tile(cosine, i), -tile(sine, i))
            put(lows, first_key + wide * 3 + i, value.astype(jnp.bfloat16))
            put(lows, first_value + wide * 3 + i, tile(own_part, value_tile(wide, i)).astype(jnp.bfloat16))

    for wide in range(KVH // 4):
        wide_group(wide)
        step(wide, 1)
    for group in range(QH // 4):
        for i in range(3):
            value = turn(tile(query_grads, group * 3 + i), tile(cosine, i), -tile(sine, i))
            put(lows, group * 3 + i, value.astype(jnp.bfloat16))
    for k in range(2, hops + 1):
        for wide in range(KVH // 4):
            step(wide, k)
    for wide in range(KVH // 4):
        finish(wide)
    for wide in range(KVH // 4):
        for k in range(1, hops + 1):
            @pl.when(place - (hops - k + 1) >= 0)
            def _():
                wait_bytes(parts.at[wide, hops - k], send_sem.at[wide, k - 1])


def attend_back(queries, window, log_total, grads, cosine, sine, own_segment, key_segments, shards, hops):
    rows = queries.shape[0]
    width = QH * HD
    size = (hops + 1) * rows
    bf16, f32, dma = jnp.bfloat16, jnp.float32, pltpu.SemaphoreType.DMA
    vmem = pl.BlockSpec(memory_space=pltpu.VMEM)
    wides = KVH // 4
    return pl.pallas_call(
        functools.partial(attend_back_kernel, shards, hops, rows),
        out_shape=jax.ShapeDtypeStruct((rows, 2 * width), bf16),
        in_specs=[vmem] * 8,
        out_specs=vmem,
        scratch_shapes=[
            pltpu.VMEM((rows, size), f32),
            pltpu.VMEM((rows, width), f32),
            pltpu.VMEM((wides, hops, rows, 6 * LANES), bf16),
            pltpu.VMEM((wides, hops, rows, 6 * LANES), bf16),
            pltpu.VMEM((rows, width), f32),
            dma((wides, hops)),
            dma((wides, hops)),
        ],
        compiler_params=pltpu.CompilerParams(
            collective_id=3, has_side_effects=True, vmem_limit_bytes=62 * 1024 * 1024
        ),
        name="attend_back",
    )(queries, window, log_total, grads, cosine, sine, own_segment, key_segments)


def sigmoid(value):
    return 1.0 / (1.0 + jnp.exp(-value))


def feed_kernel(
    inputs,
    attended,
    w_out,
    gain,
    w_gate,
    w_up,
    w_down,
    middle,
    normed,
    gate,
    up,
    hidden,
    result,
    total,
):
    step = pl.program_id(0)

    @pl.when(step == 0)
    def _():
        value = inputs[...] + dot(attended[...], w_out[...], NN)
        middle[...] = value
        recip = lax.rsqrt(jnp.mean(value * value, axis=-1, keepdims=True) + EPSILON)
        normed[...] = (value * recip * gain[...]).astype(jnp.bfloat16)
        total[...] = value

    gate_value = dot(normed[...], w_gate[...], NN)
    up_value = dot(normed[...], w_up[...], NN)
    low = (gate_value * sigmoid(gate_value) * up_value).astype(jnp.bfloat16)
    gate[...] = gate_value.astype(jnp.bfloat16)
    up[...] = up_value.astype(jnp.bfloat16)
    hidden[...] = low
    total[...] += dot(low, w_down[...], NN)

    @pl.when(step == pl.num_programs(0) - 1)
    def _():
        result[...] = total[...].astype(jnp.bfloat16)


def whole(shape):
    return pl.BlockSpec(shape, lambda i: (0, 0), pipeline_mode=pl.Buffered(1))


def feed_forward(inputs, attended, w_out, gain, w_gate, w_up, w_down, block=1024):
    rows, width = inputs.shape
    units = w_gate.shape[1]
    f32, bf16 = jnp.float32, jnp.bfloat16
    columns = pl.BlockSpec((rows, block), lambda i: (0, i))
    weight = pl.BlockSpec((width, block), lambda i: (0, i))
    return pl.pallas_call(
        feed_kernel,
        grid=(units // block,),
        out_shape=[
            jax.ShapeDtypeStruct((rows, width), f32),
            jax.ShapeDtypeStruct((rows, width), bf16),
            jax.ShapeDtypeStruct((rows, units), bf16),
            jax.ShapeDtypeStruct((rows, units), bf16),
            jax.ShapeDtypeStruct((rows, units), bf16),
            jax.ShapeDtypeStruct((rows, width), bf16),
        ],
        in_specs=[
            whole((rows, width)),
            whole(attended.shape),
            whole(w_out.shape),
            whole((1, width)),
            weight,
            weight,
            pl.BlockSpec((block, width), lambda i: (i, 0)),
        ],
        out_specs=[
            whole((rows, width)),
            whole((rows, width)),
            columns,
            columns,
            columns,
            whole((rows, width)),
        ],
        scratch_shapes=[pltpu.VMEM((rows, width), f32)],
        compiler_params=pltpu.CompilerParams(vmem_limit_bytes=62 * 1024 * 1024),
        cost_estimate=pl.CostEstimate(
            flops=6 * rows * width * units + 2 * rows * width * width,
            bytes_accessed=6 * width * units + 2 * width * width + 6 * rows * units + 14 * rows * width,
            transcendentals=rows * units,
        ),
        name="feed_forward",
    )(inputs, attended, w_out, gain[None], w_gate, w_up, w_down)


def feed_back_kernel(
    grads,
    middle,
    gain,
    w_out,
    gate,
    up,
    w_gate,
    w_up,
    w_down,
    gate_low,
    up_low,
    grad_middle,
    attn_grad,
    grad_attended,
    gain_grad,
    branch,
    total,
):
    step = pl.program_id(0)

    @pl.when(step == 0)
    def _():
        branch[...] = grads[...].astype(jnp.bfloat16)
        total[...] = jnp.zeros_like(total)

    grad_hidden = dot(branch[...], w_down[...], NT)
    gate_value, up_value = gate[...].astype(jnp.float32), up[...].astype(jnp.float32)
    share = sigmoid(gate_value)
    one = (grad_hidden * up_value * (share * (1.0 + gate_value * (1.0 - share)))).astype(jnp.bfloat16)
    two = (grad_hidden * (gate_value * share)).astype(jnp.bfloat16)
    gate_low[...] = one
    up_low[...] = two
    total[...] += dot(one, w_gate[...], NT) + dot(two, w_up[...], NT)

    @pl.when(step == pl.num_programs(0) - 1)
    def _():
        value = middle[...]
        recip = lax.rsqrt(jnp.mean(value * value, axis=-1, keepdims=True) + EPSILON)
        scaled = value * recip
        grad = total[...]
        gain_grad[...] = jnp.sum(grad * scaled, axis=0, keepdims=True)
        grad = grad * gain[...]
        grad = grads[...] + recip * (
            grad - scaled * jnp.mean(grad * scaled, axis=-1, keepdims=True)
        )
        grad_middle[...] = grad
        attn_grad[...] = grad.astype(jnp.bfloat16)
        grad_attended[...] = dot(attn_grad[...], w_out[...], NT).astype(jnp.bfloat16)


def feed_back(grads, middle, gain, w_out, gate, up, w_gate, w_up, w_down, block=1024):
    rows, width = grads.shape
    units = w_gate.shape[1]
    f32, bf16 = jnp.float32, jnp.bfloat16
    columns = pl.BlockSpec((rows, block), lambda i: (0, i))
    weight = pl.BlockSpec((width, block), lambda i: (0, i))
    return pl.pallas_call(
        feed_back_kernel,
        grid=(units // block,),
        out_shape=[
            jax.ShapeDtypeStruct((rows, units), bf16),
            jax.ShapeDtypeStruct((rows, units), bf16),
            jax.ShapeDtypeStruct((rows, width), f32),
            jax.ShapeDtypeStruct((rows, width), bf16),
            jax.ShapeDtypeStruct((rows, w_out.shape[0]), bf16),
            jax.ShapeDtypeStruct((1, width), f32),
        ],
        in_specs=[
            whole((rows, width)),
            whole((rows, width)),
            whole((1, width)),
            whole(w_out.shape),
            columns,
            columns,
            weight,
            weight,
            pl.BlockSpec((block, width), lambda i: (i, 0)),
        ],
        out_specs=[
            columns,
            columns,
            whole((rows, width)),
            whole((rows, width)),
            whole((rows, w_out.shape[0])),
            whole((1, width)),
        ],
        scratch_shapes=[pltpu.VMEM((rows, width), bf16), pltpu.VMEM((rows, width), f32)],
        compiler_params=pltpu.CompilerParams(vmem_limit_bytes=62 * 1024 * 1024),
        cost_estimate=pl.CostEstimate(
            flops=6 * rows * width * units + 2 * rows * width * width,
            bytes_accessed=6 * width * units + 2 * width * width + 8 * rows * units + 16 * rows * width,
            transcendentals=rows * units,
        ),
        name="feed_back",
    )(grads, middle, gain[None], w_out, gate, up, w_gate, w_up, w_down)


def from_behind(x, axis, by):
    devices = lax.axis_size(axis)
    pairs = [(i, i + by) for i in range(devices) if 0 <= i + by < devices]
    return lax.ppermute(x, axis, pairs)


def swap(x, bit):
    members = lax.axis_size("replica")
    return lax.ppermute(x, "replica", [(r, r ^ (1 << bit)) for r in range(members)])


def mirror(x):
    members, shards = lax.axis_size("replica"), lax.axis_size("shard")
    pairs = [
        (r * shards + s, r * shards + shards - 1 - s)
        for r in range(1, members, 2)
        for s in range(shards)
        if 2 * s != shards - 1
    ]
    moved = lax.ppermute(x, ("replica", "shard"), pairs)
    return jnp.where(lax.axis_index("replica") % 2 == 1, moved, x)


def gain_width(rows):
    return -(-2 * rows // (PARTS * LANES)) * PARTS * LANES


def gather_layer(pieces):
    norm_attn, w_query, w_key, w_value, w_out, norm_ffn, w_gate, w_up, w_down = pieces
    rows = norm_attn.shape[0]
    shards = lax.axis_size("shard")
    gains = jnp.concatenate([norm_attn, norm_ffn])
    gains = jnp.pad(gains[None], ((0, 15), (0, gain_width(rows) - 2 * rows)))
    w_qkv = to_tiles(jnp.concatenate([w_query, w_key, w_value], axis=1))
    w_qkv, w_out, w_gate, w_up, w_down, gains = gather_weights(
        [w_qkv, w_out, w_gate, w_up, w_down, gains], shards
    )
    gains = gains.reshape(shards, 16, -1)[:, 0].astype(jnp.float32)
    norm_attn = gains[:, :rows].reshape(-1)
    norm_ffn = gains[:, rows : 2 * rows].reshape(-1)
    return norm_attn, w_qkv, rows_to_tiles(w_out), norm_ffn, w_gate, w_up, w_down


def sequence_tables(segment, rows, hops):
    place = line_place(lax.axis_size("shard"))
    local_segment = lax.dynamic_slice_in_dim(segment, place * rows, rows)
    starts = jnp.sum((segment[None, :] < local_segment[:, None]).astype(jnp.int32), axis=1)
    cosine, sine = rope_tables(place * rows + jnp.arange(rows, dtype=jnp.int32) - starts)
    padded = jnp.concatenate([jnp.full((hops * rows,), -1, jnp.int32), segment])
    key_segments = jnp.concatenate(
        [lax.dynamic_slice_in_dim(padded, (place + hops - d) * rows, rows) for d in range(hops + 1)]
    )
    return cosine, sine, local_segment[:, None], key_segments[None, :]


def matmul(left, right):
    return jnp.dot(left, right, preferred_element_type=jnp.float32)


def matmul_back(left, right):
    return jnp.einsum("tq,dq->td", left, right, preferred_element_type=jnp.float32)


def row_product(left, right):
    return jnp.einsum("td,tq->dq", left, right, preferred_element_type=jnp.float32)


def forward_layer(inputs, weights, tables, shards, hops):
    norm_attn, w_qkv, w_out, norm_ffn, w_gate, w_up, w_down = weights
    recip_one = lax.rsqrt(jnp.mean(inputs * inputs, axis=-1, keepdims=True) + EPSILON)
    scaled = inputs * recip_one
    normed = (scaled * norm_attn).astype(jnp.bfloat16)
    queries, window, attended, log_total = attend(matmul(normed, w_qkv), *tables, shards, hops)
    middle, normed_mid, gate, up, hidden, result = feed_forward(
        inputs, attended, w_out, norm_ffn, w_gate, w_up, w_down
    )
    saved = (
        scaled,
        recip_one,
        normed,
        queries,
        window,
        log_total,
        attended,
        middle,
        normed_mid,
        gate,
        up,
        hidden,
        tables,
    )
    return (result, saved)


def backward_layer(grad_result, weights, saved, shards, hops):
    norm_attn, w_qkv, w_out, norm_ffn, w_gate, w_up, w_down = weights
    (
        scaled,
        recip_one,
        normed,
        queries,
        window,
        log_total,
        attended,
        middle,
        normed_mid,
        gate,
        up,
        hidden,
        tables,
    ) = saved
    branch_grad = grad_result.astype(jnp.bfloat16)
    gate_low, up_low, grad_middle, attn_grad, grad_attended, grad_norm_ffn = feed_back(
        grad_result, middle, norm_ffn, w_out, gate, up, w_gate, w_up, w_down
    )
    qkv_low = attend_back(queries, window, log_total, grad_attended, *tables, shards, hops)
    grad_normed = matmul_back(qkv_low, w_qkv)
    grad_norm_attn = jnp.sum(grad_normed * scaled, axis=0)
    grad_scaled = grad_normed * norm_attn
    grad_inputs = grad_middle + recip_one * (
        grad_scaled - scaled * jnp.mean(grad_scaled * scaled, axis=-1, keepdims=True)
    )
    operands = (
        normed,
        qkv_low,
        attended,
        attn_grad,
        normed_mid,
        gate_low,
        up_low,
        hidden,
        branch_grad,
    )
    return (grad_inputs, (grad_norm_attn, grad_norm_ffn[0]), operands)


def reduce_gradients(operand_pairs, gains, last_grads):
    (
        normed,
        qkv_low,
        attended,
        attn_grad,
        normed_mid,
        gate_low,
        up_low,
        hidden,
        branch_grad,
    ) = (jnp.concatenate(parts, axis=0) for parts in zip(*operand_pairs))
    shards = lax.axis_size("shard")
    rows = gains[0].shape[0] // shards

    def product(left, right):
        return row_product(left, right).astype(jnp.bfloat16)

    gain_term = jnp.stack([gain.reshape(shards, rows) for gain in gains], axis=1)
    gain_term = gain_term.reshape(shards, 1, 2 * rows).astype(jnp.bfloat16)
    gain_term = jnp.pad(gain_term, ((0, 0), (0, 15), (0, gain_width(rows) - 2 * rows)))
    gain_term, last_grads = lax.optimization_barrier((gain_term, last_grads))
    cut = up_low.shape[1] // 4 * 3
    leading = [
        product(hidden, branch_grad),
        product(normed_mid, gate_low),
        product(normed_mid, up_low[:, :cut]),
        gain_term.reshape(shards * 16, -1),
    ]
    trailing = [
        product(normed_mid, up_low[:, cut:]),
        product(from_tiles(attended), attn_grad),
        product(normed, from_tiles(qkv_low)),
    ]
    totals = [total.astype(jnp.float32) for total in reduce_terms(leading, trailing, shards)]
    members = lax.axis_size("replica")
    for bit in range(PARTS.bit_length() - 1, members.bit_length() - 1):
        totals = [total + swap(total, bit) for total in totals]
    down, gate, up, own_gains, up_rest, out, qkv = totals
    up = jnp.concatenate([up, up_rest], axis=1)
    return (
        own_gains[0, :rows],
        qkv[:, : QH * HD],
        qkv[:, QH * HD : (QH + KVH) * HD],
        qkv[:, (QH + KVH) * HD :],
        out,
        own_gains[0, rows : 2 * rows],
        gate,
        up,
        down,
    ), last_grads


def body(
    tokens,
    segments,
    norm_attn,
    w_query,
    w_key,
    w_value,
    w_out,
    norm_ffn,
    w_gate,
    w_up,
    w_down,
    cotangent,
):
    micro_count = tokens.shape[0]
    row_count = tokens.shape[2]
    width = tokens.shape[3]
    seq_length = segments.shape[2]
    shards = lax.axis_size("shard")
    hops = line_hops(shards, row_count, seq_length // 2)
    first_section = lax.axis_index("section") == 0

    def choose(early, late):
        return jax.tree.map(lambda a, b: jnp.where(first_section, a, b), early, late)

    weights = gather_layer(
        (
            norm_attn[0],
            w_query[0],
            w_key[0],
            w_value[0],
            w_out[0],
            norm_ffn[0],
            w_gate[0],
            w_up[0],
            w_down[0],
        )
    )
    later, gathered = lax.optimization_barrier((tokens[1:], weights[0]))
    weights = (gathered,) + weights[1:]
    tokens = jnp.concatenate([mirror(tokens[:1]), mirror(later)]) if micro_count > 1 else mirror(tokens)
    all_tables = [sequence_tables(segments[m, 0], row_count, hops) for m in range(micro_count)]
    saved_ticks = []
    result_ticks = []
    later_grads = []
    arriving = jnp.zeros((row_count, width), jnp.bfloat16)
    for tick_index in range(micro_count + 1):
        own_input = tokens[min(tick_index, micro_count - 1), 0].astype(jnp.float32)
        layer_input = jnp.where(first_section, own_input, arriving.astype(jnp.float32))
        if tick_index > 0:
            layer_input, later_grads[-1] = lax.optimization_barrier((layer_input, later_grads[-1]))
        tables = choose(
            all_tables[min(tick_index, micro_count - 1)], all_tables[max(tick_index - 1, 0)]
        )
        result_low, saved = forward_layer(layer_input, weights, tables, shards, hops)
        result_ticks.append(result_low)
        saved_ticks.append(saved)
        if tick_index < micro_count:
            grad, attended = lax.optimization_barrier((cotangent[tick_index, 0], saved[6]))
            later_grads.append(mirror(grad))
        if tick_index < micro_count:
            arriving = from_behind(result_low, "section", 1)
    flow_ticks = []
    gain_sums = None
    operand_ticks = []
    returning = jnp.zeros((row_count, width), jnp.bfloat16)
    for tick_index in range(micro_count + 1):
        later_grad = later_grads[min(tick_index, micro_count - 1)].astype(jnp.float32)
        incoming = jnp.where(first_section, returning.astype(jnp.float32), later_grad)
        active = jnp.where(first_section, tick_index >= 1, tick_index < micro_count)
        incoming = jnp.where(active, incoming, 0.0)
        if 0 < tick_index < micro_count:
            saved = choose(saved_ticks[tick_index - 1], saved_ticks[tick_index + 1])
        else:
            saved = saved_ticks[1 if tick_index == 0 else micro_count - 1]
        grad_inputs, gains, operands = backward_layer(incoming, weights, saved, shards, hops)
        flow_ticks.append(grad_inputs)
        if tick_index < micro_count:
            returning = from_behind(grad_inputs.astype(jnp.bfloat16), "section", -1)
        gain_sums = gains if gain_sums is None else jax.tree.map(jnp.add, gain_sums, gains)
        operand_ticks.append(operands)
    edge_operands = choose(operand_ticks[micro_count], operand_ticks[0])
    flows = [mirror(choose(flow_ticks[m + 1], flow_ticks[m])) for m in range(micro_count)]
    totals, flows[-1] = reduce_gradients(
        operand_ticks[1:micro_count] + [edge_operands], gain_sums, flows[-1]
    )
    section_outputs = mirror(
        jnp.stack(
            [choose(result_ticks[index], result_ticks[index + 1]) for index in range(micro_count)]
        )
    )
    input_grads = jnp.stack(flows)
    return (section_outputs[None, :, None], input_grads[None, :, None]) + tuple(
        total[None] for total in totals
    )


def solution(mesh):
    in_specs = (
        P(None, "replica", "shard", None),
        P(None, "replica", None),
        P("section", "shard"),
        P("section", "shard", None),
        P("section", "shard", None),
        P("section", "shard", None),
        P("section", "shard", None),
        P("section", "shard"),
        P("section", "shard", None),
        P("section", "shard", None),
        P("section", "shard", None),
        P(None, "replica", "shard", None),
    )
    out_specs = (
        P("section", None, "replica", "shard", None),
        P("section", None, "replica", "shard", None),
        P("section", "shard"),
        P("section", "shard", None),
        P("section", "shard", None),
        P("section", "shard", None),
        P("section", "shard", None),
        P("section", "shard"),
        P("section", "shard", None),
        P("section", "shard", None),
        P("section", "shard", None),
    )
    return jax.shard_map(body, mesh=mesh, in_specs=in_specs, out_specs=out_specs, check_vma=False)
```

```python
import functools

import jax
import jax.numpy as jnp
import numpy as np
from jax import lax
from jax.experimental import pallas as pl
from jax.experimental.pallas import tpu as pltpu
from jax.sharding import PartitionSpec as P

QH = 16
KVH = 8
HD = 96
PARTS = 4
LANES = 128


EPSILON = 1e-05
ROPE_BASE = 100000.0


def start_remote(source, target, send_sem, recv_sem, device):
    pltpu.make_async_remote_copy(
        src_ref=source,
        dst_ref=target,
        send_sem=send_sem,
        recv_sem=recv_sem,
        device_id=device,
        device_id_type=pl.DeviceIdType.MESH,
    ).start()


def wait_bytes(ref, sem):
    pltpu.make_async_copy(ref, ref, sem).wait()


def greet(shards):
    place = lax.axis_index("shard")
    member = lax.axis_index("replica")
    barrier = pltpu.get_barrier_semaphore()
    pl.semaphore_signal(barrier, inc=1, device_id={"replica": member ^ 1}, device_id_type=pl.DeviceIdType.MESH)
    pl.semaphore_signal(barrier, inc=1, device_id={"replica": member ^ 2}, device_id_type=pl.DeviceIdType.MESH)

    @pl.when(place > 0)
    def _():
        pl.semaphore_signal(barrier, inc=1, device_id={"shard": place - 1}, device_id_type=pl.DeviceIdType.MESH)

    @pl.when(place < shards - 1)
    def _():
        pl.semaphore_signal(barrier, inc=1, device_id={"shard": place + 1}, device_id_type=pl.DeviceIdType.MESH)

    pl.semaphore_wait(barrier, 2 + (place > 0).astype(jnp.int32) + (place < shards - 1).astype(jnp.int32))


def gather_kernel(shards, chunks, count, turns, matrix, *refs):
    pieces, wholes = refs[:count], refs[count : 2 * count]
    held = refs[2 * count : 3 * count]
    (local_sem, own_send, pass_send, line_recv, x_send, x_recv, core_send, core_recv) = refs[
        3 * count :
    ]
    place = lax.axis_index("shard")
    member = lax.axis_index("replica")
    part = member % PARTS
    greet(shards)

    def loads(index):
        return pltpu.make_async_copy(pieces[index], held[index], local_sem.at[index])

    def stores(index):
        rows = pieces[index].shape[0]
        target = wholes[index].at[pl.ds(pl.multiple_of(place * rows, rows), rows), :]
        return pltpu.make_async_copy(held[index], target, local_sem.at[index])

    for index in range(count):
        loads(index).start()

    def window(chunk, block, whose):
        index, first, length = chunk
        rows = pieces[index].shape[0]
        width = pieces[index].shape[1] // PARTS
        return wholes[index].at[
            pl.ds(pl.multiple_of(block * rows + first, length), length),
            pl.ds(pl.multiple_of(whose * width, width), width),
        ]

    def own(j):
        index, first, length = chunks[j]
        width = pieces[index].shape[1] // PARTS
        source = (held if turns[index] else pieces)[index].at[
            pl.ds(first, length), pl.ds(pl.multiple_of(part * width, width), width)
        ]
        for slot, way in enumerate((1, -1)):
            @pl.when((place + way >= 0) & (place + way < shards))
            def _():
                start_remote(
                    source,
                    window(chunks[j], place, part),
                    own_send.at[j, slot],
                    line_recv.at[j, place],
                    {"shard": place + way},
                )

    def hop(j, k):
        for way in (1, -1):
            block = place - way * k

            @pl.when((block >= 0) & (block < shards))
            def _():
                mine = window(chunks[j], block, part)
                wait_bytes(mine, line_recv.at[j, block])

                @pl.when((place + way >= 0) & (place + way < shards))
                def _():
                    start_remote(
                        mine, mine, pass_send.at[j, block], line_recv.at[j, block], {"shard": place + way}
                    )

                start_remote(mine, mine, x_send.at[j, block], x_recv.at[j, block], {"replica": member ^ 2})
                start_remote(
                    mine, mine, core_send.at[j, block, 0], core_recv.at[j, block, 0], {"replica": member ^ 1}
                )

    def across(j, k):
        for way in (1, -1):
            block = place - way * k

            @pl.when((block >= 0) & (block < shards))
            def _():
                theirs = window(chunks[j], block, part ^ 2)
                wait_bytes(theirs, x_recv.at[j, block])
                start_remote(
                    theirs, theirs, core_send.at[j, block, 1], core_recv.at[j, block, 1], {"replica": member ^ 1}
                )

    def prepare(index):
        loads(index).wait()
        block = held[index]
        if turns[index] == "columns":
            span = matrix.shape[0]
            for at in range(0, block.shape[1], span):
                part_value = dot(block[:, at : at + span], matrix[...], NN)
                block[:, at : at + span] = part_value.astype(block.dtype)
        elif turns[index] == "rows":
            span = matrix.shape[0]
            for at in range(0, block.shape[0], span):
                part_value = dot(matrix[...], block[at : at + span, :], TN)
                block[at : at + span, :] = part_value.astype(block.dtype)
        stores(index).start()

    total = len(chunks)
    waiting = list(range(count))
    for step in range(max(total + shards + 1, count + 1)):
        if step < total:
            index = chunks[step][0]
            if turns[index] and index in waiting:
                waiting.remove(index)
                prepare(index)
            own(step)
        if 1 <= step <= count and step - 1 in waiting:
            waiting.remove(step - 1)
            prepare(step - 1)
        for k in range(1, shards):
            if 0 <= step - k < total:
                hop(step - k, k)
        for k in range(1, shards):
            if 0 <= step - k - 1 < total:
                across(step - k - 1, k)

    for j in range(total):
        for slot, way in enumerate((1, -1)):
            @pl.when((place + way >= 0) & (place + way < shards))
            def _():
                wait_bytes(window(chunks[j], place, part), own_send.at[j, slot])

        for k in range(1, shards):
            for way in (1, -1):
                block = place - way * k

                @pl.when((block >= 0) & (block < shards))
                def _():
                    mine = window(chunks[j], block, part)

                    @pl.when((place + way >= 0) & (place + way < shards))
                    def _():
                        wait_bytes(mine, pass_send.at[j, block])

                    wait_bytes(mine, x_send.at[j, block])
                    for which in range(2):
                        wait_bytes(mine, core_send.at[j, block, which])
                        wait_bytes(mine, core_recv.at[j, block, which])
    for index in range(count):
        stores(index).wait()


def gather_weights(pieces, turns, shards, pace=192 * 1024):
    chunks = []
    for index, piece in enumerate(pieces):
        rows, width = piece.shape
        cuts = 1
        while rows % (2 * cuts * 16) == 0 and rows // cuts * (width // PARTS) > pace:
            cuts *= 2
        for cut in range(cuts):
            chunks.append((index, cut * (rows // cuts), rows // cuts))
    count, total = len(pieces), len(chunks)
    dma = pltpu.SemaphoreType.DMA
    return pl.pallas_call(
        functools.partial(gather_kernel, shards, tuple(chunks), count, tuple(turns)),
        out_shape=[jax.ShapeDtypeStruct((shards * p.shape[0], p.shape[1]), p.dtype) for p in pieces],
        in_specs=[pl.BlockSpec(memory_space=pltpu.VMEM)] + [pl.BlockSpec(memory_space=pl.ANY)] * count,
        out_specs=[pl.BlockSpec(memory_space=pl.ANY)] * count,
        scratch_shapes=[pltpu.VMEM(p.shape, p.dtype) for p in pieces]
        + [
            dma((count,)),
            dma((total, 2)),
            dma((total, shards)),
            dma((total, shards)),
            dma((total, shards)),
            dma((total, shards)),
            dma((total, shards, 2)),
            dma((total, shards, 2)),
        ],
        compiler_params=pltpu.CompilerParams(collective_id=0, has_side_effects=True, vmem_limit_bytes=24 * 1024 * 1024),
        name="gather_weights",
    )(jnp.asarray(tile_matrix(), jnp.bfloat16), *pieces)


def add_rows(target, left, right, rows):
    step = next(size for size in (128, 64, 16) if rows % size == 0)

    def body(i, carry):
        window = pl.ds(pl.multiple_of(i * step, step), step)
        target[window, :] = (
            left[window, :].astype(jnp.float32) + right[window, :].astype(jnp.float32)
        ).astype(target.dtype)
        return carry

    lax.fori_loop(0, rows // step, body, 0)


def reduce_kernel(shards, plan, count, *refs):
    leads, trails, heights, kinds = plan
    chunks = leads + trails
    total = len(chunks)
    terms, refs = refs[:count], refs[count:]
    sums, refs = refs[:count], refs[count:]
    near, refs = refs[:count], refs[count:]
    landed, refs = refs[:total], refs[total:]
    passing, refs = refs[:total], refs[total:]
    swapped, refs = refs[: len(trails)], refs[len(trails) :]
    stages = []
    for kind in range(len(kinds)):
        stages.append(refs[:6])
        refs = refs[6:]
    trail_stage, refs = refs[:4], refs[4:]
    (load_sem, core_send, core_recv, x_send, x_recv, line_send, line_recv) = refs[:7]
    (end_local, end_x_send, end_x_recv, end_core_send, end_core_recv) = refs[7:]
    place = lax.axis_index("shard")
    member = lax.axis_index("replica")
    core = member % 2
    side = (member // 2) % 2
    x_mate = {"replica": member ^ 2}
    core_mate = {"replica": member ^ 1}
    greet(shards)

    def leading(j):
        return j < len(leads)

    def height(j):
        return heights[chunks[j][0]]

    def columns(j, whose):
        index, first, width = chunks[j]
        part = terms[index].shape[1] // PARTS
        return pl.ds(pl.multiple_of(whose * part + first, LANES), width)

    def send_near(j):
        index = chunks[j][0]
        for which in range(2):
            start_remote(
                terms[index].at[:, columns(j, (1 - core) * 2 + which)],
                near[index].at[:, columns(j, which)],
                core_send.at[j, which],
                core_recv.at[j, which],
                core_mate,
            )

    def staged(j):
        if leading(j):
            a0, a1, b0, b1, c, d = stages[kinds.index((height(j), chunks[j][2]))]
            return (b0, b1, c, d) if j % 2 else (a0, a1, c, d)
        return trail_stage

    def load_copies(j):
        index = chunks[j][0]
        whose = (1 - side, side) if leading(j) else (0, 1)
        at = staged(j)
        sem = 0 if leading(j) else 4
        sources = [terms[index].at[:, columns(j, core * 2 + w)] for w in whose]
        sources += [near[index].at[:, columns(j, w)] for w in whose]
        return [pltpu.make_async_copy(s, at[i], load_sem.at[sem + i]) for i, s in enumerate(sources)]

    def load(j):
        for which in range(2):
            wait_bytes(near[chunks[j][0]].at[:, columns(j, which)], core_recv.at[j, which])
        for copy in load_copies(j):
            copy.start()

    def near_sum(j):
        size = shards * height(j)
        at = staged(j)
        for copy in load_copies(j):
            copy.wait()
        if leading(j):
            add_rows(at[0], at[0], at[2], size)
            start_remote(at[0], landed[j], x_send.at[j], x_recv.at[j], x_mate)
            add_rows(at[1], at[1], at[3], size)
        else:
            width = chunks[j][2]
            for which in range(2):
                window = landed[j].at[:, pl.ds(which * width, width)]
                add_rows(window, at[which], at[2 + which], size)

    def x_sum(j):
        at = staged(j)
        wait_bytes(at[0], x_send.at[j])
        wait_bytes(landed[j], x_recv.at[j])
        add_rows(landed[j], landed[j], at[1], shards * height(j))

    def block(j, t):
        rows = height(j)
        return landed[j].at[pl.ds(pl.multiple_of(t * rows, rows), rows), :]

    def inside(t):
        return (t >= 0) & (t < shards)

    def line(j, hop):
        for slot, way in enumerate((1, -1)):
            t = place + way * (shards - hop)
            target = passing[j].at[slot, hop - 1]
            sems = (line_send.at[j, slot, hop - 1], line_recv.at[j, slot, hop - 1])
            ahead = {"shard": place + way}
            own = block(j, jnp.clip(t, 0, shards - 1))
            if hop == 1:

                @pl.when(inside(t))
                def _():
                    start_remote(own, target, *sems, ahead)
            else:
                arrived = passing[j].at[slot, hop - 2]

                @pl.when(inside(t) & inside(place - way))
                def _():
                    wait_bytes(arrived, line_recv.at[j, slot, hop - 2])
                    add_rows(arrived, arrived, own, height(j))
                    start_remote(arrived, target, *sems, ahead)

                @pl.when(inside(t) & jnp.logical_not(inside(place - way)))
                def _():
                    start_remote(own, target, *sems, ahead)

    def sum_window(j, whose):
        return sums[chunks[j][0]].at[:, columns(j, whose)]

    def share(j):
        width = chunks[j][2]
        for which in range(1 if leading(j) else 2):
            rows = block(j, place).at[:, pl.ds(which * width, width)]
            target = sum_window(j, core * 2 + (side if leading(j) else which))
            pltpu.make_async_copy(rows, target, end_local.at[j, which]).start()
            start_remote(rows, target, end_core_send.at[j, which], end_core_recv.at[j, which], core_mate)

    def line_end(j):
        mine = block(j, place)
        for slot, way in enumerate((1, -1)):

            @pl.when(inside(place - way))
            def _():
                arrived = passing[j].at[slot, shards - 2]
                wait_bytes(arrived, line_recv.at[j, slot, shards - 2])
                add_rows(mine, mine, arrived, height(j))

        target = sum_window(j, core * 2 + side) if leading(j) else swapped[j - len(leads)]
        start_remote(mine, target, end_x_send.at[j], end_x_recv.at[j], x_mate)
        if leading(j):
            share(j)

    def finish(j):
        if leading(j):
            theirs = sum_window(j, core * 2 + (1 - side))
            wait_bytes(theirs, end_x_recv.at[j])
            start_remote(theirs, theirs, end_core_send.at[j, 1], end_core_recv.at[j, 1], core_mate)
        else:
            mine, other = block(j, place), swapped[j - len(leads)]
            wait_bytes(mine, end_x_send.at[j])
            wait_bytes(other, end_x_recv.at[j])
            add_rows(mine, mine, other, height(j))
            share(j)

    first, second = len(leads), len(trails)
    for j in range(max(first, second)):
        if j < first:
            send_near(j)
        if j < second:
            send_near(first + j)
    load(0)
    load(first)
    for step in range(max(first + shards + 2, second + shards + 1)):
        if step < first:
            near_sum(step)
        if step < second:
            near_sum(first + step)
            if step + 1 < second:
                load(first + step + 1)
            line(first + step, 1)
        for hop in range(2, shards):
            if 0 <= step - hop < first:
                line(step - hop, hop)
            if 0 <= step - hop + 1 < second:
                line(first + step - hop + 1, hop)
        if 0 <= step - shards < first:
            line_end(step - shards)
        if 0 <= step - shards + 1 < second:
            line_end(first + step - shards + 1)
        if 0 <= step - shards - 1 < first:
            finish(step - shards - 1)
        if 0 <= step - shards < second:
            finish(first + step - shards)
        if 1 <= step <= first:
            x_sum(step - 1)
            line(step - 1, 1)
        if step + 1 < first:
            load(step + 1)

    for j in range(total):
        for which in range(2):
            wait_bytes(near[chunks[j][0]].at[:, columns(j, which)], core_send.at[j, which])
        for slot, way in enumerate((1, -1)):
            for hop in range(1, shards):

                @pl.when(inside(place + way * (shards - hop)))
                def _():
                    wait_bytes(passing[j].at[slot, hop - 1], line_send.at[j, slot, hop - 1])

        if leading(j):
            wait_bytes(sum_window(j, 0), end_x_send.at[j])
        for which in range(2):
            if which == 0 or not leading(j):
                wait_bytes(sum_window(j, 0), end_local.at[j, which])
            wait_bytes(sum_window(j, 0), end_core_send.at[j, which])
            wait_bytes(sum_window(j, 0), end_core_recv.at[j, which])


def reduce_terms(leading, trailing, shards, lead_cells=1536 * 256):
    terms = list(leading) + list(trailing)
    count = len(terms)
    heights = tuple(t.shape[0] // shards for t in terms)
    leads, trails = [], []
    for index, term in enumerate(terms):
        part = term.shape[1] // PARTS
        if index < len(leading):
            width = part
            while width % (2 * LANES) == 0 and width * term.shape[0] > lead_cells:
                width //= 2
            if width * term.shape[0] > lead_cells and width % LANES == 0:
                width = LANES
            leads += [(index, first, width) for first in range(0, part, width)]
        else:
            trails += [(index, first, LANES) for first in range(0, part, LANES)]
    kinds = []
    for index, first, width in leads:
        if (heights[index], width) not in kinds:
            kinds.append((heights[index], width))
    chunks = leads + trails
    total = len(chunks)
    bf16, dma = jnp.bfloat16, pltpu.SemaphoreType.DMA

    def rows_and_width(j):
        index, first, width = chunks[j]
        return heights[index], width if j < len(leads) else 2 * width

    scratch = []
    for j in range(total):
        rows, width = rows_and_width(j)
        scratch.append(pltpu.VMEM((shards * rows, width), bf16))
    for j in range(total):
        rows, width = rows_and_width(j)
        scratch.append(pltpu.VMEM((2, shards - 1, rows, width), bf16))
    for j in range(len(leads), total):
        rows, width = rows_and_width(j)
        scratch.append(pltpu.VMEM((rows, width), bf16))
    for rows, width in kinds:
        scratch += [pltpu.VMEM((shards * rows, width), bf16)] * 6
    scratch += [pltpu.VMEM((shards * heights[-1], LANES), bf16)] * 4
    scratch += [
        dma((8,)),
        dma((total, 2)),
        dma((total, 2)),
        dma((total,)),
        dma((total,)),
        dma((total, 2, shards - 1)),
        dma((total, 2, shards - 1)),
        dma((total, 2)),
        dma((total,)),
        dma((total,)),
        dma((total, 2)),
        dma((total, 2)),
    ]
    outs = pl.pallas_call(
        functools.partial(reduce_kernel, shards, (tuple(leads), tuple(trails), heights, tuple(kinds)), count),
        out_shape=[jax.ShapeDtypeStruct((t.shape[0] // shards, t.shape[1]), bf16) for t in terms]
        + [jax.ShapeDtypeStruct((t.shape[0], t.shape[1] // 2), bf16) for t in terms],
        in_specs=[pl.BlockSpec(memory_space=pl.ANY)] * count,
        out_specs=[pl.BlockSpec(memory_space=pl.ANY)] * (2 * count),
        scratch_shapes=scratch,
        compiler_params=pltpu.CompilerParams(
            collective_id=1, has_side_effects=True, vmem_limit_bytes=62 * 1024 * 1024
        ),
        name="reduce_terms",
    )(*terms)
    return outs[:count]


def tile_order():
    order = np.zeros(4 * HD, np.int32)
    for tile in range(3):
        for lane in range(LANES):
            upper, low = divmod(lane, LANES // 2)
            if low < HD // 2:
                head, item = tile, low
            else:
                head, item = 3, 16 * tile + low - HD // 2
            order[tile * LANES + lane] = head * HD + upper * (HD // 2) + item
    return order


def tile_matrix():
    order = tile_order()
    return (np.arange(4 * HD)[:, None] == order[None, :]).astype(np.float32)


def from_tiles(x):
    matrix = jnp.asarray(tile_matrix().T, jnp.bfloat16)
    span = 4 * HD
    return jnp.concatenate(
        [
            jnp.dot(x[:, i : i + span], matrix, preferred_element_type=jnp.float32).astype(x.dtype)
            for i in range(0, x.shape[1], span)
        ],
        axis=1,
    )


def rows_to_tiles(x):
    matrix = jnp.asarray(tile_matrix().T, jnp.bfloat16)
    groups = x.reshape(-1, 4 * HD, x.shape[1])
    moved = jnp.einsum("lk,gkn->gln", matrix, groups, preferred_element_type=jnp.float32)
    return moved.astype(x.dtype).reshape(x.shape)


def rope_tables(positions):
    item = tile_order() % (HD // 2)
    frequency = ROPE_BASE ** (-(jnp.asarray(item, jnp.float32) * 2.0) / HD)
    angles = positions.astype(jnp.float32)[:, None] * frequency[None, :]
    upper = (np.arange(3 * LANES) // (LANES // 2)) % 2 == 1
    sign = jnp.asarray(np.where(upper, 1.0, -1.0), jnp.float32)
    return jnp.cos(angles), jnp.sin(angles) * sign[None, :]


def spare_lanes(shape):
    return lax.broadcasted_iota(jnp.int32, shape, 1) % (LANES // 2) >= HD // 2


def last_head(tiles):
    spare = spare_lanes(tiles[0].shape)
    return sum(
        pltpu.roll(jnp.where(spare, tiles[i], 0.0), LANES - HD // 2 + 16 * i, 1) for i in range(3)
    )


def merge_heads(heads):
    spare = spare_lanes(heads[0].shape)
    return [
        jnp.where(spare, pltpu.roll(heads[3], HD // 2 - 16 * i, 1), heads[i])
        for i in range(3)
    ]


def tile(ref, index):
    return ref[:, index * LANES : (index + 1) * LANES]


def put(ref, index, value):
    ref[:, index * LANES : (index + 1) * LANES] = value


def turn(value, cosine, sine):
    return value * cosine + pltpu.roll(value, LANES // 2, 1) * sine


def key_tile(group, i):
    return group * 6 + i


def value_tile(group, i):
    return group * 6 + 3 + i


def fill_bias(bias, own_segment, key_segments, rows):
    size = key_segments.shape[1]
    same = own_segment[...] == key_segments[...]
    query = lax.broadcasted_iota(jnp.int32, (rows, size), 0)
    key = lax.broadcasted_iota(jnp.int32, (rows, size), 1)
    bias[...] = jnp.where(same & ((key >= rows) | (key <= query)), 0.0, -1e30)


def inside(place, shards):
    return (place >= 0) & (place < shards)


def line_place(shards):
    place = lax.axis_index("shard")
    mirrored = lax.axis_index("replica") % 2 == 1
    return jnp.where(mirrored, shards - 1 - place, place)


def line_device(place, shards):
    mirrored = lax.axis_index("replica") % 2 == 1
    return {"shard": jnp.where(mirrored, shards - 1 - place, place)}


def greet_line(shards, way):
    place = line_place(shards)
    barrier = pltpu.get_barrier_semaphore()

    @pl.when(inside(place - way, shards))
    def _():
        pl.semaphore_signal(
            barrier,
            inc=1,
            device_id=line_device(place - way, shards),
            device_id_type=pl.DeviceIdType.MESH,
        )

    @pl.when(inside(place + way, shards))
    def _():
        pl.semaphore_wait(barrier, 1)


def dot(left, right, dims):
    return lax.dot_general(left, right, (dims, ((), ())), preferred_element_type=jnp.float32)


NT = ((1,), (1,))
NN = ((1,), (0,))
TN = ((0,), (0,))


def attend_kernel(
    shards, hops, rows, raw, cosine, sine, own_segment, key_segments,
    queries, window, attended, log_total,
    held, last, bias, query_heads, send_sem, recv_sem, keep_sem,
):
    place = line_place(shards)
    greet_line(shards, 1)

    def slot(distance):
        return held.at[pl.ds(distance * rows, rows), :]

    first_key, first_value = QH * 3 // 4, QH * 3 // 4 + KVH * 3 // 4
    for group in range(KVH // 4):
        for i in range(3):
            value = turn(tile(raw, first_key + group * 3 + i), tile(cosine, i), tile(sine, i))
            held[pl.ds(0, rows), key_tile(group, i) * LANES : (key_tile(group, i) + 1) * LANES] = value.astype(
                jnp.bfloat16
            )
            value = tile(raw, first_value + group * 3 + i)
            held[pl.ds(0, rows), value_tile(group, i) * LANES : (value_tile(group, i) + 1) * LANES] = (
                value.astype(jnp.bfloat16)
            )

    def send(distance):
        @pl.when((place + 1 < shards) & (place - distance >= 0))
        def _():
            start_remote(
                slot(distance),
                slot(distance + 1),
                send_sem.at[distance],
                recv_sem.at[distance],
                line_device(place + 1, shards),
            )

    send(0)
    fill_bias(bias, own_segment, key_segments, rows)
    for group in range(QH // 4):
        tiles = []
        for i in range(3):
            value = turn(tile(raw, group * 3 + i), tile(cosine, i), tile(sine, i))
            put(queries, group * 3 + i, value.astype(jnp.bfloat16))
            tiles.append(value)
        spare = spare_lanes(tiles[0].shape)
        for i in range(3):
            query_heads[group * 4 + i] = jnp.where(spare, 0.0, tiles[i]).astype(jnp.bfloat16)
        query_heads[group * 4 + 3] = last_head(tiles).astype(jnp.bfloat16)

    def receive(distance):
        @pl.when(place - distance >= 0)
        def _():
            wait_bytes(slot(distance), recv_sem.at[distance - 1])

        @pl.when(place - distance < 0)
        def _():
            held[pl.ds(distance * rows, rows), :] = jnp.zeros((rows, held.shape[1]), held.dtype)

        if distance < hops:
            send(distance)

    def scores_values(head, first, size):
        wide, item = divmod(head // 2, 4)
        span = pl.ds(first, size)
        if item == 3:
            keys, values = last[wide * 2, span], last[wide * 2 + 1, span]
        else:
            at = [spot(wide, item) * LANES for spot in (key_tile, value_tile)]
            keys, values = (held[span, lane : lane + LANES] for lane in at)
        return dot(query_heads[head], keys, NT) * HD ** (-0.5) + bias[:, first : first + size], values

    def fill_last(first, size):
        for wide in range(KVH // 4):
            for which, at in enumerate((key_tile(wide, 0), value_tile(wide, 0))):
                tiles = [
                    held[pl.ds(first, size), (at + i) * LANES : (at + i + 1) * LANES].astype(jnp.float32)
                    for i in range(3)
                ]
                last[wide * 2 + which, pl.ds(first, size)] = last_head(tiles).astype(jnp.bfloat16)

    for distance in range(1, hops):
        receive(distance)
    near = hops * rows
    fill_last(0, near)
    state = []
    for head in range(QH):
        scores, values = scores_values(head, 0, near)
        top = jnp.max(scores, axis=1, keepdims=True)
        exponent = jnp.exp(scores - top)
        total = jnp.sum(exponent, axis=1, keepdims=True)
        state.append((top, total, dot(exponent.astype(jnp.bfloat16), values, NN)))
    receive(hops)
    keep = pltpu.make_async_copy(held, window, keep_sem)
    keep.start()
    fill_last(near, rows)
    lane = lax.broadcasted_iota(jnp.int32, (rows, LANES), 1)
    totals = jnp.zeros((rows, LANES), jnp.float32)
    for group in range(QH // 4):
        outs = []
        for head in range(group * 4, group * 4 + 4):
            before, total, out = state[head]
            scores, values = scores_values(head, near, rows)
            top = jnp.maximum(before, jnp.max(scores, axis=1, keepdims=True))
            exponent = jnp.exp(scores - top)
            shrink = jnp.exp(before - top)
            total = total * shrink + jnp.sum(exponent, axis=1, keepdims=True)
            out = out * shrink + dot(exponent.astype(jnp.bfloat16), values, NN)
            outs.append(out * (1.0 / total))
            totals = jnp.where(lane == head, top + jnp.log(total), totals)
        for i, merged in enumerate(merge_heads(outs)):
            put(attended, group * 3 + i, merged.astype(jnp.bfloat16))
    log_total[...] = totals
    keep.wait()
    for distance in range(hops):
        @pl.when((place + 1 < shards) & (place - distance >= 0))
        def _():
            wait_bytes(slot(distance), send_sem.at[distance])


def line_hops(shards, rows, longest):
    return min(shards - 1, -(-(longest - 1) // rows))


def attend(raw, cosine, sine, own_segment, key_segments, shards, hops):
    rows = raw.shape[0]
    width = QH * HD
    size = (hops + 1) * rows
    bf16, f32, dma = jnp.bfloat16, jnp.float32, pltpu.SemaphoreType.DMA
    vmem = pl.BlockSpec(memory_space=pltpu.VMEM)
    return pl.pallas_call(
        functools.partial(attend_kernel, shards, hops, rows),
        out_shape=[
            jax.ShapeDtypeStruct((rows, width), bf16),
            jax.ShapeDtypeStruct((size, width), bf16),
            jax.ShapeDtypeStruct((rows, width), bf16),
            jax.ShapeDtypeStruct((rows, LANES), f32),
        ],
        in_specs=[vmem] * 5,
        out_specs=[vmem, pl.BlockSpec(memory_space=pl.ANY), vmem, vmem],
        scratch_shapes=[
            pltpu.VMEM((size, width), bf16),
            pltpu.VMEM((KVH // 2, size, LANES), bf16),
            pltpu.VMEM((rows, size), f32),
            pltpu.VMEM((QH, rows, LANES), bf16),
            dma((hops,)),
            dma((hops,)),
            dma,
        ],
        compiler_params=pltpu.CompilerParams(
            collective_id=2, has_side_effects=True, vmem_limit_bytes=62 * 1024 * 1024
        ),
        name="attend",
    )(raw, cosine, sine, own_segment, key_segments)


def attend_back_kernel(
    shards, hops, rows, queries, window, log_total, grads, cosine, sine, own_segment, key_segments,
    lows,
    bias, own_part, parts, landing, query_grads, send_sem, recv_sem,
):
    place = line_place(shards)
    greet_line(shards, -1)
    fill_bias(bias, own_segment, key_segments, rows)
    span = 6 * LANES

    def heads_of(ref, group):
        tiles = [tile(ref, group * 3 + i).astype(jnp.float32) for i in range(3)]
        spare = spare_lanes(tiles[0].shape)
        heads = [jnp.where(spare, 0.0, t).astype(jnp.bfloat16) for t in tiles]
        return heads + [last_head(tiles).astype(jnp.bfloat16)]

    def column(head):
        lane = lax.broadcasted_iota(jnp.int32, (rows, LANES), 1)
        return jnp.sum(jnp.where(lane == head, log_total[...], 0.0), axis=1, keepdims=True)

    def wide_group(wide):
        heads = heads_of(queries, 2 * wide) + heads_of(queries, 2 * wide + 1)
        grad_heads = heads_of(grads, 2 * wide) + heads_of(grads, 2 * wide + 1)
        key_grads, value_grads = [], []
        query_out = []
        key_tiles = [tile(window, key_tile(wide, i)) for i in range(3)]
        value_tiles = [tile(window, value_tile(wide, i)) for i in range(3)]
        key_tiles.append(last_head([t.astype(jnp.float32) for t in key_tiles]).astype(jnp.bfloat16))
        value_tiles.append(last_head([t.astype(jnp.float32) for t in value_tiles]).astype(jnp.bfloat16))
        for item in range(4):
            keys, values = key_tiles[item], value_tiles[item]
            key_grad = value_grad = None
            for one in (2 * item, 2 * item + 1):
                query, grad = heads[one], grad_heads[one]
                scores = dot(query, keys, NT) * HD ** (-0.5) + bias[...]
                probs = jnp.exp(scores - column(wide * 8 + one))
                grad_probs = dot(grad, values, NT)
                along = jnp.sum(probs * grad_probs, axis=1, keepdims=True)
                grad_scores = (probs * (grad_probs - along)).astype(jnp.bfloat16)
                query_out.append(dot(grad_scores, keys, NN) * HD ** (-0.5))
                key_one = dot(grad_scores, query, TN)
                value_one = dot(probs.astype(jnp.bfloat16), grad, TN)
                key_grad = key_one if key_grad is None else key_grad + key_one
                value_grad = value_one if value_grad is None else value_grad + value_one
            key_grads.append(key_grad * HD ** (-0.5))
            value_grads.append(value_grad)
        for which, grads_of in enumerate((key_grads, value_grads)):
            for i, merged in enumerate(merge_heads(grads_of)):
                at = which * 3 + i
                own_part[:, (wide * 6 + at) * LANES : (wide * 6 + at + 1) * LANES] = merged[:rows]
                for distance in range(1, hops + 1):
                    parts[wide, distance - 1, :, at * LANES : (at + 1) * LANES] = merged[
                        distance * rows : (distance + 1) * rows
                    ].astype(jnp.bfloat16)
        for half in range(2):
            for i, merged in enumerate(merge_heads(query_out[half * 4 : half * 4 + 4])):
                put(query_grads, (2 * wide + half) * 3 + i, merged)

    def step(wide, k):
        distance = hops - k + 1
        source = parts.at[wide, distance - 1]
        target = landing.at[wide, k - 1]
        sems = (send_sem.at[wide, k - 1], recv_sem.at[wide, k - 1])

        @pl.when(place - distance >= 0)
        def _():
            if k > 1:
                @pl.when(place + 1 < shards)
                def _():
                    arrived = landing.at[wide, k - 2]
                    wait_bytes(arrived, recv_sem.at[wide, k - 2])
                    source[...] = (
                        source[...].astype(jnp.float32) + arrived[...].astype(jnp.float32)
                    ).astype(jnp.bfloat16)

            start_remote(source, target, *sems, line_device(place - 1, shards))

    def finish(wide):
        @pl.when(place + 1 < shards)
        def _():
            arrived = landing.at[wide, hops - 1]
            wait_bytes(arrived, recv_sem.at[wide, hops - 1])
            own_part[:, wide * span : (wide + 1) * span] += arrived[...].astype(jnp.float32)

        first_key, first_value = QH * 3 // 4, QH * 3 // 4 + KVH * 3 // 4
        for i in range(3):
            value = turn(tile(own_part, key_tile(wide, i)), tile(cosine, i), -tile(sine, i))
            put(lows, first_key + wide * 3 + i, value.astype(jnp.bfloat16))
            put(lows, first_value + wide * 3 + i, tile(own_part, value_tile(wide, i)).astype(jnp.bfloat16))

    for wide in range(KVH // 4):
        wide_group(wide)
        step(wide, 1)
    for group in range(QH // 4):
        for i in range(3):
            value = turn(tile(query_grads, group * 3 + i), tile(cosine, i), -tile(sine, i))
            put(lows, group * 3 + i, value.astype(jnp.bfloat16))
    for k in range(2, hops + 1):
        for wide in range(KVH // 4):
            step(wide, k)
    for wide in range(KVH // 4):
        finish(wide)
    for wide in range(KVH // 4):
        for k in range(1, hops + 1):
            @pl.when(place - (hops - k + 1) >= 0)
            def _():
                wait_bytes(parts.at[wide, hops - k], send_sem.at[wide, k - 1])


def attend_back(queries, window, log_total, grads, cosine, sine, own_segment, key_segments, shards, hops):
    rows = queries.shape[0]
    width = QH * HD
    size = (hops + 1) * rows
    bf16, f32, dma = jnp.bfloat16, jnp.float32, pltpu.SemaphoreType.DMA
    vmem = pl.BlockSpec(memory_space=pltpu.VMEM)
    wides = KVH // 4
    return pl.pallas_call(
        functools.partial(attend_back_kernel, shards, hops, rows),
        out_shape=jax.ShapeDtypeStruct((rows, 2 * width), bf16),
        in_specs=[vmem] * 8,
        out_specs=vmem,
        scratch_shapes=[
            pltpu.VMEM((rows, size), f32),
            pltpu.VMEM((rows, width), f32),
            pltpu.VMEM((wides, hops, rows, 6 * LANES), bf16),
            pltpu.VMEM((wides, hops, rows, 6 * LANES), bf16),
            pltpu.VMEM((rows, width), f32),
            dma((wides, hops)),
            dma((wides, hops)),
        ],
        compiler_params=pltpu.CompilerParams(
            collective_id=3, has_side_effects=True, vmem_limit_bytes=62 * 1024 * 1024
        ),
        name="attend_back",
    )(queries, window, log_total, grads, cosine, sine, own_segment, key_segments)


def sigmoid(value):
    return 1.0 / (1.0 + jnp.exp(-value))


def feed_kernel(
    inputs,
    attended,
    w_out,
    gain,
    w_gate,
    w_up,
    w_down,
    middle,
    normed,
    gate,
    up,
    hidden,
    result,
    total,
):
    step = pl.program_id(0)

    @pl.when(step == 0)
    def _():
        value = inputs[...] + dot(attended[...], w_out[...], NN)
        middle[...] = value
        recip = lax.rsqrt(jnp.mean(value * value, axis=-1, keepdims=True) + EPSILON)
        normed[...] = (value * recip * gain[...]).astype(jnp.bfloat16)
        total[...] = value

    gate_value = dot(normed[...], w_gate[...], NN)
    up_value = dot(normed[...], w_up[...], NN)
    low = (gate_value * sigmoid(gate_value) * up_value).astype(jnp.bfloat16)
    gate[...] = gate_value.astype(jnp.bfloat16)
    up[...] = up_value.astype(jnp.bfloat16)
    hidden[...] = low
    total[...] += dot(low, w_down[...], NN)

    @pl.when(step == pl.num_programs(0) - 1)
    def _():
        result[...] = total[...].astype(jnp.bfloat16)


def whole(shape):
    return pl.BlockSpec(shape, lambda i: (0, 0), pipeline_mode=pl.Buffered(1))


def feed_forward(inputs, attended, w_out, gain, w_gate, w_up, w_down, block=1024):
    rows, width = inputs.shape
    units = w_gate.shape[1]
    f32, bf16 = jnp.float32, jnp.bfloat16
    columns = pl.BlockSpec((rows, block), lambda i: (0, i))
    weight = pl.BlockSpec((width, block), lambda i: (0, i))
    return pl.pallas_call(
        feed_kernel,
        grid=(units // block,),
        out_shape=[
            jax.ShapeDtypeStruct((rows, width), f32),
            jax.ShapeDtypeStruct((rows, width), bf16),
            jax.ShapeDtypeStruct((rows, units), bf16),
            jax.ShapeDtypeStruct((rows, units), bf16),
            jax.ShapeDtypeStruct((rows, units), bf16),
            jax.ShapeDtypeStruct((rows, width), bf16),
        ],
        in_specs=[
            whole((rows, width)),
            whole(attended.shape),
            whole(w_out.shape),
            whole((1, width)),
            weight,
            weight,
            pl.BlockSpec((block, width), lambda i: (i, 0)),
        ],
        out_specs=[
            whole((rows, width)),
            whole((rows, width)),
            columns,
            columns,
            columns,
            whole((rows, width)),
        ],
        scratch_shapes=[pltpu.VMEM((rows, width), f32)],
        compiler_params=pltpu.CompilerParams(vmem_limit_bytes=62 * 1024 * 1024),
        cost_estimate=pl.CostEstimate(
            flops=6 * rows * width * units + 2 * rows * width * width,
            bytes_accessed=6 * width * units + 2 * width * width + 6 * rows * units + 14 * rows * width,
            transcendentals=rows * units,
        ),
        name="feed_forward",
    )(inputs, attended, w_out, gain[None], w_gate, w_up, w_down)


def feed_back_kernel(
    grads,
    middle,
    gain,
    w_out,
    gate,
    up,
    w_gate,
    w_up,
    w_down,
    gate_low,
    up_low,
    grad_middle,
    attn_grad,
    grad_attended,
    gain_grad,
    branch,
    total,
):
    step = pl.program_id(0)

    @pl.when(step == 0)
    def _():
        branch[...] = grads[...].astype(jnp.bfloat16)
        total[...] = jnp.zeros_like(total)

    grad_hidden = dot(branch[...], w_down[...], NT)
    gate_value, up_value = gate[...].astype(jnp.float32), up[...].astype(jnp.float32)
    share = sigmoid(gate_value)
    one = (grad_hidden * up_value * (share * (1.0 + gate_value * (1.0 - share)))).astype(jnp.bfloat16)
    two = (grad_hidden * (gate_value * share)).astype(jnp.bfloat16)
    gate_low[...] = one
    up_low[...] = two
    total[...] += dot(one, w_gate[...], NT) + dot(two, w_up[...], NT)

    @pl.when(step == pl.num_programs(0) - 1)
    def _():
        value = middle[...]
        recip = lax.rsqrt(jnp.mean(value * value, axis=-1, keepdims=True) + EPSILON)
        scaled = value * recip
        grad = total[...]
        gain_grad[...] = jnp.sum(grad * scaled, axis=0, keepdims=True)
        grad = grad * gain[...]
        grad = grads[...] + recip * (
            grad - scaled * jnp.mean(grad * scaled, axis=-1, keepdims=True)
        )
        grad_middle[...] = grad
        attn_grad[...] = grad.astype(jnp.bfloat16)
        grad_attended[...] = dot(attn_grad[...], w_out[...], NT).astype(jnp.bfloat16)


def feed_back(grads, middle, gain, w_out, gate, up, w_gate, w_up, w_down, block=1024):
    rows, width = grads.shape
    units = w_gate.shape[1]
    f32, bf16 = jnp.float32, jnp.bfloat16
    columns = pl.BlockSpec((rows, block), lambda i: (0, i))
    weight = pl.BlockSpec((width, block), lambda i: (0, i))
    return pl.pallas_call(
        feed_back_kernel,
        grid=(units // block,),
        out_shape=[
            jax.ShapeDtypeStruct((rows, units), bf16),
            jax.ShapeDtypeStruct((rows, units), bf16),
            jax.ShapeDtypeStruct((rows, width), f32),
            jax.ShapeDtypeStruct((rows, width), bf16),
            jax.ShapeDtypeStruct((rows, w_out.shape[0]), bf16),
            jax.ShapeDtypeStruct((1, width), f32),
        ],
        in_specs=[
            whole((rows, width)),
            whole((rows, width)),
            whole((1, width)),
            whole(w_out.shape),
            columns,
            columns,
            weight,
            weight,
            pl.BlockSpec((block, width), lambda i: (i, 0)),
        ],
        out_specs=[
            columns,
            columns,
            whole((rows, width)),
            whole((rows, width)),
            whole((rows, w_out.shape[0])),
            whole((1, width)),
        ],
        scratch_shapes=[pltpu.VMEM((rows, width), bf16), pltpu.VMEM((rows, width), f32)],
        compiler_params=pltpu.CompilerParams(vmem_limit_bytes=62 * 1024 * 1024),
        cost_estimate=pl.CostEstimate(
            flops=6 * rows * width * units + 2 * rows * width * width,
            bytes_accessed=6 * width * units + 2 * width * width + 8 * rows * units + 16 * rows * width,
            transcendentals=rows * units,
        ),
        name="feed_back",
    )(grads, middle, gain[None], w_out, gate, up, w_gate, w_up, w_down)


def from_behind(x, axis, by):
    devices = lax.axis_size(axis)
    pairs = [(i, i + by) for i in range(devices) if 0 <= i + by < devices]
    return lax.ppermute(x, axis, pairs)


def swap(x, bit):
    members = lax.axis_size("replica")
    return lax.ppermute(x, "replica", [(r, r ^ (1 << bit)) for r in range(members)])


def mirror(x):
    members, shards = lax.axis_size("replica"), lax.axis_size("shard")
    pairs = [
        (r * shards + s, r * shards + shards - 1 - s)
        for r in range(1, members, 2)
        for s in range(shards)
        if 2 * s != shards - 1
    ]
    moved = lax.ppermute(x, ("replica", "shard"), pairs)
    return jnp.where(lax.axis_index("replica") % 2 == 1, moved, x)


def gain_width(rows):
    return -(-2 * rows // (PARTS * LANES)) * PARTS * LANES


def gather_layer(pieces):
    norm_attn, w_query, w_key, w_value, w_out, norm_ffn, w_gate, w_up, w_down = pieces
    rows = norm_attn.shape[0]
    shards = lax.axis_size("shard")
    gains = jnp.concatenate([norm_attn, norm_ffn])
    gains = jnp.pad(gains[None], ((0, 15), (0, gain_width(rows) - 2 * rows)))
    w_qkv = jnp.concatenate([w_query, w_key, w_value], axis=1)
    inside_rows = rows % (4 * HD) == 0
    w_gate, w_up, w_down, gains, w_out, w_qkv = gather_weights(
        [w_gate, w_up, w_down, gains, w_out, w_qkv],
        [None, None, None, None, "rows" if inside_rows else None, "columns"],
        shards,
    )
    if not inside_rows:
        w_out = rows_to_tiles(w_out)
    gains = gains.reshape(shards, 16, -1)[:, 0].astype(jnp.float32)
    norm_attn = gains[:, :rows].reshape(-1)
    norm_ffn = gains[:, rows : 2 * rows].reshape(-1)
    return norm_attn, w_qkv, w_out, norm_ffn, w_gate, w_up, w_down


def sequence_tables(segment, rows, hops):
    place = line_place(lax.axis_size("shard"))
    local_segment = lax.dynamic_slice_in_dim(segment, place * rows, rows)
    starts = jnp.sum((segment[None, :] < local_segment[:, None]).astype(jnp.int32), axis=1)
    cosine, sine = rope_tables(place * rows + jnp.arange(rows, dtype=jnp.int32) - starts)
    padded = jnp.concatenate([jnp.full((hops * rows,), -1, jnp.int32), segment])
    key_segments = jnp.concatenate(
        [lax.dynamic_slice_in_dim(padded, (place + hops - d) * rows, rows) for d in range(hops + 1)]
    )
    return cosine, sine, local_segment[:, None], key_segments[None, :]


def matmul(left, right):
    return jnp.dot(left, right, preferred_element_type=jnp.float32)


def matmul_back(left, right):
    return jnp.einsum("tq,dq->td", left, right, preferred_element_type=jnp.float32)


def row_product(left, right):
    return jnp.einsum("td,tq->dq", left, right, preferred_element_type=jnp.float32)


def forward_layer(inputs, weights, tables, shards, hops):
    norm_attn, w_qkv, w_out, norm_ffn, w_gate, w_up, w_down = weights
    recip_one = lax.rsqrt(jnp.mean(inputs * inputs, axis=-1, keepdims=True) + EPSILON)
    scaled = inputs * recip_one
    normed = (scaled * norm_attn).astype(jnp.bfloat16)
    queries, window, attended, log_total = attend(matmul(normed, w_qkv), *tables, shards, hops)
    middle, normed_mid, gate, up, hidden, result = feed_forward(
        inputs, attended, w_out, norm_ffn, w_gate, w_up, w_down
    )
    saved = (
        scaled,
        recip_one,
        normed,
        queries,
        window,
        log_total,
        attended,
        middle,
        normed_mid,
        gate,
        up,
        hidden,
        tables,
    )
    return (result, saved)


def backward_layer(grad_result, weights, saved, shards, hops):
    norm_attn, w_qkv, w_out, norm_ffn, w_gate, w_up, w_down = weights
    (
        scaled,
        recip_one,
        normed,
        queries,
        window,
        log_total,
        attended,
        middle,
        normed_mid,
        gate,
        up,
        hidden,
        tables,
    ) = saved
    branch_grad = grad_result.astype(jnp.bfloat16)
    gate_low, up_low, grad_middle, attn_grad, grad_attended, grad_norm_ffn = feed_back(
        grad_result, middle, norm_ffn, w_out, gate, up, w_gate, w_up, w_down
    )
    qkv_low = attend_back(queries, window, log_total, grad_attended, *tables, shards, hops)
    grad_normed = matmul_back(qkv_low, w_qkv)
    grad_norm_attn = jnp.sum(grad_normed * scaled, axis=0)
    grad_scaled = grad_normed * norm_attn
    grad_inputs = grad_middle + recip_one * (
        grad_scaled - scaled * jnp.mean(grad_scaled * scaled, axis=-1, keepdims=True)
    )
    operands = (
        normed,
        qkv_low,
        attended,
        attn_grad,
        normed_mid,
        gate_low,
        up_low,
        hidden,
        branch_grad,
    )
    return (grad_inputs, (grad_norm_attn, grad_norm_ffn[0]), operands)


def reduce_gradients(operand_pairs, gains, last_grads):
    (
        normed,
        qkv_low,
        attended,
        attn_grad,
        normed_mid,
        gate_low,
        up_low,
        hidden,
        branch_grad,
    ) = (jnp.concatenate(parts, axis=0) for parts in zip(*operand_pairs))
    shards = lax.axis_size("shard")
    rows = gains[0].shape[0] // shards

    def product(left, right):
        return row_product(left, right).astype(jnp.bfloat16)

    gain_term = jnp.stack([gain.reshape(shards, rows) for gain in gains], axis=1)
    gain_term = gain_term.reshape(shards, 1, 2 * rows).astype(jnp.bfloat16)
    gain_term = jnp.pad(gain_term, ((0, 0), (0, 15), (0, gain_width(rows) - 2 * rows)))
    gain_term, last_grads = lax.optimization_barrier((gain_term, last_grads))
    cut = up_low.shape[1] // 4 * 3
    leading = [
        product(hidden, branch_grad),
        product(normed_mid, gate_low),
        product(normed_mid, up_low[:, :cut]),
        gain_term.reshape(shards * 16, -1),
    ]
    trailing = [
        product(normed_mid, up_low[:, cut:]),
        product(from_tiles(attended), attn_grad),
        product(normed, from_tiles(qkv_low)),
    ]
    totals = [total.astype(jnp.float32) for total in reduce_terms(leading, trailing, shards)]
    members = lax.axis_size("replica")
    for bit in range(PARTS.bit_length() - 1, members.bit_length() - 1):
        totals = [total + swap(total, bit) for total in totals]
    down, gate, up, own_gains, up_rest, out, qkv = totals
    up = jnp.concatenate([up, up_rest], axis=1)
    return (
        own_gains[0, :rows],
        qkv[:, : QH * HD],
        qkv[:, QH * HD : (QH + KVH) * HD],
        qkv[:, (QH + KVH) * HD :],
        out,
        own_gains[0, rows : 2 * rows],
        gate,
        up,
        down,
    ), last_grads


def body(
    tokens,
    segments,
    norm_attn,
    w_query,
    w_key,
    w_value,
    w_out,
    norm_ffn,
    w_gate,
    w_up,
    w_down,
    cotangent,
):
    micro_count = tokens.shape[0]
    row_count = tokens.shape[2]
    width = tokens.shape[3]
    seq_length = segments.shape[2]
    shards = lax.axis_size("shard")
    hops = line_hops(shards, row_count, seq_length // 2)
    first_section = lax.axis_index("section") == 0

    def choose(early, late):
        return jax.tree.map(lambda a, b: jnp.where(first_section, a, b), early, late)

    weights = gather_layer(
        (
            norm_attn[0],
            w_query[0],
            w_key[0],
            w_value[0],
            w_out[0],
            norm_ffn[0],
            w_gate[0],
            w_up[0],
            w_down[0],
        )
    )
    later, gathered = lax.optimization_barrier((tokens[1:], weights[0]))
    weights = (gathered,) + weights[1:]
    tokens = jnp.concatenate([mirror(tokens[:1]), mirror(later)]) if micro_count > 1 else mirror(tokens)
    all_tables = [sequence_tables(segments[m, 0], row_count, hops) for m in range(micro_count)]
    saved_ticks = []
    result_ticks = []
    later_grads = []
    arriving = jnp.zeros((row_count, width), jnp.bfloat16)
    for tick_index in range(micro_count + 1):
        own_input = tokens[min(tick_index, micro_count - 1), 0].astype(jnp.float32)
        layer_input = jnp.where(first_section, own_input, arriving.astype(jnp.float32))
        if tick_index > 0:
            layer_input, later_grads[-1] = lax.optimization_barrier((layer_input, later_grads[-1]))
        tables = choose(
            all_tables[min(tick_index, micro_count - 1)], all_tables[max(tick_index - 1, 0)]
        )
        result_low, saved = forward_layer(layer_input, weights, tables, shards, hops)
        result_ticks.append(result_low)
        saved_ticks.append(saved)
        if tick_index < micro_count:
            grad, attended = lax.optimization_barrier((cotangent[tick_index, 0], saved[6]))
            later_grads.append(mirror(grad))
        if tick_index < micro_count:
            arriving = from_behind(result_low, "section", 1)
    flow_ticks = []
    gain_sums = None
    operand_ticks = []
    returning = jnp.zeros((row_count, width), jnp.bfloat16)
    for tick_index in range(micro_count + 1):
        later_grad = later_grads[min(tick_index, micro_count - 1)].astype(jnp.float32)
        incoming = jnp.where(first_section, returning.astype(jnp.float32), later_grad)
        active = jnp.where(first_section, tick_index >= 1, tick_index < micro_count)
        incoming = jnp.where(active, incoming, 0.0)
        if 0 < tick_index < micro_count:
            saved = choose(saved_ticks[tick_index - 1], saved_ticks[tick_index + 1])
        else:
            saved = saved_ticks[1 if tick_index == 0 else micro_count - 1]
        grad_inputs, gains, operands = backward_layer(incoming, weights, saved, shards, hops)
        flow_ticks.append(grad_inputs)
        if tick_index < micro_count:
            returning = from_behind(grad_inputs.astype(jnp.bfloat16), "section", -1)
        gain_sums = gains if gain_sums is None else jax.tree.map(jnp.add, gain_sums, gains)
        operand_ticks.append(operands)
    edge_operands = choose(operand_ticks[micro_count], operand_ticks[0])
    flows = [mirror(choose(flow_ticks[m + 1], flow_ticks[m])) for m in range(micro_count)]
    totals, flows[-1] = reduce_gradients(
        operand_ticks[1:micro_count] + [edge_operands], gain_sums, flows[-1]
    )
    section_outputs = mirror(
        jnp.stack(
            [choose(result_ticks[index], result_ticks[index + 1]) for index in range(micro_count)]
        )
    )
    input_grads = jnp.stack(flows)
    return (section_outputs[None, :, None], input_grads[None, :, None]) + tuple(
        total[None] for total in totals
    )


def solution(mesh):
    in_specs = (
        P(None, "replica", "shard", None),
        P(None, "replica", None),
        P("section", "shard"),
        P("section", "shard", None),
        P("section", "shard", None),
        P("section", "shard", None),
        P("section", "shard", None),
        P("section", "shard"),
        P("section", "shard", None),
        P("section", "shard", None),
        P("section", "shard", None),
        P(None, "replica", "shard", None),
    )
    out_specs = (
        P("section", None, "replica", "shard", None),
        P("section", None, "replica", "shard", None),
        P("section", "shard"),
        P("section", "shard", None),
        P("section", "shard", None),
        P("section", "shard", None),
        P("section", "shard", None),
        P("section", "shard"),
        P("section", "shard", None),
        P("section", "shard", None),
        P("section", "shard", None),
    )
    return jax.shard_map(body, mesh=mesh, in_specs=in_specs, out_specs=out_specs, check_vma=False)
```
